32 devices in a mesh: section: 2 (over x), expert: 4 (over z), replica: 4 (over y, core).
Axes of the slice: x: 2, y: 2, z: 4, core: 2. Of those that a mesh axis runs over, the one named last changes fastest.
Arguments:
- x_in: bfloat16 [2, 4096, 768], P(None, ('expert', 'replica')), may hold values from -6 to 6
- cotangent: bfloat16 [2, 4096, 768], P(None, ('expert', 'replica')), may hold values from -6 to 6
- segments: int32 [2, 16, 256], P(None, ('expert', 'replica')), may hold values from 0 to 1, never falling along the last dimension, each value on 1 to 192 neighbouring positions
- routes: int32 [2, 2, 4096, 2], P('section', None, ('expert', 'replica')), may hold values from 0 to 3, all different within a row; in each aligned block of 256 rows (0 to 255, 256 to 511, ..., all dimensions but the last counted through in order) at most 160 rows name the same one
- gains: bfloat16 [2, 2, 768], P('section', None, 'expert'), may hold values from 0.5 to 1.5
- w_qkv: bfloat16 [2, 768, 2304], P('section', 'expert'), may hold values from -0.21875 to 0.21875
- w_out: bfloat16 [2, 768, 768], P('section', 'expert'), may hold values from -1.75 to 1.75
- router: bfloat16 [2, 768, 4], P('section', 'expert'), may hold values from -0.21875 to 0.21875
- rel_bias: bfloat16 [2, 32, 12], P('section', 'expert'), may hold values from -4 to 302
- w_gate_up: bfloat16 [2, 4, 2, 768, 3072], P('section', 'expert'), may hold values from -0.21875 to 0.21875
- w_down: bfloat16 [2, 4, 3072, 768], P('section', 'expert'), may hold values from -0.109375 to 0.109375
Outputs:
- section_out: bfloat16 [2, 2, 4096, 768], P('section', None, ('expert', 'replica'))
- input_grad: bfloat16 [2, 2, 4096, 768], P('section', None, ('expert', 'replica'))
- grad_gains: float32 [2, 2, 768], P('section', None, 'expert')
- grad_qkv: float32 [2, 768, 2304], P('section', 'expert')
- grad_out: float32 [2, 768, 768], P('section', 'expert')
- grad_router: float32 [2, 768, 4], P('section', 'expert')
- grad_bias: float32 [2, 32, 12], P('section', 'expert')
- grad_gate_up: float32 [2, 4, 2, 768, 3072], P('section', 'expert', None, None, 'replica')
- grad_down: float32 [2, 4, 3072, 768], P('section', 'expert', 'replica')
The draws below stay inside these ranges and needn't reach their ends.
Inputs may be any that keep to these rules, and one draw needn't show every extreme that they name: `segments`: in each slot the ids never fall; each slot holds two sequences, each of 64 to 192 positions. `routes`: the two experts of a token differ; among the rows of one slot of one layer and micro-batch (aligned blocks of 256 rows) no expert is named more than 160 times, and in some block one expert is named exactly 160 times.
All inputs are finite; a program needn't handle non-finite values.
Results may differ from the reference program's by a relative error of at most 0.03.
Values may be sent and summed in bfloat16 or wider, within the bound.
No kernel may reach another device: no remote copies, remote signals or barrier semaphores. Data moves between devices by JAX's collectives and lax.ppermute only.
A program may use at most 384 MiB of HBM per device.

```python
import math
from functools import partial
import jax
import jax.numpy as jnp
import numpy as np
from jax import lax

D = 768
H = 12
DH = 64
FF = 3072
NB = 32
MAXDIST = 128
MICRO = 2
SLOT = 256
LAYERS = 2
EXPERTS = 4
CAP = 160
GROUPS = 16
TOKENS = 4096


def draw_rel_bias(key, part):
    first_key = jax.random.fold_in(key, 0)
    shape = (LAYERS, NB, H)
    return jnp.clip(jax.random.normal(first_key, shape, jnp.float32), -4.0, 4.0).astype(jnp.bfloat16)


def block_levels(own_key, shape, shards, smallest, high):
    level = 1.0
    for dim, parts in shards:
        steps = jax.random.uniform(jax.random.fold_in(jax.random.fold_in(own_key, 6), dim), (parts,), jnp.float32, smallest / len(shards), high / len(shards))
        level = level * jnp.repeat(jnp.exp(steps), shape[dim] // parts).reshape((-1,) + (1,) * (len(shape) - 1 - dim))
    return level


def length_profile(number_of, total, bound, lean):
    loads = [(1 << 20) // math.isqrt(rank ** lean) + 1 for rank in range(2, number_of + 1)]
    spare, given = total - bound - (number_of - 1), [1] * (number_of - 1)
    while spare > 0:
        free = [i for i in range(number_of - 1) if given[i] < bound]
        pool, budget = sum([loads[i] for i in free]), spare
        for i in free:
            extra = min(bound - given[i], max(1, budget * loads[i] // pool), spare)
            given[i] = given[i] + extra
            spare = spare - extra
    return np.array([bound] + given)


def uneven(own_key, amount, total, limit, lean):
    if amount == 2:
        one = jax.random.randint(own_key, (), max(1, total - limit), min(limit, total - 1) + 1)
        return jnp.stack([one, total - one])
    lengths = jnp.asarray(length_profile(amount, total, limit, lean), jnp.int32)
    twos = (amount - 1) // 2
    giver, sink = lengths[1:1 + 2 * twos:2], lengths[2:2 + 2 * twos:2]
    margin = jnp.minimum(giver - 1, limit - sink)
    moved = jax.random.randint(jax.random.fold_in(own_key, 1), (twos,), 0, 1 << 20) % (margin + 1)
    lengths = lengths.at[1:1 + 2 * twos:2].set(giver - moved).at[2:2 + 2 * twos:2].set(sink + moved)
    return lengths[jax.random.permutation(jax.random.fold_in(own_key, 2), amount)]


def routed_block(stream_key, own, number, rows, amount, top, bound, lean):
    ranking = jax.random.permutation(stream_key, amount)
    heavy_load, ordinary = shares(amount, rows * top, bound, lean, True), shares(amount, rows * top, bound, lean, False)
    places = jnp.arange(amount)

    def named(lengths, rotation):
        used = int((lengths > 0).sum())
        fixed = max(1, used // 4)
        passed = fixed + (places - fixed + rotation * (used - fixed)) % max(1, amount - fixed)
        return jnp.zeros((amount,), jnp.int32).at[ranking[jnp.where(places < fixed, places, passed)]].set(jnp.asarray(lengths, jnp.int32))

    lengths = jnp.where(number % 4 == 0, named(heavy_load, number // 4), named(ordinary, number - number // 4 - 1))
    mixed = jax.random.permutation(jax.random.fold_in(own, 3), amount)
    donor, sink = mixed[0:amount // 2 * 2:2], mixed[1:amount // 2 * 2:2]
    margin = jnp.minimum(lengths[donor] - 1, bound - lengths[sink]) // 2
    margin = jnp.where((donor == ranking[0]) | (sink == ranking[0]) | (lengths[sink] == 0), 0, jnp.maximum(margin, 0))
    passed = jax.random.randint(jax.random.fold_in(own, 4), (amount // 2,), 0, 1 << 20) % (margin + 1)
    lengths = lengths.at[donor].add(-passed).at[sink].add(passed)
    labels = jnp.searchsorted(jnp.cumsum(lengths), jnp.arange(rows * top), side="right").astype(jnp.int32)
    table = labels.reshape(top, rows).T
    table = table[jax.random.permutation(jax.random.fold_in(own, 1), rows)]
    rotation = jax.random.randint(jax.random.fold_in(own, 2), (rows, 1), 0, top)
    return jnp.take_along_axis(table, (jnp.arange(top)[None, :] + rotation) % top, axis=1)


def shares(count, total, limit, slope, full):
    loads = [(1 << 20) // math.isqrt(standing ** slope) + 1 for standing in range(1, count + 1)]
    largest = limit if full else min(limit, max(-(-total // count), total * loads[0] // sum(loads)))
    least = 1 if total - largest >= count - 1 else 0
    given, surplus = [largest] + [least] * (count - 1), total - largest - least * (count - 1)
    while surplus > 0:
        candidates = [i for i in range(1, count) if given[i] < largest] or [i for i in range(1, count) if given[i] < limit]
        mass, left = sum([loads[i] for i in candidates]), surplus
        for i in candidates:
            more = min(limit - given[i], max(1, left * loads[i] // mass), surplus)
            given[i] = given[i] + more
            surplus = surplus - more
    return np.array(given)


def noise(own_key, extent, scale, limit, cuts=(), kind=jnp.bfloat16):
    drawn = jax.random.normal(own_key, extent, jnp.float32) * scale
    if len(cuts) > 0:
        drawn = block_levels(own_key, extent, cuts, -0.22, 0.18) * drawn
    return jnp.clip(drawn, min=-limit, max=limit).astype(kind)


def setup_inputs(seed: int = 0) -> dict:
    streams_of = jax.random.split(jax.random.key(seed), 12)
    x_in = noise(streams_of[0], (MICRO, TOKENS, D), 1.0, 6.0, ((1, 16),))
    cotangent = noise(streams_of[1], (MICRO, TOKENS, D), 1.0, 6.0, ((1, 16),))
    segments = jax.vmap(lambda own: jnp.searchsorted(jnp.cumsum(uneven(own, 2, SLOT, 3 * SLOT // 4, 1)), jnp.arange(SLOT), side="right"))(jax.random.split(streams_of[2], MICRO * GROUPS)).reshape((MICRO, GROUPS, SLOT)).astype(jnp.int32)
    routes_keys = jax.random.split(jax.random.fold_in(streams_of[3], 1), LAYERS * MICRO * TOKENS // SLOT)
    routes_turns = jax.random.permutation(jax.random.fold_in(streams_of[3], 3), LAYERS * MICRO * TOKENS // SLOT)
    routes = jax.vmap(lambda own, number: routed_block(jax.random.fold_in(streams_of[3], 2), own, number, SLOT, EXPERTS, 2, CAP, 2))(routes_keys, routes_turns).reshape((LAYERS, MICRO, TOKENS, 2))
    gains = jnp.clip(1.0 + 0.1 * jax.random.normal(streams_of[4], (LAYERS, 2, D), jnp.float32), 0.5, 1.5).astype(jnp.bfloat16)
    w_qkv = noise(streams_of[5], (LAYERS, D, 3 * D), D ** -0.5, 0.21875, ((0, 2), (1, 4)))
    w_out = noise(streams_of[6], (LAYERS, D, D), (max(D // 64, 1)) ** -0.5, 1.75, ((0, 2), (1, 4)))
    router = noise(streams_of[7], (LAYERS, D, EXPERTS), D ** -0.5, 0.21875, ((0, 2), (1, 4)))
    rel_bias = draw_rel_bias(jax.random.fold_in(streams_of[11], 71), 0)
    w_gate_up = noise(streams_of[9], (LAYERS, EXPERTS, 2, D, FF), D ** -0.5, 0.21875, ((0, 2), (1, 4)))
    w_down = noise(streams_of[10], (LAYERS, EXPERTS, FF, D), FF ** -0.5, 0.109375, ((0, 2), (1, 4)))
    return {"x_in": x_in, "cotangent": cotangent, "segments": segments, "routes": routes, "gains": gains, "w_qkv": w_qkv, "w_out": w_out, "router": router, "rel_bias": rel_bias, "w_gate_up": w_gate_up, "w_down": w_down}


@jax.custom_vjp
def low(v):
    return lax.optimization_barrier(v.astype(jnp.bfloat16)).astype(jnp.float32)

@jax.custom_vjp
def low_back(v):
    return v

def low_keep(v):
    return (low(v), None)

def low_pass(kept, grad):
    return (grad,)

def back_keep(v):
    return (v, None)

def back_low(kept, grad):
    return (low(grad),)
low.defvjp(low_keep, low_pass)
low_back.defvjp(back_keep, back_low)
EPS = 1e-06
SCALE = 0.125
MASKED = -1000000000.0
HIGHEST = lax.Precision.HIGHEST

def bucket_ids(size, buckets, reach):
    places = np.arange(size)
    distance = np.maximum(places[:, None] - places[None, :], 0)
    exact = buckets // 2
    scaled = np.log(np.maximum(distance, 1) / exact) / math.log(reach / exact) * (buckets - exact)
    spread = exact + np.floor(np.maximum(scaled, 0.0)).astype(np.int64)
    return np.where(distance < exact, distance, np.minimum(spread, buckets - 1)).astype(np.int32)

def norm(x, gain):
    return x * lax.rsqrt(lax.optimization_barrier(jnp.mean(x * x, axis=-1, keepdims=True)) + EPS) * gain

def attend_slot(qkv, segment, table):
    ids = bucket_ids(SLOT, NB, MAXDIST)
    query = qkv[:, :D].reshape(SLOT, H, DH)
    keys = qkv[:, D:2 * D].reshape(SLOT, H, DH)
    values = qkv[:, 2 * D:].reshape(SLOT, H, DH)
    bias = jnp.transpose(jnp.take(table, jnp.asarray(ids), axis=0), (2, 0, 1))
    scores = jnp.einsum('qhd,khd->hqk', query, keys, precision=HIGHEST) * SCALE + bias
    scores = low_back(scores)
    places = jnp.arange(SLOT, dtype=jnp.int32)
    allowed = (places[:, None] >= places[None, :]) & (segment[:, None] == segment[None, :])
    scores = jnp.where(allowed[None], scores, MASKED)
    top = lax.optimization_barrier(jnp.max(scores, axis=-1, keepdims=True))
    weights = jnp.exp(scores - top)
    probs = weights / lax.optimization_barrier(jnp.sum(weights, axis=-1, keepdims=True))
    mixed = jnp.einsum('hqk,khd->qhd', low(probs), values, precision=HIGHEST)
    return mixed.reshape(SLOT, D)

def expert_block(pack):
    rows_in, gate_up, down = pack
    both = low_back(jnp.einsum('rd,cdf->crf', rows_in, gate_up, precision=HIGHEST))
    hidden = low(jax.nn.gelu(both[0], approximate=True) * both[1])
    return low(low_back(jnp.dot(hidden, down, precision=HIGHEST)))

def layer(routes_now, segments_now, params, x_in):
    gains, qkv_w, out_w, router_w, table, gate_up, down = params
    x = low_back(x_in)
    tokens = x.shape[0]
    attn_in = low(norm(x, gains[0]))
    qkv = low(low_back(jnp.dot(attn_in, qkv_w, precision=HIGHEST)))

    def one_slot(pair):
        return attend_slot(pair[0], pair[1], table)
    mixed = lax.map(jax.checkpoint(one_slot), (qkv.reshape(GROUPS, SLOT, 3 * D), segments_now))
    mixed = low(low_back(mixed.reshape(tokens, D)))
    attn = low_back(jnp.dot(mixed, out_w, precision=HIGHEST))
    resid = x + attn
    moe_in = low(norm(resid, gains[1]))
    logits = low_back(jnp.dot(moe_in, router_w, precision=HIGHEST))
    pick = routes_now[:, :, None] == jnp.arange(EXPERTS, dtype=jnp.int32)[None, None, :]
    chosen = lax.optimization_barrier(jnp.sum(jnp.where(pick, logits[:, None, :], 0.0), axis=-1))
    first = jax.nn.sigmoid(chosen[:, 0] - chosen[:, 1])
    second = jax.nn.sigmoid(chosen[:, 1] - chosen[:, 0])
    flat = routes_now.reshape(GROUPS, 2 * SLOT)
    hits = (flat[:, :, None] == jnp.arange(EXPERTS, dtype=jnp.int32)[None, None, :]).astype(jnp.int32)
    before = jnp.cumsum(hits, axis=1, dtype=jnp.int32) - hits
    place = lax.optimization_barrier(jnp.sum(before * hits, axis=-1, dtype=jnp.int32))
    group = jnp.arange(GROUPS, dtype=jnp.int32)[:, None]
    dest = ((flat * GROUPS + group) * CAP + place).reshape(-1).astype(jnp.int32)
    rows = jnp.repeat(moe_in, 2, axis=0)
    buffer = jnp.zeros((EXPERTS * GROUPS * CAP, D), jnp.float32).at[dest].set(rows)
    buffer = low_back(buffer).reshape(EXPERTS, GROUPS * CAP, D)
    outputs = lax.map(jax.checkpoint(expert_block), (buffer, gate_up, down))
    back = outputs.reshape(-1, D)[dest].reshape(tokens, 2, D)
    moe = first[:, None] * back[:, 0] + second[:, None] * back[:, 1]
    return low(resid + moe)

def reference(x_in, cotangent, segments, routes, gains, w_qkv, w_out, router, rel_bias, w_gate_up, w_down):
    arrays = (gains, w_qkv, w_out, router, rel_bias, w_gate_up, w_down)
    params = [tuple((array[depth].astype(jnp.float32) for array in arrays)) for depth in range(LAYERS)]
    totals = [jax.tree.map(jnp.zeros_like, params[depth]) for depth in range(LAYERS)]
    first_outs, second_outs, first_grads, second_grads = ([], [], [], [])
    for micro in range(MICRO):
        first_out, first_pull = jax.vjp(partial(layer, routes[0, micro], segments[micro]), params[0], x_in[micro].astype(jnp.float32))
        second_out, second_pull = jax.vjp(partial(layer, routes[1, micro], segments[micro]), params[1], first_out)
        second_params, middle_grad = second_pull(cotangent[micro].astype(jnp.float32))
        first_params, start_grad = first_pull(middle_grad)
        totals[0] = jax.tree.map(jnp.add, totals[0], first_params)
        totals[1] = jax.tree.map(jnp.add, totals[1], second_params)
        first_outs.append(first_out)
        second_outs.append(second_out)
        first_grads.append(start_grad)
        second_grads.append(middle_grad)
    section_out = jnp.stack([jnp.stack(first_outs), jnp.stack(second_outs)]).astype(jnp.bfloat16)
    input_grad = jnp.stack([jnp.stack(first_grads), jnp.stack(second_grads)]).astype(jnp.bfloat16)
    grads = [jnp.stack([totals[0][index], totals[1][index]]) for index in range(7)]
    return (section_out, input_grad, grads[0], grads[1], grads[2], grads[3], grads[4], grads[5], grads[6])
```

```python
import functools
import math

import jax
import jax.numpy as jnp
import numpy as np
from jax import lax
from jax.experimental import pallas as pl
from jax.experimental.pallas import tpu as pltpu
from jax.sharding import PartitionSpec as P

D = 768
H = 12
DH = 64
NB = 32
MAXDIST = 128
EPS = 1e-06
SCALE = 0.125
MASKED = -1000000000.0

LANES = 128
COL_OUT = 3 * D
COL_SMALL = 4 * D
WIDE = 4 * D + LANES
LANE_GAIN = 32
LANE_BIAS = 64
HOPS = (0, 2, 1, 3)
SUB = 1


F32 = jnp.float32
BF16 = jnp.bfloat16


def dot(a, b):
    return lax.dot_general(a, b, (((1,), (0,)), ((), ())), preferred_element_type=F32)


def dot_nt(a, b):
    return lax.dot_general(a, b, (((1,), (1,)), ((), ())), preferred_element_type=F32)


def dot_tn(a, b):
    return lax.dot_general(a, b, (((0,), (0,)), ((), ())), preferred_element_type=F32)


def bucket_ids(size, buckets, reach):
    distance = np.arange(size)
    exact = buckets // 2
    scaled = np.log(np.maximum(distance, 1) / exact) / math.log(reach / exact) * (buckets - exact)
    spread = exact + np.floor(np.maximum(scaled, 0.0)).astype(np.int64)
    return np.where(distance < exact, distance, np.minimum(spread, buckets - 1)).astype(np.int32)


def bucket_rows(slot, experts):
    ids = bucket_ids(slot, NB, MAXDIST)
    rows, held = D // experts, NB // experts
    table = np.zeros((D, slot), np.float32)
    for column in range(slot):
        bucket = ids[(slot - column) % slot]
        table[bucket // held * rows + bucket % held, column] = 1.0
    return table


def lane(shape):
    return lax.broadcasted_iota(jnp.int32, shape, 1)


def sublane(shape):
    return lax.broadcasted_iota(jnp.int32, shape, 0)


def one_hot(mask):
    return jnp.where(mask, 1.0, 0.0).astype(BF16)


def gain_rows(small):
    pick = one_hot(lane((8, LANES)) == sublane((8, LANES)) + LANE_GAIN)
    return dot_nt(pick, small)


def inverse_rms(x):
    return lax.rsqrt(jnp.mean(x * x, axis=-1, keepdims=True) + EPS)


def norm_back(x, gain, grad):
    inverse = inverse_rms(x)
    scaled = grad * gain
    along = jnp.mean(scaled * x, axis=-1, keepdims=True)
    return (
        inverse * scaled - x * (inverse * inverse * inverse * along),
        jnp.sum(grad * x * inverse, axis=0, keepdims=True),
    )


def column(values, index):
    return jnp.sum(jnp.where(lane(values.shape) == index, values, 0.0), axis=1, keepdims=True)


def set_masks(seg_col, seg_row, fence):
    slot = fence.shape[0]
    allowed = (sublane((slot, slot)) >= lane((slot, slot))) & (seg_col[...] == seg_row[...])
    fence[...] = jnp.where(allowed, 0.0, MASKED)


def bias_of(table, head, slot):
    row = table[pl.ds(LANE_BIAS + head, 1), :]
    return pltpu.roll(jnp.broadcast_to(row, (slot, slot)), 0, 1, stride=1, stride_axis=0)


def attend(x, pk, onehot, seg_col, seg_row, routes, dest_row, qkv, mixed, lse, resid, moe_in, weights, packed, table, fence):
    slot = x.shape[0]
    small = pk[:, COL_SMALL:]
    gains = gain_rows(small)
    table[...] = dot_tn(small, onehot[...])
    set_masks(seg_col, seg_row, fence)
    attn_in = (x * inverse_rms(x) * gains[0:1]).astype(BF16)
    for part in range(3):
        span = slice(part * D, (part + 1) * D)
        qkv[:, span] = dot(attn_in, pk[:, span]).astype(BF16)
    lse[...] = jnp.zeros_like(lse)

    def pair(index, _):
        start = pl.multiple_of(index * LANES, LANES)
        query = qkv[:, pl.ds(start, LANES)]
        keys = qkv[:, pl.ds(pl.multiple_of(D + start, LANES), LANES)]
        values = qkv[:, pl.ds(pl.multiple_of(2 * D + start, LANES), LANES)]
        total = jnp.zeros((slot, LANES), F32)
        for half in range(2):
            head = 2 * index + half
            own = lane((slot, LANES)) // DH == half
            scores = dot_nt(jnp.where(own, query, 0.0).astype(BF16), keys) * SCALE
            scores = scores + bias_of(table, head, slot) + fence[...]
            top = jnp.max(scores, axis=-1, keepdims=True)
            powers = jnp.exp(scores - top)
            norm = jnp.sum(powers, axis=-1, keepdims=True)
            probs = (powers / norm).astype(BF16)
            total = total + dot(probs, jnp.where(own, values, 0.0).astype(BF16))
            lse[...] = jnp.where(lane((slot, LANES)) == head, top + jnp.log(norm), lse[...])
        mixed[:, pl.ds(start, LANES)] = total.astype(BF16)
        return 0

    lax.fori_loop(0, H // 2, pair, 0)
    after = x + dot(mixed[...], pk[:, COL_OUT:COL_SMALL])
    resid[...] = after
    normed = (after * inverse_rms(after) * gains[1:2]).astype(BF16)
    moe_in[...] = normed
    logits = dot(normed, small)
    chosen = [
        jnp.sum(jnp.where(lane(logits.shape) == routes[:, k : k + 1], logits, 0.0), axis=1, keepdims=True)
        for k in range(2)
    ]
    first = jax.nn.sigmoid(chosen[0] - chosen[1])
    second = jax.nn.sigmoid(chosen[1] - chosen[0])
    places = lane((slot, LANES))
    weights[...] = jnp.where(places == 0, first, jnp.where(places == 1, second, 0.0))
    rows = sublane((packed.shape[0], slot))
    spread = one_hot((rows == dest_row[0:1, :]) | (rows == dest_row[1:2, :]))
    packed[...] = dot(spread, normed).astype(BF16)


def fetch_rows(dest_col, source, index):
    slot = dest_col.shape[0]
    places = lane((slot, source.shape[0]))
    return dot(one_hot(places == dest_col[:, index : index + 1]), source[...])


def combine(resid, weights, dest_col, returned):
    back = [fetch_rows(dest_col, returned, k) for k in range(2)]
    out = resid[...] + column(weights[...], 0) * back[0] + column(weights[...], 1) * back[1]
    return out.astype(BF16), back


def dispatch_back(grad, weights, back, dest_row, packed, grad_weights):
    slot = grad.shape[0]
    places = lane((slot, LANES))
    sums = [jnp.sum(grad * back[k], axis=-1, keepdims=True) for k in range(2)]
    grad_weights[...] = jnp.where(places == 0, sums[0], jnp.where(places == 1, sums[1], 0.0))
    rows = sublane((packed.shape[0], slot))
    total = jnp.zeros(packed.shape, F32)
    for k in range(2):
        scaled = (column(weights[...], k) * grad).astype(BF16)
        total = total + dot(one_hot(rows == dest_row[k : k + 1, :]), scaled)
    packed[...] = total.astype(BF16)


def first_kernel(x, pk, onehot, seg_col, seg_row, routes, dest_row, *rest):
    attend(x[...].astype(F32), pk, onehot, seg_col, seg_row, routes, dest_row, *rest)


def middle_kernel(resid, weights, dest_col, returned, pk, onehot, seg_col, seg_row, routes, dest_row, out, back0, back1, *rest):
    after, back = combine(resid, weights, dest_col, returned)
    out[...] = after
    back0[...] = back[0].astype(BF16)
    back1[...] = back[1].astype(BF16)
    attend(after.astype(F32), pk, onehot, seg_col, seg_row, routes, dest_row, *rest)


def turn_kernel(resid, weights, dest_col, dest_row, returned, cotangent, out, packed, grad_weights):
    after, back = combine(resid, weights, dest_col, returned)
    out[...] = after
    dispatch_back(cotangent[...].astype(F32), weights, back, dest_row, packed, grad_weights)


def attend_back(x_ref, pk, onehot, seg_col, seg_row, routes, dest_col, grad_out, returned, resid, moe_in, weights, grad_weights,
                qkv, mixed, lse, grad_pk, grad_in, table, fence, grad_mixed, grad_qkv, sums, flip):
    slot = resid.shape[0]
    small = pk[:, COL_SMALL:]
    gains = gain_rows(small)
    table[...] = dot_tn(small, onehot[...])
    set_masks(seg_col, seg_row, fence)
    places = lane((slot, returned.shape[0]))
    both = one_hot((places == dest_col[:, 0:1]) | (places == dest_col[:, 1:2]))
    grad_moe = dot(both, returned[...])
    first, second = column(weights[...], 0), column(weights[...], 1)
    diff = column(grad_weights[...], 0) * first * (1.0 - first) - column(grad_weights[...], 1) * second * (1.0 - second)
    spots = lane((slot, LANES))
    grad_logits = jnp.where(
        spots == routes[:, 0:1], diff, jnp.where(spots == routes[:, 1:2], -diff, 0.0)
    ).astype(BF16)
    grad_moe = grad_moe + dot_nt(grad_logits, small)
    back, gain_moe = norm_back(resid[...], gains[1:2], grad_moe)
    grad_resid = grad_out[...].astype(F32) + back
    grad_attn = grad_resid.astype(BF16)
    grad_pk[:, COL_OUT:COL_SMALL] = dot_tn(mixed[...], grad_attn).astype(BF16)
    grad_mixed[...] = dot_nt(grad_attn, pk[:, COL_OUT:COL_SMALL]).astype(BF16)
    sums[...] = jnp.zeros_like(sums)
    flip[...] = one_hot(sublane((slot, slot)) + lane((slot, slot)) == slot - 1)

    def pair(index, _):
        start = pl.multiple_of(index * LANES, LANES)
        spans = [pl.ds(pl.multiple_of(part * D + start, LANES), LANES) for part in range(3)]
        query, keys, values = (qkv[:, span] for span in spans)
        grad = grad_mixed[:, pl.ds(start, LANES)]
        totals = [jnp.zeros((slot, LANES), F32) for _ in range(3)]
        for half in range(2):
            head = 2 * index + half
            own = lane((slot, LANES)) // DH == half
            query_own = jnp.where(own, query, 0.0).astype(BF16)
            grad_own = jnp.where(own, grad, 0.0).astype(BF16)
            scores = dot_nt(query_own, keys) * SCALE + bias_of(table, head, slot) + fence[...]
            probs = jnp.exp(scores - column(lse[...], head))
            grad_probs = dot_nt(grad_own, values)
            delta = jnp.sum(grad_probs * probs, axis=-1, keepdims=True)
            grad_scores = probs * (grad_probs - delta)
            grad_scores = grad_scores.astype(BF16)
            turned = pltpu.roll(dot(flip[...], grad_scores), 1, 1, stride=1, stride_axis=0)
            sums[pl.ds(LANE_BIAS + head, 1), :] = jnp.sum(turned, axis=0, keepdims=True)
            totals[0] = totals[0] + dot(grad_scores, jnp.where(own, keys, 0.0).astype(BF16))
            totals[1] = totals[1] + dot_tn(grad_scores, query_own)
            totals[2] = totals[2] + dot_tn(probs.astype(BF16), grad_own)
        for part, factor in enumerate((SCALE, SCALE, 1.0)):
            grad_qkv[:, spans[part]] = (totals[part] * factor).astype(BF16)
        return 0

    lax.fori_loop(0, H // 2, pair, 0)
    x = x_ref[...].astype(F32)
    attn_in = (x * inverse_rms(x) * gains[0:1]).astype(BF16)
    grad_attn_in = jnp.zeros((slot, D), F32)
    for part in range(3):
        span = slice(part * D, (part + 1) * D)
        grad_pk[:, span] = dot_tn(attn_in, grad_qkv[:, span]).astype(BF16)
        grad_attn_in = grad_attn_in + dot_nt(grad_qkv[:, span], pk[:, span])
    back, gain_attn = norm_back(x, gains[0:1], grad_attn_in)
    total = (grad_resid + back).astype(BF16)
    grad_in[...] = total
    pick = one_hot(lane((8, LANES)) == sublane((8, LANES)) + LANE_GAIN)
    row = sublane((8, D))
    gain_grads = jnp.where(row == 0, gain_attn, jnp.where(row == 1, gain_moe, 0.0)).astype(BF16)
    grad_small = dot_tn(moe_in[...], grad_logits) + dot_tn(gain_grads, pick) + dot_nt(onehot[...], sums[...].astype(BF16))
    grad_pk[:, COL_SMALL:] = grad_small.astype(BF16)
    return total


def back_kernel(*refs):
    attend_back(*refs)


def back_turn_kernel(x, *refs):
    ins, (own_weights, back0, back1, dest_row), (grad_pk, grad_in, packed, grad_weights), scratch = (
        refs[:15], refs[15:19], refs[19:23], refs[23:]
    )
    total = attend_back(x, *ins, grad_pk, grad_in, *scratch)
    back = [back0[...].astype(F32), back1[...].astype(F32)]
    dispatch_back(total.astype(F32), own_weights, back, dest_row, packed, grad_weights)


def struct(shape, dtype):
    return jax.ShapeDtypeStruct(shape, dtype)


def cost(flops, moved, exps=0):
    return pl.CostEstimate(flops=int(flops), bytes_accessed=int(moved), transcendentals=int(exps))


def attend_shapes(slot, rows):
    return [
        struct((slot, 3 * D), BF16),
        struct((slot, D), BF16),
        struct((slot, LANES), F32),
        struct((slot, D), F32),
        struct((slot, D), BF16),
        struct((slot, LANES), F32),
        struct((rows, D), BF16),
    ]


def attend_scratch(slot):
    return [pltpu.VMEM((LANES, slot), F32), pltpu.VMEM((slot, slot), F32)]


ATTEND_COST = dict(flops=4 * 10**9, moved=10**7, exps=10**6)


def attend_first(slot, rows):
    return pl.pallas_call(
        first_kernel,
        out_shape=attend_shapes(slot, rows),
        scratch_shapes=attend_scratch(slot),
        cost_estimate=cost(**ATTEND_COST),
        name="attend_first",
    )


def attend_middle(slot, rows):
    return pl.pallas_call(
        middle_kernel,
        out_shape=[struct((slot, D), BF16)] * 3 + attend_shapes(slot, rows),
        scratch_shapes=attend_scratch(slot),
        cost_estimate=cost(**ATTEND_COST),
        name="attend_middle",
    )


def turn(slot, rows):
    return pl.pallas_call(
        turn_kernel,
        out_shape=[struct((slot, D), BF16), struct((rows, D), BF16), struct((slot, LANES), F32)],
        cost_estimate=cost(10**9, 4 * 10**6),
        name="turn",
    )


def back_scratch(slot):
    return attend_scratch(slot) + [
        pltpu.VMEM((slot, D), BF16),
        pltpu.VMEM((slot, 3 * D), BF16),
        pltpu.VMEM((LANES, slot), F32),
        pltpu.VMEM((slot, slot), BF16),
    ]


def attend_backward(slot):
    return pl.pallas_call(
        back_kernel,
        out_shape=[struct((D, WIDE), BF16), struct((slot, D), BF16)],
        scratch_shapes=back_scratch(slot),
        cost_estimate=cost(10**10, 2 * 10**7, 10**6),
        name="attend_backward",
    )


def attend_backward_turn(slot, rows):
    return pl.pallas_call(
        back_turn_kernel,
        out_shape=[
            struct((D, WIDE), BF16),
            struct((slot, D), BF16),
            struct((rows, D), BF16),
            struct((slot, LANES), F32),
        ],
        scratch_shapes=back_scratch(slot),
        cost_estimate=cost(10**10, 2 * 10**7, 10**6),
        name="attend_backward_turn",
    )


def stream(info, local, pieces, wide, tall, sems):
    local_gate_up, local_down = local
    count = wide.shape[-1]

    def copies(slot, source_gate_up, source_down):
        return [
            pltpu.make_async_copy(source_gate_up[0], wide.at[slot, 0], sems.at[slot, 0]),
            pltpu.make_async_copy(source_gate_up[1], wide.at[slot, 1], sems.at[slot, 1]),
            pltpu.make_async_copy(source_down, tall.at[slot], sems.at[slot, 2]),
        ]

    def from_local(step, slot):
        quarter = info[1 + lax.div(step, SUB)]
        start = pl.multiple_of(quarter * (SUB * count) + lax.rem(step, SUB) * count, LANES)
        span = pl.ds(start, count)
        return copies(
            slot, [local_gate_up.at[0, 0, c, :, span] for c in range(2)], local_down.at[0, 0, span, :]
        )

    def from_piece(which, step, slot):
        span = pl.ds(pl.multiple_of(lax.rem(step, SUB) * count, LANES), count)
        gate_up, down = pieces[which]
        return copies(slot, [gate_up.at[c, :, span] for c in range(2)], down.at[span, :])

    def start(step):
        slot = lax.rem(step, 2)

        @pl.when(info[0] == 0)
        def _():
            for copy in from_local(step, slot):
                copy.start()

        for which in range(len(pieces)):

            @pl.when((info[0] != 0) & (lax.div(step, SUB) == which))
            def _():
                for copy in from_piece(which, step, slot):
                    copy.start()

    step = pl.program_id(0)

    @pl.when(step == 0)
    def _():
        start(step)

    @pl.when(step + 1 < pl.num_programs(0))
    def _():
        start(step + 1)

    slot = lax.rem(step, 2)
    for copy in copies(slot, [wide.at[slot, 0], wide.at[slot, 1]], tall.at[slot]):
        copy.wait()
    return slot


ROOT = math.sqrt(2.0 / math.pi)


def expert_kernel(info, rows, local_gate_up, local_down, *refs):
    pieces = [refs[2 * k : 2 * k + 2] for k in range(len(HOPS))]
    result, kept, total, wide, tall, sems = refs[2 * len(HOPS) :]
    slot = stream(info, (local_gate_up, local_down), pieces, wide, tall, sems)
    gate = dot(rows[...], wide[slot, 0])
    up = dot(rows[...], wide[slot, 1])
    kept[0] = gate.astype(BF16)
    kept[1] = up.astype(BF16)
    bent = jnp.tanh(ROOT * (gate + 0.044715 * (gate * gate * gate)))
    hidden = (0.5 * gate * (1.0 + bent) * up).astype(BF16)
    part = dot(hidden, tall[slot])

    @pl.when(pl.program_id(0) == 0)
    def _():
        total[...] = part

    @pl.when(pl.program_id(0) > 0)
    def _():
        total[...] += part

    @pl.when(pl.program_id(0) == pl.num_programs(0) - 1)
    def _():
        result[...] = total[...].astype(BF16)


def expert_back_kernel(info, grads, kept, local_gate_up, local_down, *refs):
    pieces = [refs[2 * k : 2 * k + 2] for k in range(len(HOPS))]
    result, grad_both, hidden_out, total, wide, tall, sems = refs[2 * len(HOPS) :]
    slot = stream(info, (local_gate_up, local_down), pieces, wide, tall, sems)
    grad_hidden = dot_nt(grads[...], tall[slot])
    gate, up = kept[0].astype(F32), kept[1].astype(F32)
    square = gate * gate
    bent = jnp.tanh(ROOT * gate * (1.0 + 0.044715 * square))
    half = 0.5 * (1.0 + bent)
    slope = half + (0.5 * ROOT) * gate * (1.0 - bent * bent) * (1.0 + (3 * 0.044715) * square)
    bent_gate = gate * half
    hidden_out[...] = (bent_gate * up).astype(BF16)
    grad_gate = (grad_hidden * up * slope).astype(BF16)
    grad_up = (grad_hidden * bent_gate).astype(BF16)
    grad_both[0] = grad_gate
    grad_both[1] = grad_up
    part = dot_nt(grad_gate, wide[slot, 0]) + dot_nt(grad_up, wide[slot, 1])

    @pl.when(pl.program_id(0) == 0)
    def _():
        total[...] = part

    @pl.when(pl.program_id(0) > 0)
    def _():
        total[...] += part

    @pl.when(pl.program_id(0) == pl.num_programs(0) - 1)
    def _():
        result[...] = total[...].astype(BF16)


def whole(shape):
    return pl.BlockSpec(shape, lambda j: (0,) * len(shape))


def expert_call(rows, units, back):
    quarter = units // len(HOPS)
    count = quarter // SUB
    steps = len(HOPS) * SUB
    anywhere = pl.BlockSpec(memory_space=pl.ANY)
    scalars = pl.BlockSpec(memory_space=pltpu.SMEM)
    pair = pl.BlockSpec((2, rows, count), lambda j: (0, 0, j))
    sources = [anywhere] * (2 + 2 * len(HOPS))
    scratch = [
        pltpu.VMEM((rows, D), F32),
        pltpu.VMEM((2, 2, D, count), BF16),
        pltpu.VMEM((2, count, D), BF16),
        pltpu.SemaphoreType.DMA((2, 3)),
    ]
    moved = 2 * (3 * D * units + 2 * rows * units + 2 * rows * D)
    if back:
        return pl.pallas_call(
            expert_back_kernel,
            grid=(steps,),
            in_specs=[scalars, whole((rows, D)), pair] + sources,
            out_specs=[whole((rows, D)), pair, pl.BlockSpec((rows, count), lambda j: (0, j))],
            out_shape=[
                struct((rows, D), BF16),
                struct((2, rows, units), BF16),
                struct((rows, units), BF16),
            ],
            scratch_shapes=scratch,
            cost_estimate=cost(6 * rows * D * units, moved, rows * units),
            name="expert_back",
        )
    return pl.pallas_call(
        expert_kernel,
        grid=(steps,),
        in_specs=[scalars, whole((rows, D))] + sources,
        out_specs=[whole((rows, D)), pair],
        out_shape=[struct((rows, D), BF16), struct((2, rows, units), BF16)],
        scratch_shapes=scratch,
        cost_estimate=cost(6 * rows * D * units, moved, rows * units),
        name="expert",
    )


def expert_grads(rows, grads, grad_both, hidden):
    return dot_tn(rows[...], grad_both[0]), dot_tn(rows[...], grad_both[1]), dot_tn(hidden[...], grads[...])


def sent_grads_kernel(rows, grads, grad_both, hidden, out):
    for index, value in enumerate(expert_grads(rows, grads, grad_both, hidden)):
        out[0, index] = value.astype(BF16)


def kept_grads_kernel(rows, grads, grad_both, hidden, arrived, own, other):
    parts = expert_grads(rows, grads, grad_both, hidden)

    @pl.when(pl.program_id(0) == 0)
    def _():
        for index, value in enumerate(parts):
            other[index] = (value + arrived[0, index].astype(F32)).astype(BF16)

    @pl.when(pl.program_id(0) == 1)
    def _():
        for index, value in enumerate(parts):
            own[index] = (value + arrived[0, index].astype(F32)).astype(BF16)


def grads_call(rows, units, sent):
    quarter = units // len(HOPS)
    place = (lambda j: 2 + j) if sent else (lambda j: 1 - j)
    in_specs = [
        whole((rows, D)),
        whole((rows, D)),
        pl.BlockSpec((2, rows, quarter), lambda j: (0, 0, place(j))),
        pl.BlockSpec((rows, quarter), lambda j: (0, place(j))),
    ]
    moved = 2 * (2 * rows * D + 3 * rows * quarter * 2 + 2 * 3 * quarter * D)
    estimate = cost(2 * 6 * rows * D * quarter, moved)
    block = (1, 3, D, quarter)
    if sent:
        return pl.pallas_call(
            sent_grads_kernel,
            grid=(2,),
            in_specs=in_specs,
            out_specs=pl.BlockSpec(block, lambda j: (j, 0, 0, 0)),
            out_shape=struct((2, 3, D, quarter), BF16),
            cost_estimate=estimate,
            name="sent_grads",
        )
    return pl.pallas_call(
        kept_grads_kernel,
        grid=(2,),
        in_specs=in_specs + [pl.BlockSpec(block, lambda j: (1 - j, 0, 0, 0))],
        out_specs=[whole((3, D, quarter))] * 2,
        out_shape=[struct((3, D, quarter), BF16)] * 2,
        cost_estimate=estimate,
        name="kept_grads",
    )


def across(value):
    return lax.ppermute(value, "section", [(0, 1), (1, 0)])


def hop(value, step):
    return lax.ppermute(value, "replica", [(r, r ^ step) for r in range(lax.axis_size("replica"))])


def exchange(value):
    return lax.all_to_all(value, "expert", split_axis=0, concat_axis=0, tiled=True)


def in_order(pieces, replica):
    own, far, near, both = pieces
    odd = replica % 2 == 1
    low = (jnp.where(odd, near, own), jnp.where(odd, own, near))
    high = (jnp.where(odd, both, far), jnp.where(odd, far, both))
    top = replica // 2 == 1
    return [jnp.where(top, b, a) for a, b in zip(low + high, high + low)]


def spread_dense(quarter, experts, replica):
    piece = exchange(jnp.broadcast_to(quarter[None], (experts,) + quarter.shape))
    far = hop(piece, 2)
    near, both = hop(piece, 1), hop(far, 1)
    ordered = in_order([piece, far, near, both], replica)
    return jnp.stack(ordered, axis=1).reshape(D, WIDE)


def reduce_dense(grads, experts, replica):
    parts = grads.reshape(experts, len(HOPS), -1, WIDE)
    pieces = [lax.dynamic_index_in_dim(parts, replica ^ h, 1, keepdims=False) for h in HOPS]
    arrived = hop(jnp.stack(pieces[2:]), 1)
    other = (pieces[1].astype(F32) + arrived[1].astype(F32)).astype(BF16)
    arrived_far = hop(other, 2)
    own = pieces[0].astype(F32) + arrived[0].astype(F32) + arrived_far.astype(F32)
    rows = exchange(own.astype(BF16))
    return jnp.sum(rows.astype(F32), axis=0)


def pack_dense(gains, w_qkv, w_out, router, rel_bias):
    rows, experts = router.shape
    small = jnp.zeros((rows, LANES), BF16)
    small = small.at[:, :experts].set(router)
    small = small.at[:, LANE_GAIN : LANE_GAIN + 2].set(gains.T)
    small = small.at[: rel_bias.shape[0], LANE_BIAS : LANE_BIAS + H].set(rel_bias)
    return jnp.concatenate([w_qkv, w_out, small], axis=1)


def destinations(routes, experts, capacity):
    slot = routes.shape[1]
    hits = (routes[..., None] == jnp.arange(experts, dtype=jnp.int32)).astype(F32)
    places = np.arange(slot)
    before = jnp.asarray(places[:, None] > places[None, :], BF16)
    counts = jnp.einsum(
        "ts,lse->lte", before, jnp.sum(hits, axis=2).astype(BF16), preferred_element_type=F32
    )
    place = jnp.sum(hits * counts[:, :, None, :], axis=-1).astype(jnp.int32)
    return routes * capacity + place


def per_device(
    x_in, cotangent, segments, routes, gains, w_qkv, w_out, router, rel_bias, w_gate_up, w_down
):
    section = lax.axis_index("section")
    replica = lax.axis_index("replica")
    first = section == 0
    experts = router.shape[2]
    slot = x_in.shape[1]
    capacity = 5 * slot // (2 * experts)
    rows = experts * capacity
    units = w_down.shape[2]
    quarter_units = units // len(HOPS)

    def mine(value):
        return lax.dynamic_index_in_dim(value, section, 0, keepdims=False)

    def by_layer(value, swapped):
        return jnp.where(first, value, swapped), jnp.where(first, swapped, value)

    dense = pack_dense(gains[0], w_qkv[0], w_out[0], router[0], rel_bias[0])
    part = dense.shape[0] // len(HOPS)
    dense_quarter = lax.dynamic_slice_in_dim(dense, replica * part, part, 0)
    quarters = by_layer(dense_quarter, across(dense_quarter))
    routed = jnp.stack(
        by_layer(mine(routes[0]), across(lax.dynamic_index_in_dim(routes[0], 1 - section, 0, keepdims=False)))
    )
    start = replica * quarter_units
    gate_up_piece = across(lax.dynamic_slice_in_dim(w_gate_up[0, 0], start, quarter_units, 2))
    down_piece = across(lax.dynamic_slice_in_dim(w_down[0, 0], start, quarter_units, 0))
    gate_up_far, down_far = hop(gate_up_piece, 2), hop(down_piece, 2)
    pieces = [
        gate_up_piece,
        down_piece,
        gate_up_far,
        down_far,
        hop(gate_up_piece, 1),
        hop(down_piece, 1),
        hop(gate_up_far, 1),
        hop(down_far, 1),
    ]
    owners = [replica ^ h for h in HOPS]
    infos = [
        jnp.stack([jnp.where(first, layer, 1 - layer).astype(jnp.int32)] + owners).astype(jnp.int32)
        for layer in range(2)
    ]

    dest = destinations(routed, experts, capacity)
    dest_rows = jnp.swapaxes(dest, 1, 2)
    onehot = jnp.asarray(bucket_rows(slot, experts), BF16)
    segment = mine(segments[:, 0])
    seg_col, seg_row = segment[:, None], segment[None, :]
    x = mine(x_in)
    packs = [spread_dense(quarter, experts, replica) for quarter in quarters]

    def layer_common(layer):
        return (packs[layer], onehot, seg_col, seg_row, routed[layer])

    def experts_forward(layer, packed):
        received = exchange(packed.reshape(experts, capacity, D)).reshape(rows, D)
        result, kept = expert_call(rows, units, False)(infos[layer], received, w_gate_up, w_down, *pieces)
        returned = exchange(result.reshape(experts, capacity, D)).reshape(rows, D)
        return received, kept, returned

    qkv0, mixed0, lse0, resid0, moe_in0, weights0, packed0 = attend_first(slot, rows)(
        x, *layer_common(0), dest_rows[0]
    )
    received0, kept0, returned0 = experts_forward(0, packed0)
    out0, back00, back01, qkv1, mixed1, lse1, resid1, moe_in1, weights1, packed1 = attend_middle(slot, rows)(
        resid0, weights0, dest[0], returned0, *layer_common(1), dest_rows[1]
    )
    received1, kept1, returned1 = experts_forward(1, packed1)
    out1, grad_packed1, grad_weights1 = turn(slot, rows)(
        resid1, weights1, dest[1], dest_rows[1], returned1, mine(cotangent)
    )

    def experts_backward(layer, received, kept, grad_packed):
        arrived = exchange(grad_packed.reshape(experts, capacity, D)).reshape(rows, D)
        result, grad_both, hidden = expert_call(rows, units, True)(
            infos[layer], arrived, kept, w_gate_up, w_down, *pieces
        )
        returned = exchange(result.reshape(experts, capacity, D)).reshape(rows, D)
        sent = grads_call(rows, units, True)(received, arrived, grad_both, hidden)
        own, other = grads_call(rows, units, False)(received, arrived, grad_both, hidden, hop(sent, 1))
        return returned, own.astype(F32) + hop(other, 2).astype(F32)

    grad_returned1, expert_grad1 = experts_backward(1, received1, kept1, grad_packed1)
    grad_dense1, grad_in1, grad_packed0, grad_weights0 = attend_backward_turn(slot, rows)(
        out0, *layer_common(1), dest[1], mine(cotangent), grad_returned1, resid1, moe_in1, weights1, grad_weights1,
        qkv1, mixed1, lse1, weights0, back00, back01, dest_rows[0]
    )
    grad_returned0, expert_grad0 = experts_backward(0, received0, kept0, grad_packed0)
    grad_dense0, grad_in0 = attend_backward(slot)(
        x, *layer_common(0), dest[0], grad_in1, grad_returned0, resid0, moe_in0, weights0, grad_weights0,
        qkv0, mixed0, lse0
    )

    late = lax.ppermute(expert_grad1.astype(BF16), "section", [(0, 1)])
    early = lax.ppermute(expert_grad0.astype(BF16), "section", [(1, 0)])
    expert_grad = jnp.where(
        first, expert_grad0 + early.astype(F32), expert_grad1 + late.astype(F32)
    )
    grad_gate_up = expert_grad[:2][None, None]
    grad_down = expert_grad[2][None, None]

    dense0 = reduce_dense(grad_dense0, experts, replica)
    dense1 = reduce_dense(grad_dense1, experts, replica)
    total = jnp.where(first, dense0, dense1) + across(jnp.where(first, dense1, dense0).astype(BF16)).astype(F32)
    total = total.astype(BF16)
    far = hop(total, 2)
    near, both = hop(total, 1), hop(far, 1)
    grads = jnp.concatenate(in_order([total, far, near, both], replica)).astype(F32)
    small = grads[:, COL_SMALL:]

    def both_micro(value0, value1):
        own, swapped = jnp.where(first, value0, value1), across(jnp.where(first, value1, value0))
        return jnp.stack([jnp.where(first, own, swapped), jnp.where(first, swapped, own)])[None]

    return (
        both_micro(out0, out1),
        both_micro(grad_in0, grad_in1),
        small[:, LANE_GAIN : LANE_GAIN + 2].T[None],
        grads[:, : 3 * D][None],
        grads[:, COL_OUT:COL_SMALL][None],
        small[:, :experts][None],
        small[: rel_bias.shape[1], LANE_BIAS : LANE_BIAS + H][None],
        grad_gate_up,
        grad_down,
    )


def solution(mesh):
    in_specs = (
        P(None, ("expert", "replica"), None),
        P(None, ("expert", "replica"), None),
        P(None, ("expert", "replica"), None),
        P("section", None, ("expert", "replica"), None),
        P("section", None, "expert"),
        P("section", "expert", None),
        P("section", "expert", None),
        P("section", "expert", None),
        P("section", "expert", None),
        P("section", "expert", None, None, None),
        P("section", "expert", None, None),
    )
    out_specs = (
        P("section", None, ("expert", "replica"), None),
        P("section", None, ("expert", "replica"), None),
        P("section", None, "expert"),
        P("section", "expert", None),
        P("section", "expert", None),
        P("section", "expert", None),
        P("section", "expert", None),
        P("section", "expert", None, None, "replica"),
        P("section", "expert", "replica", None),
    )
    return jax.shard_map(
        per_device, mesh=mesh, in_specs=in_specs, out_specs=out_specs, check_vma=False
    )
```

```python
import functools
import math

import jax
import jax.numpy as jnp
import numpy as np
from jax import lax
from jax.experimental import pallas as pl
from jax.experimental.pallas import tpu as pltpu
from jax.sharding import PartitionSpec as P


D = 768
H = 12
DH = 64
NB = 32
MAXDIST = 128
EPS = 1e-06
SCALE = 0.125
MASKED = -1000000000.0

LANES = 128
HALF = D // 2
COL_SMALL = 3 * HALF
WIDE_A = COL_SMALL + LANES
WIDE_B = HALF
WIDE = WIDE_A + WIDE_B
LANE_GAIN = 32
LANE_BIAS = 64
HOPS = (0, 2, 1, 3)
GROUPS = ((0, 1), (3, 2))
SECTION, EXPERT, REPLICA = "section", "expert", "replica"


F32 = jnp.float32
BF16 = jnp.bfloat16


def dot(a, b):
    return lax.dot_general(a, b, (((1,), (0,)), ((), ())), preferred_element_type=F32)


def dot_nt(a, b):
    return lax.dot_general(a, b, (((1,), (1,)), ((), ())), preferred_element_type=F32)


def dot_tn(a, b):
    return lax.dot_general(a, b, (((0,), (0,)), ((), ())), preferred_element_type=F32)


def bucket_ids(size, buckets, reach):
    distance = np.arange(size)
    exact = buckets // 2
    scaled = np.log(np.maximum(distance, 1) / exact) / math.log(reach / exact) * (buckets - exact)
    spread = exact + np.floor(np.maximum(scaled, 0.0)).astype(np.int64)
    return np.where(distance < exact, distance, np.minimum(spread, buckets - 1)).astype(np.int32)


def bucket_rows(slot, experts):
    ids = bucket_ids(slot, NB, MAXDIST)
    rows, held = D // experts, NB // experts
    table = np.zeros((D, slot), np.float32)
    for column in range(slot):
        bucket = ids[(slot - column) % slot]
        table[bucket // held * rows + bucket % held, column] = 1.0
    return table


def lane(shape):
    return lax.broadcasted_iota(jnp.int32, shape, 1)


def sublane(shape):
    return lax.broadcasted_iota(jnp.int32, shape, 0)


def one_hot(mask):
    return jnp.where(mask, 1.0, 0.0).astype(BF16)


def gain_rows(small):
    pick = one_hot(lane((8, LANES)) == sublane((8, LANES)) + LANE_GAIN)
    return dot_nt(pick, small)


def inverse_rms(x):
    return lax.rsqrt(jnp.mean(x * x, axis=-1, keepdims=True) + EPS)


def norm_back(x, gain, grad):
    inverse = inverse_rms(x)
    scaled = grad * gain
    along = jnp.mean(scaled * x, axis=-1, keepdims=True)
    return (
        inverse * scaled - x * (inverse * inverse * inverse * along),
        jnp.sum(grad * x * inverse, axis=0, keepdims=True),
    )


def column(values, index):
    return jnp.sum(jnp.where(lane(values.shape) == index, values, 0.0), axis=1, keepdims=True)


def set_masks(seg_col, seg_row, fence):
    slot = fence.shape[0]
    allowed = (sublane((slot, slot)) >= lane((slot, slot))) & (seg_col[...] == seg_row[...])
    fence[...] = jnp.where(allowed, 0.0, MASKED)


def bias_of(table, head, slot):
    row = table[pl.ds(LANE_BIAS + head, 1), :]
    return pltpu.roll(jnp.broadcast_to(row, (slot, slot)), 0, 1, stride=1, stride_axis=0)


def columns(core, other, part=0):
    half = 1 - core[0] if other else core[0]
    return pl.ds(pl.multiple_of(part * D + half * HALF, LANES), HALF)


def dense_views(refs):
    if len(refs) == 4:
        return refs
    return [ref.at[:, span] for ref in refs for span in (pl.ds(0, WIDE_A), pl.ds(WIDE_A, WIDE_B))]


def mix(x, core, dense, onehot, seg_col, seg_row, qkv, mixed, lse, table, fence):
    slot = x.shape[0]
    small = dense[0][:, COL_SMALL:]
    gains = gain_rows(small)
    table[...] = dot_tn(small, onehot[...])
    set_masks(seg_col, seg_row, fence)
    wide = x[...].astype(F32)
    attn_in = (wide * inverse_rms(wide) * gains[0:1]).astype(BF16)
    for other in range(2):
        value = dot(attn_in, dense[2 * other][...]).astype(BF16)
        for part in range(3):
            qkv[:, columns(core, other, part)] = value[:, part * HALF : (part + 1) * HALF]
    lse[...] = jnp.zeros_like(lse)

    def pair(index, _):
        start = pl.multiple_of(index * LANES, LANES)
        query = qkv[:, pl.ds(start, LANES)]
        keys = qkv[:, pl.ds(pl.multiple_of(D + start, LANES), LANES)]
        values = qkv[:, pl.ds(pl.multiple_of(2 * D + start, LANES), LANES)]
        total = jnp.zeros((slot, LANES), F32)
        for half in range(2):
            head = 2 * index + half
            own = lane((slot, LANES)) // DH == half
            scores = dot_nt(jnp.where(own, query, 0.0).astype(BF16), keys) * SCALE
            scores = scores + bias_of(table, head, slot) + fence[...]
            top = jnp.max(scores, axis=-1, keepdims=True)
            powers = jnp.exp(scores - top)
            norm = jnp.sum(powers, axis=-1, keepdims=True)
            probs = (powers / norm).astype(BF16)
            total = total + dot(probs, jnp.where(own, values, 0.0).astype(BF16))
            lse[...] = jnp.where(lane((slot, LANES)) == head, top + jnp.log(norm), lse[...])
        mixed[:, pl.ds(start, LANES)] = total.astype(BF16)
        return 0

    lax.fori_loop(0, H // 2, pair, 0)


def project(x, core, small, outs, mixed, routes, dest_row, resid, moe_in, weights, *packed):
    slot = x.shape[0]
    gains = gain_rows(small)
    for other in range(2):
        span = columns(core, other)
        resid[:, span] = x[:, span].astype(F32) + dot(mixed[...], outs[other][...])
    after = resid[...]
    normed = (after * inverse_rms(after) * gains[1:2]).astype(BF16)
    moe_in[...] = normed
    logits = dot(normed, small)
    chosen = [
        jnp.sum(jnp.where(lane(logits.shape) == routes[:, k : k + 1], logits, 0.0), axis=1, keepdims=True)
        for k in range(2)
    ]
    first = jax.nn.sigmoid(chosen[0] - chosen[1])
    second = jax.nn.sigmoid(chosen[1] - chosen[0])
    places = lane((slot, LANES))
    weights[...] = jnp.where(places == 0, first, jnp.where(places == 1, second, 0.0))
    for index, piece in enumerate(packed):
        rows = sublane((piece.shape[0], slot)) + index * piece.shape[0]
        spread = one_hot((rows == dest_row[0:1, :]) | (rows == dest_row[1:2, :]))
        piece[...] = dot(spread, normed).astype(BF16)


def fetch_rows(dest_col, returned, indices):
    slot = dest_col.shape[0]
    total = jnp.zeros((slot, D), F32)
    for number, piece in enumerate(returned):
        places = lane((slot, piece.shape[0])) + number * piece.shape[0]
        mask = places == dest_col[:, indices[0] : indices[0] + 1]
        for index in indices[1:]:
            mask = mask | (places == dest_col[:, index : index + 1])
        total = total + dot(one_hot(mask), piece[...])
    return total


def combine(resid, weights, dest_col, returned):
    back = [fetch_rows(dest_col, returned, [k]) for k in range(2)]
    out = resid[...] + column(weights[...], 0) * back[0] + column(weights[...], 1) * back[1]
    return out.astype(BF16), back


def dispatch_back(grad, weights, back, dest_row, packed, grad_weights):
    slot = grad.shape[0]
    places = lane((slot, LANES))
    sums = [jnp.sum(grad * back[k], axis=-1, keepdims=True) for k in range(2)]
    grad_weights[...] = jnp.where(places == 0, sums[0], jnp.where(places == 1, sums[1], 0.0))
    scaled = [(column(weights[...], k) * grad).astype(BF16) for k in range(2)]
    for index, piece in enumerate(packed):
        rows = sublane((piece.shape[0], slot)) + index * piece.shape[0]
        total = dot(one_hot(rows == dest_row[0:1, :]), scaled[0]) + dot(one_hot(rows == dest_row[1:2, :]), scaled[1])
        piece[...] = total.astype(BF16)


def mix_kernel(core, x, own_a, other_a, onehot, seg_col, seg_row, qkv, mixed, lse, small, *scratch):
    small[...] = own_a[:, COL_SMALL:]
    mix(x, core, (own_a, None, other_a), onehot, seg_col, seg_row, qkv, mixed, lse, *scratch)


def project_kernel(core, x, small, own_b, other_b, *refs):
    project(x, core, small[...], (own_b, other_b), *refs)


def middle_kernel(count, core, resid, weights, dest_col, *refs):
    returned, refs = refs[:count], refs[count:]
    dense, (onehot, seg_col, seg_row, routes, dest_row), refs = dense_views(refs[:2]), refs[2:7], refs[7:]
    (out, back0, back1, qkv, mixed, lse), projected, scratch = refs[:6], refs[6:-2], refs[-2:]
    after, back = combine(resid, weights, dest_col, returned)
    out[...] = after
    back0[...] = back[0].astype(BF16)
    back1[...] = back[1].astype(BF16)
    mix(out, core, dense, onehot, seg_col, seg_row, qkv, mixed, lse, *scratch)
    project(out, core, dense[0][:, COL_SMALL:], (dense[1], dense[3]), mixed, routes, dest_row, *projected)


def turn_kernel(count, resid, weights, dest_col, dest_row, cotangent, *refs):
    returned, out, packed, grad_weights = refs[:count], refs[count], refs[count + 1 : -1], refs[-1]
    after, back = combine(resid, weights, dest_col, returned)
    out[...] = after
    dispatch_back(cotangent[...].astype(F32), weights, back, dest_row, packed, grad_weights)


def attend_back(core, x_ref, dense, onehot, seg_col, seg_row, routes, dest_col, grad_out, resid, moe_in, weights, grad_weights,
                qkv, mixed, lse, returned, grad_own, grad_other, grad_in, table, fence, grad_mixed, grad_qkv, sums, flip, grad_attn):
    slot = resid.shape[0]
    outs = (grad_own, grad_other)
    small = dense[0][:, COL_SMALL:]
    gains = gain_rows(small)
    table[...] = dot_tn(small, onehot[...])
    set_masks(seg_col, seg_row, fence)
    grad_moe = fetch_rows(dest_col, returned, [0, 1])
    first, second = column(weights[...], 0), column(weights[...], 1)
    diff = column(grad_weights[...], 0) * first * (1.0 - first) - column(grad_weights[...], 1) * second * (1.0 - second)
    spots = lane((slot, LANES))
    grad_logits = jnp.where(
        spots == routes[:, 0:1], diff, jnp.where(spots == routes[:, 1:2], -diff, 0.0)
    ).astype(BF16)
    grad_moe = grad_moe + dot_nt(grad_logits, small)
    back, gain_moe = norm_back(resid[...], gains[1:2], grad_moe)
    grad_resid = grad_out[...].astype(F32) + back
    grad_attn[...] = grad_resid.astype(BF16)
    parts = [grad_attn[:, columns(core, other)] for other in range(2)]
    for other in range(2):
        outs[other][:, WIDE_A:] = dot_tn(mixed[...], parts[other]).astype(BF16)
    grad_mixed[...] = (
        dot_nt(parts[0], dense[1][...]) + dot_nt(parts[1], dense[3][...])
    ).astype(BF16)
    sums[...] = jnp.zeros_like(sums)
    flip[...] = one_hot(sublane((slot, slot)) + lane((slot, slot)) == slot - 1)

    def pair(index, _):
        start = pl.multiple_of(index * LANES, LANES)
        spans = [pl.ds(pl.multiple_of(part * D + start, LANES), LANES) for part in range(3)]
        query, keys, values = (qkv[:, span] for span in spans)
        grad = grad_mixed[:, pl.ds(start, LANES)]
        totals = [jnp.zeros((slot, LANES), F32) for _ in range(3)]
        for half in range(2):
            head = 2 * index + half
            own = lane((slot, LANES)) // DH == half
            query_own = jnp.where(own, query, 0.0).astype(BF16)
            grad_own = jnp.where(own, grad, 0.0).astype(BF16)
            scores = dot_nt(query_own, keys) * SCALE + bias_of(table, head, slot) + fence[...]
            probs = jnp.exp(scores - column(lse[...], head))
            grad_probs = dot_nt(grad_own, values)
            delta = jnp.sum(grad_probs * probs, axis=-1, keepdims=True)
            grad_scores = (probs * (grad_probs - delta)).astype(BF16)
            turned = pltpu.roll(dot(flip[...], grad_scores), 1, 1, stride=1, stride_axis=0)
            sums[pl.ds(LANE_BIAS + head, 1), :] = jnp.sum(turned, axis=0, keepdims=True)
            totals[0] = totals[0] + dot(grad_scores, jnp.where(own, keys, 0.0).astype(BF16))
            totals[1] = totals[1] + dot_tn(grad_scores, query_own)
            totals[2] = totals[2] + dot_tn(probs.astype(BF16), grad_own)
        for part, factor in enumerate((SCALE, SCALE, 1.0)):
            grad_qkv[:, spans[part]] = (totals[part] * factor).astype(BF16)
        return 0

    lax.fori_loop(0, H // 2, pair, 0)
    x = x_ref[...].astype(F32)
    attn_in = (x * inverse_rms(x) * gains[0:1]).astype(BF16)
    grad_attn_in = jnp.zeros((slot, D), F32)
    for other in range(2):
        grads = jnp.concatenate([grad_qkv[:, columns(core, other, part)] for part in range(3)], axis=1)
        outs[other][:, :COL_SMALL] = dot_tn(attn_in, grads).astype(BF16)
        grad_attn_in = grad_attn_in + dot_nt(grads, dense[2 * other][:, :COL_SMALL])
    back, gain_attn = norm_back(x, gains[0:1], grad_attn_in)
    total = (grad_resid + back).astype(BF16)
    grad_in[...] = total
    pick = one_hot(lane((8, LANES)) == sublane((8, LANES)) + LANE_GAIN)
    row = sublane((8, D))
    gain_grads = jnp.where(row == 0, gain_attn, jnp.where(row == 1, gain_moe, 0.0)).astype(BF16)
    grad_small = dot_tn(moe_in[...], grad_logits) + dot_tn(gain_grads, pick) + dot_nt(onehot[...], sums[...].astype(BF16))
    for out in outs:
        out[:, COL_SMALL:WIDE_A] = grad_small.astype(BF16)
    return total


def back_kernel(count, core, x, *refs):
    dense, refs = dense_views(refs[:4]), refs[4:]
    common, returned, rest = refs[:13], refs[13 : 13 + count], refs[13 + count :]
    attend_back(core, x, dense, *common, returned, *rest)


def back_turn_kernel(count, core, x, *refs):
    dense, refs = dense_views(refs[:2]), refs[2:]
    common, returned, refs = refs[:13], refs[13 : 13 + count], refs[13 + count :]
    own_weights, back0, back1, dest_row, grad_own, grad_other, grad_in = refs[:7]
    packed, grad_weights, scratch = refs[7 : 7 + count], refs[7 + count], refs[8 + count :]
    total = attend_back(core, x, dense, *common, returned, grad_own, grad_other, grad_in, *scratch)
    back = [back0[...].astype(F32), back1[...].astype(F32)]
    dispatch_back(total.astype(F32), own_weights, back, dest_row, packed, grad_weights)


def struct(shape, dtype):
    return jax.ShapeDtypeStruct(shape, dtype)


def cost(flops, moved, exps=0):
    return pl.CostEstimate(flops=int(flops), bytes_accessed=int(moved), transcendentals=int(exps))


def mix_shapes(slot):
    return [struct((slot, 3 * D), BF16), struct((slot, D), BF16), struct((slot, LANES), F32)]


def project_shapes(slot, packed):
    return [
        struct((slot, D), F32),
        struct((slot, D), BF16),
        struct((slot, LANES), F32),
    ] + packed


def attend_scratch(slot):
    return [pltpu.VMEM((LANES, slot), F32), pltpu.VMEM((slot, slot), F32)]


def back_scratch(slot):
    return attend_scratch(slot) + [
        pltpu.VMEM((slot, D), BF16),
        pltpu.VMEM((slot, 3 * D), BF16),
        pltpu.VMEM((LANES, slot), F32),
        pltpu.VMEM((slot, slot), BF16),
        pltpu.VMEM((slot, D), BF16),
    ]


def back_shapes(slot):
    return [struct((D, WIDE), BF16)] * 2 + [struct((slot, D), BF16)]


def kernel_call(body, inputs, out_shape, scratch, estimate, scalars=1):
    specs = [pl.BlockSpec(memory_space=pltpu.SMEM if k < scalars else pltpu.VMEM) for k in range(len(inputs))]
    return pl.pallas_call(
        body,
        in_specs=specs,
        out_shape=out_shape,
        scratch_shapes=scratch,
        cost_estimate=estimate,
    )(*inputs)


def stream(info, local, pieces, wide, tall, sems):
    local_gate_up, local_down = local
    count = wide.shape[-1]

    half = count // 2

    def copies(slot, gate, up, low, high):
        return [
            pltpu.make_async_copy(gate, wide.at[slot, 0], sems.at[slot, 0]),
            pltpu.make_async_copy(up, wide.at[slot, 1], sems.at[slot, 1]),
            pltpu.make_async_copy(low, tall.at[slot, pl.ds(0, half)], sems.at[slot, 2]),
            pltpu.make_async_copy(high, tall.at[slot, pl.ds(half, half)], sems.at[slot, 3]),
        ]

    def start(step):
        slot = lax.rem(step, 2)

        @pl.when(info[0] == 0)
        def _():
            first = pl.multiple_of(info[1 + step] * count, LANES)
            gate, up = (local_gate_up.at[0, 0, c, :, pl.ds(first, count)] for c in range(2))
            low, high = (local_down.at[0, 0, pl.ds(first + c * half, half), :] for c in range(2))
            for copy in copies(slot, gate, up, low, high):
                copy.start()

        for which in range(len(pieces)):

            @pl.when((info[0] != 0) & (step == which))
            def _():
                for copy in copies(slot, *pieces[which]):
                    copy.start()

    step = pl.program_id(0)

    @pl.when(step == 0)
    def _():
        start(step)

    @pl.when(step + 1 < len(pieces))
    def _():
        start(step + 1)

    slot = lax.rem(step, 2)
    for copy in copies(slot, wide.at[slot, 0], wide.at[slot, 1], *(tall.at[slot, pl.ds(c * half, half)] for c in range(2))):
        copy.wait()
    return slot


ROOT = math.sqrt(2.0 / math.pi)


ARRAYS = 4


def join(refs, scratch):
    at = 0
    for ref in refs:
        span = slice(at, at + ref.shape[-2])
        at += ref.shape[-2]
        scratch[..., span, :] = ref[...]


def accumulate(total, part, results):
    @pl.when(pl.program_id(0) == 0)
    def _():
        total[...] = part

    @pl.when(pl.program_id(0) > 0)
    def _():
        total[...] += part

    @pl.when(pl.program_id(0) == len(HOPS) - 1)
    def _():
        for index, result in enumerate(results):
            count = result.shape[0]
            result[...] = total[index * count : (index + 1) * count, :].astype(BF16)


def split_refs(refs, count):
    sources, refs = refs[: ARRAYS * len(HOPS)], refs[ARRAYS * len(HOPS) :]
    return [sources[ARRAYS * k : ARRAYS * k + ARRAYS] for k in range(len(HOPS))], refs[:count], refs[count:]


def expert_kernel(count, info, *refs):
    rows, local, refs = refs[:count], refs[count : count + 2], refs[count + 2 :]
    pieces, results, (kept, shared, joined, total, wide, tall, sems) = split_refs(refs, count)

    @pl.when(pl.program_id(0) == 0)
    def _():
        join(rows, joined)

    @pl.when(pl.program_id(0) < len(pieces))
    def _():
        slot = stream(info, local, pieces, wide, tall, sems)
        gate = dot(joined[...], wide[slot, 0])
        up = dot(joined[...], wide[slot, 1])
        kept[0] = gate.astype(BF16)
        kept[1] = up.astype(BF16)
        bent = jnp.tanh(ROOT * (gate + 0.044715 * (gate * gate * gate)))
        hidden = (0.5 * gate * (1.0 + bent) * up).astype(BF16)
        shared[0] = hidden
        accumulate(total, dot(hidden, tall[slot]), results)

    @pl.when(pl.program_id(0) == len(pieces))
    def _():
        shared[0] = joined[...]


def expert_back_kernel(count, info, *refs):
    grads, kept, local, refs = refs[:count], refs[count], refs[count + 1 : count + 3], refs[count + 3 :]
    pieces, results, (shared, joined, total, wide, tall, sems) = split_refs(refs, count)

    @pl.when(pl.program_id(0) == 0)
    def _():
        join(grads, joined)

    @pl.when(pl.program_id(0) < len(pieces))
    def _():
        slot = stream(info, local, pieces, wide, tall, sems)
        grad_hidden = dot_nt(joined[...], tall[slot])
        gate, up = kept[0].astype(F32), kept[1].astype(F32)
        square = gate * gate
        bent = jnp.tanh(ROOT * gate * (1.0 + 0.044715 * square))
        half = 0.5 * (1.0 + bent)
        slope = half + (0.5 * ROOT) * gate * (1.0 - bent * bent) * (1.0 + (3 * 0.044715) * square)
        grad_gate = (grad_hidden * up * slope).astype(BF16)
        grad_up = (grad_hidden * gate * half).astype(BF16)
        shared[0, 0] = grad_gate
        shared[0, 1] = grad_up
        accumulate(total, dot_nt(grad_gate, wide[slot, 0]) + dot_nt(grad_up, wide[slot, 1]), results)

    @pl.when(pl.program_id(0) == len(pieces))
    def _():
        for c in range(2):
            shared[0, c] = joined[...]


def whole(shape):
    return pl.BlockSpec(shape, lambda j: (0,) * len(shape))


def expert_call(info, rows, weights, kept=None):
    steps, count = len(HOPS), len(rows)
    held, units = rows[0].shape[0], weights[1].shape[2]
    quarter, joint = units // steps, held * count
    anywhere = pl.BlockSpec(memory_space=pl.ANY)
    pair = pl.BlockSpec((2, joint, quarter), lambda j: (0, 0, jnp.minimum(j, steps - 1)))
    out_specs = [whole((held, D))] * count
    out_shape = [struct((held, D), BF16)] * count
    extra = [] if kept is None else [kept]
    if kept is None:
        out_specs += [pair, pl.BlockSpec((1, joint, quarter), lambda j: (j, 0, 0))]
        out_shape += [struct((2, joint, units), BF16), struct((steps + 1, joint, quarter), BF16)]
    else:
        out_specs.append(pl.BlockSpec((1, 2, joint, quarter), lambda j: (j, 0, 0, 0)))
        out_shape.append(struct((steps + 1, 2, joint, quarter), BF16))
    outs = pl.pallas_call(
        functools.partial(expert_kernel if kept is None else expert_back_kernel, count),
        grid=(steps + 1,),
        in_specs=[pl.BlockSpec(memory_space=pltpu.SMEM)]
        + [whole((held, D))] * count
        + [pair] * len(extra)
        + [anywhere] * len(weights),
        out_specs=out_specs,
        out_shape=out_shape,
        scratch_shapes=[
            pltpu.VMEM((joint, D), BF16),
            pltpu.VMEM((joint, D), F32),
            pltpu.VMEM((2, 2, D, quarter), BF16),
            pltpu.VMEM((2, quarter, D), BF16),
            pltpu.SemaphoreType.DMA((2, ARRAYS)),
        ],
        cost_estimate=cost(
            6 * joint * D * units, 2 * (3 * D * units + 2 * joint * units + 2 * joint * D), joint * units
        ),
    )(info, *rows, *extra, *weights)
    return outs[:count], *outs[count:]


THIRDS = 3


def grads_kernel(groups, *refs):
    rows_in, grads_in, hidden, both = (refs[2 * k * groups : 2 * (k + 1) * groups] for k in range(4))
    outs, (rows, grads, joined, pair) = refs[8 * groups : -4], refs[-4:]

    @pl.when(pl.program_id(0) + pl.program_id(1) == 0)
    def _():
        join([ref.at[0] for ref in rows_in], rows)
        join([ref.at[0, 0] for ref in grads_in], grads)

    join([ref.at[0] for ref in hidden], joined)
    join([ref.at[0] for ref in both], pair)
    values = [dot_tn(rows[...], pair[0]), dot_tn(rows[...], pair[1]), dot_tn(joined[...], grads[...])]
    for place in range(2):

        @pl.when(pl.program_id(0) == place)
        def _():
            for index, value in enumerate(values):
                outs[3 * place + index][...] = value.astype(BF16)


def grads_call(hidden, other_hidden, both, other_both):
    groups, steps, joint, quarter = len(hidden), len(HOPS), hidden[0].shape[1], hidden[0].shape[2]
    part, total = quarter // THIRDS, 2 * len(hidden) * hidden[0].shape[1]

    def specs(block, place):
        return [pl.BlockSpec(block, functools.partial(place, other)) for other in (0, 2) for _ in range(groups)]

    in_specs = [
        *specs((1, joint, quarter), lambda other, j, i: (steps, 0, 0)),
        *specs((1, 1, joint, quarter), lambda other, j, i: (steps, 0, 0, 0)),
        *specs((1, joint, part), lambda other, j, i: (1 - j + other, 0, i)),
        *specs((1, 2, joint, part), lambda other, j, i: (1 - j + other, 0, 0, i)),
    ]

    def placed(place, i, j):
        return jnp.where(j == place, i, (THIRDS - 1) * (1 - place))

    out_specs = []
    for place in range(2):
        out_specs += [pl.BlockSpec((D, part), functools.partial(lambda place, j, i: (0, placed(place, i, j)), place))] * 2
        out_specs.append(pl.BlockSpec((part, D), functools.partial(lambda place, j, i: (placed(place, i, j), 0), place)))
    hiddens, boths = [*hidden, *other_hidden], [*both, *other_both]
    return pl.pallas_call(
        functools.partial(grads_kernel, groups),
        grid=(2, THIRDS),
        in_specs=in_specs,
        out_specs=out_specs,
        out_shape=[struct((D, quarter), BF16)] * 6,
        scratch_shapes=[
            pltpu.VMEM((total, D), BF16),
            pltpu.VMEM((total, D), BF16),
            pltpu.VMEM((total, part), BF16),
            pltpu.VMEM((2, total, part), BF16),
        ],
        cost_estimate=cost(12 * total * D * quarter, 4 * total * (D + 3 * quarter)),
    )(*hiddens, *boths, *hiddens, *boths)


def finish_kernel(first, sums0, sums1, came0, came1, *refs):
    out = refs[-1]

    @pl.when(first[0] == 1)
    def _():
        out[...] = sums0[...].astype(F32) + came0[...].astype(F32)

    @pl.when(first[0] == 0)
    def _():
        out[...] = sums1[...].astype(F32) + came1[...].astype(F32)


def finish(first, arrays, rows, start, base=None):
    count, width = arrays[0].shape
    block = D // 4
    specs = [pl.BlockSpec(memory_space=pltpu.SMEM)] + [pl.BlockSpec((block, width), lambda j: (j, 0))] * 4
    extra = [] if base is None else [base]
    return pl.pallas_call(
        finish_kernel,
        grid=(count // block,),
        in_specs=specs + [pl.BlockSpec(memory_space=pl.ANY)] * len(extra),
        out_specs=pl.BlockSpec((block, width), lambda j: (j + start // block, 0)),
        out_shape=struct((rows, width), F32),
        input_output_aliases={5: 0} if extra else {},
        cost_estimate=cost(4 * count * width, 12 * count * width),
    )(first, *arrays, *extra)


def across(value, pairs=((0, 1), (1, 0))):
    return lax.ppermute(value, SECTION, pairs)


def hop(value, step):
    return lax.ppermute(value, REPLICA, [(r, r ^ step) for r in range(lax.axis_size(REPLICA))])


def swap(value, step):
    if step == 0:
        return value
    return lax.ppermute(value, EXPERT, [(e, e ^ step) for e in range(lax.axis_size(EXPERT))])


def exchange(value, experts):
    return lax.all_to_all(
        value.reshape(experts, -1, value.shape[-1]), EXPERT, split_axis=0, concat_axis=0, tiled=True
    ).reshape(value.shape)


def groups_of(experts):
    return GROUPS if experts == 4 else ((None,),)


def group_exchange(groups, experts):
    def travel(which, pieces):
        if groups[which] == (None,):
            return [exchange(pieces[0], experts)]
        return [swap(piece, step) for piece, step in zip(pieces, groups[which])]

    return travel


def spread(value, experts, me):
    if experts != 4:
        return exchange(jnp.concatenate([value] * experts), experts)
    came = {step: swap(value, step) for step in (3, 2, 1, 0)}
    for bit in (1, 2):
        flag = me & bit != 0
        came = {step: jnp.where(flag, came[step ^ bit], came[step]) for step in came}
    return jnp.concatenate([came[step] for step in range(4)])


def gathered_sum(parts, experts):
    return jnp.sum(exchange(parts, experts).reshape(experts, -1, WIDE).astype(F32), axis=0)


def ordered(top, mine, theirs):
    return jnp.where(top, theirs, mine), jnp.where(top, mine, theirs)


def joined_cores(own, other):
    return (own.astype(F32) + hop(other, 1).astype(F32)).astype(BF16)


def joined_chips(pair, top):
    mine, theirs = ordered(top, *pair)
    return (mine.astype(F32) + hop(theirs, 2).astype(F32)).astype(BF16)


def anchor_kernel(value, out):
    for index in range(value.shape[0]):
        out[index] = value[index]


def anchor(value):
    scalars = pl.BlockSpec(memory_space=pltpu.SMEM)
    return pl.pallas_call(
        anchor_kernel, in_specs=[scalars], out_specs=scalars, out_shape=struct(value.shape, value.dtype)
    )(value)


def destinations(routes, experts, capacity, me):
    slot = routes.shape[1]
    hits = (routes[..., None] == jnp.arange(experts, dtype=jnp.int32)).astype(F32)
    places = np.arange(slot)
    before = jnp.asarray(places[:, None] > places[None, :], BF16)
    counts = jnp.einsum(
        "ts,lse->lte", before, jnp.sum(hits, axis=2).astype(BF16), preferred_element_type=F32
    )
    place = jnp.sum(hits * counts[:, :, None, :], axis=-1).astype(jnp.int32)
    if experts == 4:
        routes = routes ^ me
        routes = routes ^ (routes >> 1)
    return routes * capacity + place


def step(x_in, cotangent, segments, routes, gains, w_qkv, w_out, router, rel_bias, w_gate_up, w_down):
    section = lax.axis_index(SECTION)
    replica = lax.axis_index(REPLICA)
    me = lax.axis_index(EXPERT)
    first = section == 0
    core = replica % 2
    odd, top = core == 1, replica // 2 == 1
    experts = router.shape[2]
    held = w_qkv.shape[1]
    slot = x_in.shape[1]
    capacity = 5 * slot // (2 * experts)
    groups = groups_of(experts)
    count = sum(len(group) for group in groups)
    packed_shapes = [struct((experts * capacity // count, D), BF16)] * count
    units = w_down.shape[2]
    quarter = units // len(HOPS)
    core_info = anchor(core.astype(jnp.int32)[None])
    first_info = anchor(first.astype(jnp.int32)[None])

    def mine(value):
        return lax.dynamic_index_in_dim(value, section, 0, keepdims=False)

    def by_layer(value, swapped):
        return jnp.where(first, value, swapped), jnp.where(first, swapped, value)

    def half_of(value, part=0):
        return lax.dynamic_slice_in_dim(value, part * D + core * HALF, HALF, 1)

    def placed(value, start):
        return jnp.pad(value, ((0, held - value.shape[0]), (start, LANES - start - value.shape[1])))

    def grouped(values):
        values = list(values)
        return [[values.pop(0) for _ in group] for group in groups]

    routed = jnp.stack(
        by_layer(mine(routes[0]), across(lax.dynamic_index_in_dim(routes[0], 1 - section, 0, keepdims=False)))
    )
    small = placed(router[0], 0) + placed(gains[0].T, LANE_GAIN) + placed(rel_bias[0], LANE_BIAS)
    dense_a = jnp.concatenate([half_of(w_qkv[0], part) for part in range(3)] + [small], axis=1)
    dense_b = half_of(w_out[0])
    halves_a, halves_b = by_layer(dense_a, across(dense_a)), by_layer(dense_b, across(dense_b))

    start = replica * quarter
    near = [
        lax.dynamic_slice(w_gate_up, (0, 0, c, 0, start), (1, 1, 1, D, quarter)).reshape(D, quarter) for c in range(2)
    ] + [lax.dynamic_slice_in_dim(w_down[0, 0], start + c * (quarter // 2), quarter // 2, 0) for c in range(2)]
    near = [across(piece) for piece in near]
    far = [hop(piece, 2) for piece in near]
    weights = [w_gate_up, w_down, *near, *far]
    weights += [hop(piece, 1) for piece in near + far]
    owners = [replica ^ h for h in HOPS]
    infos = [
        anchor(jnp.stack([jnp.where(first, layer, 1 - layer).astype(jnp.int32)] + owners).astype(jnp.int32))
        for layer in range(2)
    ]

    dest = destinations(routed, experts, capacity, me)
    dest_rows = jnp.swapaxes(dest, 1, 2)
    onehot = jnp.asarray(bucket_rows(slot, experts), BF16)
    segment = mine(segments[:, 0])
    seg_col, seg_row = segment[:, None], segment[None, :]
    x = mine(x_in)
    cot = mine(cotangent)

    own_a0 = spread(halves_a[0], experts, me)
    own_b0 = spread(halves_b[0], experts, me)
    dense0 = (own_a0, own_b0, hop(own_a0, 1), hop(own_b0, 1))
    block = held // 4
    part = jnp.concatenate([halves_a[1], halves_b[1]], axis=1)
    part = lax.dynamic_slice_in_dim(part, (replica // 2 * 2 + section) * block, block, 0)
    part = spread(part, experts, me)

    def doubled(flag, value, came):
        pair = ordered(flag, value.reshape(experts, -1, WIDE), came.reshape(experts, -1, WIDE))
        return jnp.concatenate(pair, axis=1).reshape(-1, WIDE)

    part = doubled(jnp.logical_not(first), part, across(part))
    own1 = doubled(top, part, hop(part, 2))
    dense1 = (own1, hop(own1, 1))

    attend_cost = cost(4 * 10**9, 10**7, 10**6)
    back_cost = cost(10**10, 2 * 10**7, 10**6)

    def experts_forward(layer, packed):
        send = group_exchange(groups, experts)
        give = group_exchange(groups, experts)
        kept, hidden, came, returned = [], [], [], []
        for g, pieces in enumerate(grouped(packed)):
            results, both, shared = expert_call(infos[layer], send(g, pieces), weights)
            kept.append(both)
            hidden.append(shared)
            returned += give(g, results)
            came.append(hop(shared, 1))
        return (kept, hidden, came), returned

    common0 = (onehot, seg_col, seg_row, routed[0])
    common1 = (onehot, seg_col, seg_row, routed[1])
    qkv0, mixed0, lse0, small0 = kernel_call(
        mix_kernel, (core_info, x, own_a0, dense0[2], onehot, seg_col, seg_row),
        mix_shapes(slot) + [struct((D, LANES), BF16)], attend_scratch(slot), attend_cost,
    )
    resid0, moe_in0, weights0, *packed0 = kernel_call(
        project_kernel, (core_info, x, small0, own_b0, dense0[3], mixed0, routed[0], dest_rows[0]),
        project_shapes(slot, packed_shapes), [], cost(10**9, 4 * 10**6),
    )
    saved0, returned0 = experts_forward(0, packed0)
    out0, back00, back01, qkv1, mixed1, lse1, resid1, moe_in1, weights1, *packed1 = kernel_call(
        functools.partial(middle_kernel, count),
        (core_info, resid0, weights0, dest[0], *returned0, *dense1, *common1, dest_rows[1]),
        [struct((slot, D), BF16)] * 3 + mix_shapes(slot) + project_shapes(slot, packed_shapes),
        attend_scratch(slot), attend_cost,
    )
    saved1, returned1 = experts_forward(1, packed1)
    out1, *packed1, grad_weights1 = kernel_call(
        functools.partial(turn_kernel, count), (resid1, weights1, dest[1], dest_rows[1], cot, *returned1),
        [struct((slot, D), BF16)] + packed_shapes + [struct((slot, LANES), F32)], [],
        cost(10**9, 4 * 10**6), scalars=0,
    )

    def experts_backward(layer, saved, packed):
        kept, hidden, came = saved
        send = group_exchange(groups, experts)
        give = group_exchange(groups, experts)
        both, came_back, returned = [], [], []
        for g, pieces in enumerate(grouped(packed)):
            results, shared = expert_call(infos[layer], send(g, pieces), weights, kept[g])
            both.append(shared)
            returned += give(g, results)
            came_back.append(hop(shared, 1))
        grads = grads_call(hidden, came, both, came_back)
        summed = []
        for k in range(3):
            came_far = hop(grads[k], 2)
            for span in ((slice(0, D // 2), slice(D // 2, D)) if k == 1 else (slice(None),)):
                summed.append((grads[3 + k][span].astype(F32) + came_far[span].astype(F32)).astype(BF16))
        pairs = ((0, 1),) if layer else ((1, 0),)
        return returned, [(value, across(value, pairs)) for value in summed]

    grad_returned1, expert_sums1 = experts_backward(1, saved1, packed1)
    grad_own1, grad_other1, grad_in1, *grad_packed0, grad_weights0 = kernel_call(
        functools.partial(back_turn_kernel, count),
        (core_info, out0, *dense1, *common1, dest[1], cot, resid1, moe_in1, weights1, grad_weights1, qkv1, mixed1, lse1,
         *grad_returned1, weights0, back00, back01, dest_rows[0]),
        back_shapes(slot) + packed_shapes + [struct((slot, LANES), F32)], back_scratch(slot), back_cost,
    )
    grad_returned0, expert_sums0 = experts_backward(0, saved0, grad_packed0)
    grad_own0, grad_other0, grad_in0 = kernel_call(
        functools.partial(back_kernel, count),
        (core_info, x, *dense0, *common0, dest[0], grad_in1, resid0, moe_in0, weights0, grad_weights0, qkv0, mixed0, lse0,
         *grad_returned0),
        back_shapes(slot), back_scratch(slot), back_cost,
    )
    ended = [(sum0, sum1, came0, came1) for (sum0, came0), (sum1, came1) in zip(expert_sums0, expert_sums1)]
    grad_down = finish(first_info, ended[3], D, 0)[None, None]
    grad_gate_up = finish(first_info, ended[0], 2 * D, 0)
    grad_gate_up = finish(first_info, ended[1], 2 * D, D, grad_gate_up)
    grad_gate_up = finish(first_info, ended[2], 2 * D, D + D // 2, grad_gate_up).reshape(1, 1, 2, D, quarter)

    part = joined_cores(grad_own1, grad_other1).reshape(experts, 2, held // 2, WIDE)
    part = joined_chips((part[:, 0], part[:, 1]), top).reshape(-1, WIDE)
    reduced1 = gathered_sum(part, experts)
    part = gathered_sum(joined_cores(grad_own0, grad_other0), experts).astype(BF16)
    reduced0 = joined_chips((part[: held // 2], part[held // 2 :]), top).astype(F32)
    total = jnp.where(first, reduced0, reduced1)
    for value, pair in ((reduced1, (0, 1)), (reduced0, (1, 0))):
        total = total + across(value.astype(BF16), (pair,)).astype(F32)
    total = total.astype(BF16)
    total = jnp.concatenate(ordered(top, total, hop(total, 2)))
    low, high = (value.astype(F32) for value in ordered(odd, total, hop(total, 1)))
    grad_qkv = jnp.concatenate(
        [value[:, part * HALF : (part + 1) * HALF] for part in range(3) for value in (low, high)], axis=1
    )
    grad_out = jnp.concatenate([value[:, WIDE_A:] for value in (low, high)], axis=1)
    small = low[:, COL_SMALL:WIDE_A]

    def both_micro(value0, value1):
        own, swapped = jnp.where(first, value0, value1), across(jnp.where(first, value1, value0))
        return jnp.stack([jnp.where(first, own, swapped), jnp.where(first, swapped, own)])[None]

    return (
        both_micro(out0, out1),
        both_micro(grad_in0, grad_in1),
        small[:, LANE_GAIN : LANE_GAIN + 2].T[None],
        grad_qkv[None],
        grad_out[None],
        small[:, :experts][None],
        small[: rel_bias.shape[1], LANE_BIAS : LANE_BIAS + H][None],
        grad_gate_up,
        grad_down,
    )


def solution(mesh):
    tokens = P(None, (EXPERT, REPLICA), None)
    layered = P(SECTION, None, (EXPERT, REPLICA), None)
    dense = P(SECTION, EXPERT, None)
    gains = P(SECTION, None, EXPERT)
    in_specs = (tokens,) * 3 + (layered, gains) + (dense,) * 4
    in_specs += (P(SECTION, EXPERT, None, None, None), P(SECTION, EXPERT, None, None))
    out_specs = (layered, layered, gains) + (dense,) * 4
    out_specs += (P(SECTION, EXPERT, None, None, REPLICA), P(SECTION, EXPERT, REPLICA, None))
    return jax.shard_map(step, mesh=mesh, in_specs=in_specs, out_specs=out_specs, check_vma=False)
```

```python
import functools
import math

import jax
import jax.numpy as jnp
import numpy as np
from jax import lax
from jax.experimental import pallas as pl
from jax.experimental.pallas import tpu as pltpu
from jax.sharding import PartitionSpec as P


D = 768
H = 12
DH = 64
NB = 32
MAXDIST = 128
EPS = 1e-06
SCALE = 0.125
MASKED = -1000000000.0

LANES = 128
HALF = D // 2
COL_SMALL = 3 * HALF
WIDE_A = COL_SMALL + LANES
WIDE_B = HALF
WIDE = WIDE_A + WIDE_B
LANE_GAIN = 32
LANE_BIAS = 64
HOPS = (0, 2, 1, 3)
GROUPS = ((0, 1), (3, 2))
SECTION, EXPERT, REPLICA = "section", "expert", "replica"


F32 = jnp.float32
BF16 = jnp.bfloat16


def dot(a, b):
    return lax.dot_general(a, b, (((1,), (0,)), ((), ())), preferred_element_type=F32)


def dot_nt(a, b):
    return lax.dot_general(a, b, (((1,), (1,)), ((), ())), preferred_element_type=F32)


def dot_tn(a, b):
    return lax.dot_general(a, b, (((0,), (0,)), ((), ())), preferred_element_type=F32)


def bucket_ids(size, buckets, reach):
    distance = np.arange(size)
    exact = buckets // 2
    scaled = np.log(np.maximum(distance, 1) / exact) / math.log(reach / exact) * (buckets - exact)
    spread = exact + np.floor(np.maximum(scaled, 0.0)).astype(np.int64)
    return np.where(distance < exact, distance, np.minimum(spread, buckets - 1)).astype(np.int32)


def bucket_rows(slot, experts):
    ids = bucket_ids(slot, NB, MAXDIST)
    rows, held = D // experts, NB // experts
    table = np.zeros((D, slot), np.float32)
    for column in range(slot):
        bucket = ids[(slot - column) % slot]
        table[bucket // held * rows + bucket % held, column] = 1.0
    return table


def lane(shape):
    return lax.broadcasted_iota(jnp.int32, shape, 1)


def sublane(shape):
    return lax.broadcasted_iota(jnp.int32, shape, 0)


def one_hot(mask):
    return jnp.where(mask, 1.0, 0.0).astype(BF16)


def gain_rows(small):
    pick = one_hot(lane((8, LANES)) == sublane((8, LANES)) + LANE_GAIN)
    return dot_nt(pick, small)


def inverse_rms(x):
    return lax.rsqrt(jnp.mean(x * x, axis=-1, keepdims=True) + EPS)


def norm_back(x, gain, grad):
    inverse = inverse_rms(x)
    scaled = grad * gain
    along = jnp.mean(scaled * x, axis=-1, keepdims=True)
    return (
        inverse * scaled - x * (inverse * inverse * inverse * along),
        jnp.sum(grad * x * inverse, axis=0, keepdims=True),
    )


def column(values, index):
    return jnp.sum(jnp.where(lane(values.shape) == index, values, 0.0), axis=1, keepdims=True)


def set_masks(seg_col, seg_row, fence):
    slot = fence.shape[0]
    allowed = (sublane((slot, slot)) >= lane((slot, slot))) & (seg_col[...] == seg_row[...])
    fence[...] = jnp.where(allowed, 0.0, MASKED)


def bias_of(table, head, slot):
    row = table[pl.ds(LANE_BIAS + head, 1), :]
    return pltpu.roll(jnp.broadcast_to(row, (slot, slot)), 0, 1, stride=1, stride_axis=0)


def columns(core, other, part=0):
    half = 1 - core[0] if other else core[0]
    return pl.ds(pl.multiple_of(part * D + half * HALF, LANES), HALF)


def dense_views(refs):
    if len(refs) == 4:
        return refs
    return [ref.at[:, span] for ref in refs for span in (pl.ds(0, WIDE_A), pl.ds(WIDE_A, WIDE_B))]


def mix(x, core, dense, onehot, seg_col, seg_row, qkv, mixed, lse, table, fence):
    slot = x.shape[0]
    small = dense[0][:, COL_SMALL:]
    gains = gain_rows(small)
    table[...] = dot_tn(small, onehot[...])
    set_masks(seg_col, seg_row, fence)
    wide = x[...].astype(F32)
    attn_in = (wide * inverse_rms(wide) * gains[0:1]).astype(BF16)
    for other in range(2):
        value = dot(attn_in, dense[2 * other][...]).astype(BF16)
        for part in range(3):
            qkv[:, columns(core, other, part)] = value[:, part * HALF : (part + 1) * HALF]
    lse[...] = jnp.zeros_like(lse)

    def pair(index, _):
        start = pl.multiple_of(index * LANES, LANES)
        query = qkv[:, pl.ds(start, LANES)]
        keys = qkv[:, pl.ds(pl.multiple_of(D + start, LANES), LANES)]
        values = qkv[:, pl.ds(pl.multiple_of(2 * D + start, LANES), LANES)]
        total = jnp.zeros((slot, LANES), F32)
        for half in range(2):
            head = 2 * index + half
            own = lane((slot, LANES)) // DH == half
            scores = dot_nt(jnp.where(own, query, 0.0).astype(BF16), keys) * SCALE
            scores = scores + bias_of(table, head, slot) + fence[...]
            top = jnp.max(scores, axis=-1, keepdims=True)
            powers = jnp.exp(scores - top)
            norm = jnp.sum(powers, axis=-1, keepdims=True)
            probs = (powers / norm).astype(BF16)
            total = total + dot(probs, jnp.where(own, values, 0.0).astype(BF16))
            lse[...] = jnp.where(lane((slot, LANES)) == head, top + jnp.log(norm), lse[...])
        mixed[:, pl.ds(start, LANES)] = total.astype(BF16)
        return 0

    lax.fori_loop(0, H // 2, pair, 0)


def project(x, core, small, outs, mixed, routes, dest_row, resid, moe_in, weights, *packed):
    slot = x.shape[0]
    gains = gain_rows(small)
    for other in range(2):
        span = columns(core, other)
        resid[:, span] = x[:, span].astype(F32) + dot(mixed[...], outs[other][...])
    after = resid[...]
    normed = (after * inverse_rms(after) * gains[1:2]).astype(BF16)
    moe_in[...] = normed
    logits = dot(normed, small)
    chosen = [
        jnp.sum(jnp.where(lane(logits.shape) == routes[:, k : k + 1], logits, 0.0), axis=1, keepdims=True)
        for k in range(2)
    ]
    first = jax.nn.sigmoid(chosen[0] - chosen[1])
    second = jax.nn.sigmoid(chosen[1] - chosen[0])
    places = lane((slot, LANES))
    weights[...] = jnp.where(places == 0, first, jnp.where(places == 1, second, 0.0))
    for index, piece in enumerate(packed):
        rows = sublane((piece.shape[0], slot)) + index * piece.shape[0]
        spread = one_hot((rows == dest_row[0:1, :]) | (rows == dest_row[1:2, :]))
        piece[...] = dot(spread, normed).astype(BF16)


def fetch_rows(dest_col, returned, indices):
    slot = dest_col.shape[0]
    total = jnp.zeros((slot, D), F32)
    for number, piece in enumerate(returned):
        places = lane((slot, piece.shape[0])) + number * piece.shape[0]
        mask = places == dest_col[:, indices[0] : indices[0] + 1]
        for index in indices[1:]:
            mask = mask | (places == dest_col[:, index : index + 1])
        total = total + dot(one_hot(mask), piece[...])
    return total


def combine(resid, weights, dest_col, returned):
    back = [fetch_rows(dest_col, returned, [k]) for k in range(2)]
    out = resid[...] + column(weights[...], 0) * back[0] + column(weights[...], 1) * back[1]
    return out.astype(BF16), back


def dispatch_back(grad, weights, back, dest_row, packed, grad_weights):
    slot = grad.shape[0]
    places = lane((slot, LANES))
    sums = [jnp.sum(grad * back[k], axis=-1, keepdims=True) for k in range(2)]
    grad_weights[...] = jnp.where(places == 0, sums[0], jnp.where(places == 1, sums[1], 0.0))
    scaled = [(column(weights[...], k) * grad).astype(BF16) for k in range(2)]
    for index, piece in enumerate(packed):
        rows = sublane((piece.shape[0], slot)) + index * piece.shape[0]
        total = dot(one_hot(rows == dest_row[0:1, :]), scaled[0]) + dot(one_hot(rows == dest_row[1:2, :]), scaled[1])
        piece[...] = total.astype(BF16)


def mix_kernel(core, x, own_a, other_a, onehot, seg_col, seg_row, qkv, mixed, lse, small, *scratch):
    small[...] = own_a[:, COL_SMALL:]
    mix(x, core, (own_a, None, other_a), onehot, seg_col, seg_row, qkv, mixed, lse, *scratch)


def project_kernel(core, x, small, own_b, other_b, *refs):
    project(x, core, small[...], (own_b, other_b), *refs)


def middle_kernel(count, core, resid, weights, dest_col, *refs):
    returned, refs = refs[:count], refs[count:]
    dense, (onehot, seg_col, seg_row, routes, dest_row), refs = dense_views(refs[:2]), refs[2:7], refs[7:]
    (out, back0, back1, qkv, mixed, lse), projected, scratch = refs[:6], refs[6:-2], refs[-2:]
    after, back = combine(resid, weights, dest_col, returned)
    out[...] = after
    back0[...] = back[0].astype(BF16)
    back1[...] = back[1].astype(BF16)
    mix(out, core, dense, onehot, seg_col, seg_row, qkv, mixed, lse, *scratch)
    project(out, core, dense[0][:, COL_SMALL:], (dense[1], dense[3]), mixed, routes, dest_row, *projected)


def turn_kernel(count, resid, weights, dest_col, dest_row, cotangent, *refs):
    returned, out, packed, grad_weights = refs[:count], refs[count], refs[count + 1 : -1], refs[-1]
    after, back = combine(resid, weights, dest_col, returned)
    out[...] = after
    dispatch_back(cotangent[...].astype(F32), weights, back, dest_row, packed, grad_weights)


def attend_back(core, x_ref, dense, onehot, seg_col, seg_row, routes, dest_col, grad_out, resid, moe_in, weights, grad_weights,
                qkv, mixed, lse, returned, grad_own, grad_other, grad_in, table, fence, grad_mixed, grad_qkv, sums, flip, grad_attn):
    slot = resid.shape[0]
    outs = (grad_own, grad_other)
    small = dense[0][:, COL_SMALL:]
    gains = gain_rows(small)
    table[...] = dot_tn(small, onehot[...])
    set_masks(seg_col, seg_row, fence)
    grad_moe = fetch_rows(dest_col, returned, [0, 1])
    first, second = column(weights[...], 0), column(weights[...], 1)
    diff = column(grad_weights[...], 0) * first * (1.0 - first) - column(grad_weights[...], 1) * second * (1.0 - second)
    spots = lane((slot, LANES))
    grad_logits = jnp.where(
        spots == routes[:, 0:1], diff, jnp.where(spots == routes[:, 1:2], -diff, 0.0)
    ).astype(BF16)
    grad_moe = grad_moe + dot_nt(grad_logits, small)
    back, gain_moe = norm_back(resid[...], gains[1:2], grad_moe)
    grad_resid = grad_out[...].astype(F32) + back
    grad_attn[...] = grad_resid.astype(BF16)
    parts = [grad_attn[:, columns(core, other)] for other in range(2)]
    for other in range(2):
        outs[other][:, WIDE_A:] = dot_tn(mixed[...], parts[other]).astype(BF16)
    grad_mixed[...] = (
        dot_nt(parts[0], dense[1][...]) + dot_nt(parts[1], dense[3][...])
    ).astype(BF16)
    sums[...] = jnp.zeros_like(sums)
    flip[...] = one_hot(sublane((slot, slot)) + lane((slot, slot)) == slot - 1)

    def pair(index, _):
        start = pl.multiple_of(index * LANES, LANES)
        spans = [pl.ds(pl.multiple_of(part * D + start, LANES), LANES) for part in range(3)]
        query, keys, values = (qkv[:, span] for span in spans)
        grad = grad_mixed[:, pl.ds(start, LANES)]
        totals = [jnp.zeros((slot, LANES), F32) for _ in range(3)]
        for half in range(2):
            head = 2 * index + half
            own = lane((slot, LANES)) // DH == half
            query_own = jnp.where(own, query, 0.0).astype(BF16)
            grad_own = jnp.where(own, grad, 0.0).astype(BF16)
            scores = dot_nt(query_own, keys) * SCALE + bias_of(table, head, slot) + fence[...]
            probs = jnp.exp(scores - column(lse[...], head))
            grad_probs = dot_nt(grad_own, values)
            delta = jnp.sum(grad_probs * probs, axis=-1, keepdims=True)
            grad_scores = (probs * (grad_probs - delta)).astype(BF16)
            turned = pltpu.roll(dot(flip[...], grad_scores), 1, 1, stride=1, stride_axis=0)
            sums[pl.ds(LANE_BIAS + head, 1), :] = jnp.sum(turned, axis=0, keepdims=True)
            totals[0] = totals[0] + dot(grad_scores, jnp.where(own, keys, 0.0).astype(BF16))
            totals[1] = totals[1] + dot_tn(grad_scores, query_own)
            totals[2] = totals[2] + dot_tn(probs.astype(BF16), grad_own)
        for part, factor in enumerate((SCALE, SCALE, 1.0)):
            grad_qkv[:, spans[part]] = (totals[part] * factor).astype(BF16)
        return 0

    lax.fori_loop(0, H // 2, pair, 0)
    x = x_ref[...].astype(F32)
    attn_in = (x * inverse_rms(x) * gains[0:1]).astype(BF16)
    grad_attn_in = jnp.zeros((slot, D), F32)
    for other in range(2):
        grads = jnp.concatenate([grad_qkv[:, columns(core, other, part)] for part in range(3)], axis=1)
        outs[other][:, :COL_SMALL] = dot_tn(attn_in, grads).astype(BF16)
        grad_attn_in = grad_attn_in + dot_nt(grads, dense[2 * other][:, :COL_SMALL])
    back, gain_attn = norm_back(x, gains[0:1], grad_attn_in)
    total = (grad_resid + back).astype(BF16)
    grad_in[...] = total
    pick = one_hot(lane((8, LANES)) == sublane((8, LANES)) + LANE_GAIN)
    row = sublane((8, D))
    gain_grads = jnp.where(row == 0, gain_attn, jnp.where(row == 1, gain_moe, 0.0)).astype(BF16)
    grad_small = dot_tn(moe_in[...], grad_logits) + dot_tn(gain_grads, pick) + dot_nt(onehot[...], sums[...].astype(BF16))
    for out in outs:
        out[:, COL_SMALL:WIDE_A] = grad_small.astype(BF16)
    return total


def back_kernel(count, core, x, *refs):
    dense, refs = dense_views(refs[:4]), refs[4:]
    common, returned, rest = refs[:13], refs[13 : 13 + count], refs[13 + count :]
    attend_back(core, x, dense, *common, returned, *rest)


def back_turn_kernel(count, core, x, *refs):
    dense, refs = dense_views(refs[:2]), refs[2:]
    common, returned, refs = refs[:13], refs[13 : 13 + count], refs[13 + count :]
    own_weights, back0, back1, dest_row, grad_own, grad_other, grad_in = refs[:7]
    packed, grad_weights, scratch = refs[7 : 7 + count], refs[7 + count], refs[8 + count :]
    total = attend_back(core, x, dense, *common, returned, grad_own, grad_other, grad_in, *scratch)
    back = [back0[...].astype(F32), back1[...].astype(F32)]
    dispatch_back(total.astype(F32), own_weights, back, dest_row, packed, grad_weights)


def struct(shape, dtype):
    return jax.ShapeDtypeStruct(shape, dtype)


def cost(flops, moved, exps=0):
    return pl.CostEstimate(flops=int(flops), bytes_accessed=int(moved), transcendentals=int(exps))


def mix_shapes(slot):
    return [struct((slot, 3 * D), BF16), struct((slot, D), BF16), struct((slot, LANES), F32)]


def project_shapes(slot, packed):
    return [
        struct((slot, D), F32),
        struct((slot, D), BF16),
        struct((slot, LANES), F32),
    ] + packed


def attend_scratch(slot):
    return [pltpu.VMEM((LANES, slot), F32), pltpu.VMEM((slot, slot), F32)]


def back_scratch(slot):
    return attend_scratch(slot) + [
        pltpu.VMEM((slot, D), BF16),
        pltpu.VMEM((slot, 3 * D), BF16),
        pltpu.VMEM((LANES, slot), F32),
        pltpu.VMEM((slot, slot), BF16),
        pltpu.VMEM((slot, D), BF16),
    ]


def back_shapes(slot):
    return [struct((D, WIDE), BF16)] * 2 + [struct((slot, D), BF16)]


def kernel_call(body, inputs, out_shape, scratch, estimate, scalars=1):
    specs = [pl.BlockSpec(memory_space=pltpu.SMEM if k < scalars else pltpu.VMEM) for k in range(len(inputs))]
    return pl.pallas_call(
        body,
        in_specs=specs,
        out_shape=out_shape,
        scratch_shapes=scratch,
        cost_estimate=estimate,
    )(*inputs)


def stream(info, local, pieces, wide, tall, sems):
    local_gate_up, local_down = local
    count = wide.shape[-1]

    half = count // 2

    def copies(slot, gate, up, low, high):
        return [
            pltpu.make_async_copy(gate, wide.at[slot, 0], sems.at[slot, 0]),
            pltpu.make_async_copy(up, wide.at[slot, 1], sems.at[slot, 1]),
            pltpu.make_async_copy(low, tall.at[slot, pl.ds(0, half)], sems.at[slot, 2]),
            pltpu.make_async_copy(high, tall.at[slot, pl.ds(half, half)], sems.at[slot, 3]),
        ]

    def start(step):
        slot = lax.rem(step, 2)

        @pl.when(info[0] == 0)
        def _():
            first = pl.multiple_of(info[1 + step] * count, LANES)
            gate, up = (local_gate_up.at[0, 0, c, :, pl.ds(first, count)] for c in range(2))
            low, high = (local_down.at[0, 0, pl.ds(first + c * half, half), :] for c in range(2))
            for copy in copies(slot, gate, up, low, high):
                copy.start()

        for which in range(len(pieces)):

            @pl.when((info[0] != 0) & (step == which))
            def _():
                for copy in copies(slot, *pieces[which]):
                    copy.start()

    step = pl.program_id(0)

    @pl.when(step == 0)
    def _():
        start(step)

    @pl.when(step + 1 < len(pieces))
    def _():
        start(step + 1)

    slot = lax.rem(step, 2)
    for copy in copies(slot, wide.at[slot, 0], wide.at[slot, 1], *(tall.at[slot, pl.ds(c * half, half)] for c in range(2))):
        copy.wait()
    return slot


ROOT = math.sqrt(2.0 / math.pi)


ARRAYS = 4


def join(refs, scratch):
    at = 0
    for ref in refs:
        span = slice(at, at + ref.shape[-2])
        at += ref.shape[-2]
        scratch[..., span, :] = ref[...]


def accumulate(total, part, results):
    @pl.when(pl.program_id(0) == 0)
    def _():
        total[...] = part

    @pl.when(pl.program_id(0) > 0)
    def _():
        total[...] += part

    @pl.when(pl.program_id(0) == len(HOPS) - 1)
    def _():
        for index, result in enumerate(results):
            count = result.shape[0]
            result[...] = total[index * count : (index + 1) * count, :].astype(BF16)


def split_refs(refs, count):
    sources, refs = refs[: ARRAYS * len(HOPS)], refs[ARRAYS * len(HOPS) :]
    return [sources[ARRAYS * k : ARRAYS * k + ARRAYS] for k in range(len(HOPS))], refs[:count], refs[count:]


def expert_kernel(count, info, *refs):
    rows, local, refs = refs[:count], refs[count : count + 2], refs[count + 2 :]
    pieces, results, (kept, shared, joined, total, wide, tall, sems) = split_refs(refs, count)

    @pl.when(pl.program_id(0) == 0)
    def _():
        join(rows, joined)

    @pl.when(pl.program_id(0) < len(pieces))
    def _():
        slot = stream(info, local, pieces, wide, tall, sems)
        gate = dot(joined[...], wide[slot, 0])
        up = dot(joined[...], wide[slot, 1])
        kept[0] = gate.astype(BF16)
        kept[1] = up.astype(BF16)
        bent = jnp.tanh(ROOT * (gate + 0.044715 * (gate * gate * gate)))
        hidden = (0.5 * gate * (1.0 + bent) * up).astype(BF16)
        shared[0] = hidden
        accumulate(total, dot(hidden, tall[slot]), results)

    @pl.when(pl.program_id(0) == len(pieces))
    def _():
        shared[0] = joined[...]


def expert_back_kernel(count, info, *refs):
    grads, kept, local, refs = refs[:count], refs[count], refs[count + 1 : count + 3], refs[count + 3 :]
    pieces, results, (shared, joined, total, wide, tall, sems) = split_refs(refs, count)

    @pl.when(pl.program_id(0) == 0)
    def _():
        join(grads, joined)

    @pl.when(pl.program_id(0) < len(pieces))
    def _():
        slot = stream(info, local, pieces, wide, tall, sems)
        grad_hidden = dot_nt(joined[...], tall[slot])
        gate, up = kept[0].astype(F32), kept[1].astype(F32)
        square = gate * gate
        bent = jnp.tanh(ROOT * gate * (1.0 + 0.044715 * square))
        half = 0.5 * (1.0 + bent)
        slope = half + (0.5 * ROOT) * gate * (1.0 - bent * bent) * (1.0 + (3 * 0.044715) * square)
        grad_gate = (grad_hidden * up * slope).astype(BF16)
        grad_up = (grad_hidden * gate * half).astype(BF16)
        shared[0, 0] = grad_gate
        shared[0, 1] = grad_up
        accumulate(total, dot_nt(grad_gate, wide[slot, 0]) + dot_nt(grad_up, wide[slot, 1]), results)

    @pl.when(pl.program_id(0) == len(pieces))
    def _():
        for c in range(2):
            shared[0, c] = joined[...]


def whole(shape):
    return pl.BlockSpec(shape, lambda j: (0,) * len(shape))


def expert_call(info, rows, weights, kept=None):
    steps, count = len(HOPS), len(rows)
    held, units = rows[0].shape[0], weights[1].shape[2]
    quarter, joint = units // steps, held * count
    anywhere = pl.BlockSpec(memory_space=pl.ANY)
    pair = pl.BlockSpec((2, joint, quarter), lambda j: (0, 0, jnp.minimum(j, steps - 1)))
    out_specs = [whole((held, D))] * count
    out_shape = [struct((held, D), BF16)] * count
    extra = [] if kept is None else [kept]
    if kept is None:
        out_specs += [pair, pl.BlockSpec((1, joint, quarter), lambda j: (j, 0, 0))]
        out_shape += [struct((2, joint, units), BF16), struct((steps + 1, joint, quarter), BF16)]
    else:
        out_specs.append(pl.BlockSpec((1, 2, joint, quarter), lambda j: (j, 0, 0, 0)))
        out_shape.append(struct((steps + 1, 2, joint, quarter), BF16))
    outs = pl.pallas_call(
        functools.partial(expert_kernel if kept is None else expert_back_kernel, count),
        grid=(steps + 1,),
        in_specs=[pl.BlockSpec(memory_space=pltpu.SMEM)]
        + [whole((held, D))] * count
        + [pair] * len(extra)
        + [anywhere] * len(weights),
        out_specs=out_specs,
        out_shape=out_shape,
        scratch_shapes=[
            pltpu.VMEM((joint, D), BF16),
            pltpu.VMEM((joint, D), F32),
            pltpu.VMEM((2, 2, D, quarter), BF16),
            pltpu.VMEM((2, quarter, D), BF16),
            pltpu.SemaphoreType.DMA((2, ARRAYS)),
        ],
        cost_estimate=cost(
            6 * joint * D * units, 2 * (3 * D * units + 2 * joint * units + 2 * joint * D), joint * units
        ),
    )(info, *rows, *extra, *weights)
    return outs[:count], *outs[count:]


THIRDS = 3


def grads_kernel(groups, *refs):
    rows_in, grads_in, hidden, both = (refs[2 * k * groups : 2 * (k + 1) * groups] for k in range(4))
    outs, (rows, grads, joined, pair) = refs[8 * groups : -4], refs[-4:]

    @pl.when(pl.program_id(0) + pl.program_id(1) == 0)
    def _():
        join([ref.at[0] for ref in rows_in], rows)
        join([ref.at[0, 0] for ref in grads_in], grads)

    join([ref.at[0] for ref in hidden], joined)
    join([ref.at[0] for ref in both], pair)
    values = [dot_tn(rows[...], pair[0]), dot_tn(rows[...], pair[1]), dot_tn(joined[...], grads[...])]
    for place in range(2):

        @pl.when(pl.program_id(0) == place)
        def _():
            for index, value in enumerate(values):
                outs[3 * place + index][...] = value.astype(BF16)


def grads_call(hidden, other_hidden, both, other_both):
    groups, steps, joint, quarter = len(hidden), len(HOPS), hidden[0].shape[1], hidden[0].shape[2]
    part, total = quarter // THIRDS, 2 * len(hidden) * hidden[0].shape[1]

    def specs(block, place):
        return [pl.BlockSpec(block, functools.partial(place, other)) for other in (0, 2) for _ in range(groups)]

    in_specs = [
        *specs((1, joint, quarter), lambda other, j, i: (steps, 0, 0)),
        *specs((1, 1, joint, quarter), lambda other, j, i: (steps, 0, 0, 0)),
        *specs((1, joint, part), lambda other, j, i: (1 - j + other, 0, i)),
        *specs((1, 2, joint, part), lambda other, j, i: (1 - j + other, 0, 0, i)),
    ]

    def placed(place, i, j):
        return jnp.where(j == place, i, (THIRDS - 1) * (1 - place))

    out_specs = []
    for place in range(2):
        out_specs += [pl.BlockSpec((D, part), functools.partial(lambda place, j, i: (0, placed(place, i, j)), place))] * 2
        out_specs.append(pl.BlockSpec((part, D), functools.partial(lambda place, j, i: (placed(place, i, j), 0), place)))
    hiddens, boths = [*hidden, *other_hidden], [*both, *other_both]
    return pl.pallas_call(
        functools.partial(grads_kernel, groups),
        grid=(2, THIRDS),
        in_specs=in_specs,
        out_specs=out_specs,
        out_shape=[struct((D, quarter), BF16)] * 6,
        scratch_shapes=[
            pltpu.VMEM((total, D), BF16),
            pltpu.VMEM((total, D), BF16),
            pltpu.VMEM((total, part), BF16),
            pltpu.VMEM((2, total, part), BF16),
        ],
        cost_estimate=cost(12 * total * D * quarter, 4 * total * (D + 3 * quarter)),
    )(*hiddens, *boths, *hiddens, *boths)


def finish_kernel(first, sums0, sums1, came0, came1, *refs):
    out = refs[-1]

    @pl.when(first[0] == 1)
    def _():
        out[...] = sums0[...].astype(F32) + came0[...].astype(F32)

    @pl.when(first[0] == 0)
    def _():
        out[...] = sums1[...].astype(F32) + came1[...].astype(F32)


def finish(first, arrays, rows, start, base=None):
    count, width = arrays[0].shape
    block = D // 4
    specs = [pl.BlockSpec(memory_space=pltpu.SMEM)] + [pl.BlockSpec((block, width), lambda j: (j, 0))] * 4
    extra = [] if base is None else [base]
    return pl.pallas_call(
        finish_kernel,
        grid=(count // block,),
        in_specs=specs + [pl.BlockSpec(memory_space=pl.ANY)] * len(extra),
        out_specs=pl.BlockSpec((block, width), lambda j: (j + start // block, 0)),
        out_shape=struct((rows, width), F32),
        input_output_aliases={5: 0} if extra else {},
        cost_estimate=cost(4 * count * width, 12 * count * width),
    )(first, *arrays, *extra)


def spell_kernel(core, own, near, qkv, out, small):
    for other, piece in enumerate((own, near)):
        for part in range(3):
            qkv[:, columns(core, other, part)] = piece[:, part * HALF : (part + 1) * HALF].astype(F32)
        out[:, columns(core, other)] = piece[:, WIDE_A:].astype(F32)
    small[...] = own[:, COL_SMALL:WIDE_A].astype(F32)


def across(value, pairs=((0, 1), (1, 0))):
    return lax.ppermute(value, SECTION, pairs)


def hop(value, step):
    return lax.ppermute(value, REPLICA, [(r, r ^ step) for r in range(lax.axis_size(REPLICA))])


def swap(value, step):
    if step == 0:
        return value
    return lax.ppermute(value, EXPERT, [(e, e ^ step) for e in range(lax.axis_size(EXPERT))])


def exchange(value, experts):
    return lax.all_to_all(
        value.reshape(experts, -1, value.shape[-1]), EXPERT, split_axis=0, concat_axis=0, tiled=True
    ).reshape(value.shape)


def groups_of(experts):
    return GROUPS if experts == 4 else ((None,),)


def group_exchange(groups, experts):
    def travel(which, pieces):
        if groups[which] == (None,):
            return [exchange(pieces[0], experts)]
        return [swap(piece, step) for piece, step in zip(pieces, groups[which])]

    return travel


def spread(value, experts, me):
    if experts != 4:
        return exchange(jnp.concatenate([value] * experts), experts)
    came = {step: swap(value, step) for step in (3, 2, 1, 0)}
    for bit in (1, 2):
        flag = me & bit != 0
        came = {step: jnp.where(flag, came[step ^ bit], came[step]) for step in came}
    return jnp.concatenate([came[step] for step in range(4)])


def gathered_sum(parts, experts):
    return jnp.sum(exchange(parts, experts).reshape(experts, -1, WIDE).astype(F32), axis=0)


def ordered(top, mine, theirs):
    return jnp.where(top, theirs, mine), jnp.where(top, mine, theirs)


def joined_cores(own, other):
    return (own.astype(F32) + hop(other, 1).astype(F32)).astype(BF16)


def joined_chips(pair, top):
    mine, theirs = ordered(top, *pair)
    return (mine.astype(F32) + hop(theirs, 2).astype(F32)).astype(BF16)


def anchor_kernel(value, out):
    for index in range(value.shape[0]):
        out[index] = value[index]


def anchor(value):
    scalars = pl.BlockSpec(memory_space=pltpu.SMEM)
    return pl.pallas_call(
        anchor_kernel, in_specs=[scalars], out_specs=scalars, out_shape=struct(value.shape, value.dtype)
    )(value)


def destinations(routes, experts, capacity, me):
    slot = routes.shape[1]
    hits = (routes[..., None] == jnp.arange(experts, dtype=jnp.int32)).astype(F32)
    places = np.arange(slot)
    before = jnp.asarray(places[:, None] > places[None, :], BF16)
    counts = jnp.einsum(
        "ts,lse->lte", before, jnp.sum(hits, axis=2).astype(BF16), preferred_element_type=F32
    )
    place = jnp.sum(hits * counts[:, :, None, :], axis=-1).astype(jnp.int32)
    if experts == 4:
        routes = routes ^ me
        routes = routes ^ (routes >> 1)
    return routes * capacity + place


def step(x_in, cotangent, segments, routes, gains, w_qkv, w_out, router, rel_bias, w_gate_up, w_down):
    section = lax.axis_index(SECTION)
    replica = lax.axis_index(REPLICA)
    me = lax.axis_index(EXPERT)
    first = section == 0
    core = replica % 2
    top = replica // 2 == 1
    experts = router.shape[2]
    held = w_qkv.shape[1]
    slot = x_in.shape[1]
    capacity = 5 * slot // (2 * experts)
    groups = groups_of(experts)
    count = sum(len(group) for group in groups)
    packed_shapes = [struct((experts * capacity // count, D), BF16)] * count
    units = w_down.shape[2]
    quarter = units // len(HOPS)
    core_info = anchor(core.astype(jnp.int32)[None])
    first_info = anchor(anchor(first.astype(jnp.int32)[None]))

    def mine(value):
        return lax.dynamic_index_in_dim(value, section, 0, keepdims=False)

    def by_layer(value, swapped):
        return jnp.where(first, value, swapped), jnp.where(first, swapped, value)

    def half_of(value, part=0):
        return lax.dynamic_slice_in_dim(value, part * D + core * HALF, HALF, 1)

    def placed(value, start):
        return jnp.pad(value, ((0, held - value.shape[0]), (start, LANES - start - value.shape[1])))

    def grouped(values):
        values = list(values)
        return [[values.pop(0) for _ in group] for group in groups]

    routed = jnp.stack(
        by_layer(mine(routes[0]), across(lax.dynamic_index_in_dim(routes[0], 1 - section, 0, keepdims=False)))
    )
    small = placed(router[0], 0) + placed(gains[0].T, LANE_GAIN) + placed(rel_bias[0], LANE_BIAS)
    dense_a = jnp.concatenate([half_of(w_qkv[0], part) for part in range(3)] + [small], axis=1)
    dense_b = half_of(w_out[0])
    halves_a, halves_b = by_layer(dense_a, across(dense_a)), by_layer(dense_b, across(dense_b))

    start = replica * quarter
    near = [
        lax.dynamic_slice(w_gate_up, (0, 0, c, 0, start), (1, 1, 1, D, quarter)).reshape(D, quarter) for c in range(2)
    ] + [lax.dynamic_slice_in_dim(w_down[0, 0], start + c * (quarter // 2), quarter // 2, 0) for c in range(2)]
    near = [across(piece) for piece in near]
    far = [hop(piece, 2) for piece in near]
    weights = [w_gate_up, w_down, *near, *far]
    weights += [hop(piece, 1) for piece in near + far]
    owners = [replica ^ h for h in HOPS]
    infos = [
        anchor(jnp.stack([jnp.where(first, layer, 1 - layer).astype(jnp.int32)] + owners).astype(jnp.int32))
        for layer in range(2)
    ]

    dest = destinations(routed, experts, capacity, me)
    dest_rows = jnp.swapaxes(dest, 1, 2)
    onehot = jnp.asarray(bucket_rows(slot, experts), BF16)
    segment = mine(segments[:, 0])
    seg_col, seg_row = segment[:, None], segment[None, :]
    x = mine(x_in)
    cot = mine(cotangent)

    own_a0 = spread(halves_a[0], experts, me)
    own_b0 = spread(halves_b[0], experts, me)
    dense0 = (own_a0, own_b0, hop(own_a0, 1), hop(own_b0, 1))
    block = held // 4
    part = jnp.concatenate([halves_a[1], halves_b[1]], axis=1)
    part = lax.dynamic_slice_in_dim(part, (replica // 2 * 2 + section) * block, block, 0)
    part = spread(part, experts, me)

    def doubled(flag, value, came):
        pair = ordered(flag, value.reshape(experts, -1, WIDE), came.reshape(experts, -1, WIDE))
        return jnp.concatenate(pair, axis=1).reshape(-1, WIDE)

    part = doubled(jnp.logical_not(first), part, across(part))
    own1 = doubled(top, part, hop(part, 2))
    dense1 = (own1, hop(own1, 1))

    attend_cost = cost(4 * 10**9, 10**7, 10**6)
    back_cost = cost(10**10, 2 * 10**7, 10**6)

    def experts_forward(layer, packed):
        send = group_exchange(groups, experts)
        give = group_exchange(groups, experts)
        kept, hidden, came, returned = [], [], [], []
        for g, pieces in enumerate(grouped(packed)):
            results, both, shared = expert_call(infos[layer], send(g, pieces), weights)
            kept.append(both)
            hidden.append(shared)
            returned += give(g, results)
            came.append(hop(shared, 1))
        return (kept, hidden, came), returned

    common0 = (onehot, seg_col, seg_row, routed[0])
    common1 = (onehot, seg_col, seg_row, routed[1])
    qkv0, mixed0, lse0, small0 = kernel_call(
        mix_kernel, (core_info, x, own_a0, dense0[2], onehot, seg_col, seg_row),
        mix_shapes(slot) + [struct((D, LANES), BF16)], attend_scratch(slot), attend_cost,
    )
    resid0, moe_in0, weights0, *packed0 = kernel_call(
        project_kernel, (core_info, x, small0, own_b0, dense0[3], mixed0, routed[0], dest_rows[0]),
        project_shapes(slot, packed_shapes), [], cost(10**9, 4 * 10**6),
    )
    saved0, returned0 = experts_forward(0, packed0)
    out0, back00, back01, qkv1, mixed1, lse1, resid1, moe_in1, weights1, *packed1 = kernel_call(
        functools.partial(middle_kernel, count),
        (core_info, resid0, weights0, dest[0], *returned0, *dense1, *common1, dest_rows[1]),
        [struct((slot, D), BF16)] * 3 + mix_shapes(slot) + project_shapes(slot, packed_shapes),
        attend_scratch(slot), attend_cost,
    )
    saved1, returned1 = experts_forward(1, packed1)
    out1, *packed1, grad_weights1 = kernel_call(
        functools.partial(turn_kernel, count), (resid1, weights1, dest[1], dest_rows[1], cot, *returned1),
        [struct((slot, D), BF16)] + packed_shapes + [struct((slot, LANES), F32)], [],
        cost(10**9, 4 * 10**6), scalars=0,
    )

    def experts_backward(layer, saved, packed):
        kept, hidden, came = saved
        send = group_exchange(groups, experts)
        give = group_exchange(groups, experts)
        both, came_back, returned = [], [], []
        for g, pieces in enumerate(grouped(packed)):
            results, shared = expert_call(infos[layer], send(g, pieces), weights, kept[g])
            both.append(shared)
            returned += give(g, results)
            came_back.append(hop(shared, 1))
        grads = grads_call(hidden, came, both, came_back)
        summed = []
        for k in range(3):
            came_far = hop(grads[k], 2)
            for span in ((slice(0, D // 2), slice(D // 2, D)) if k == 1 else (slice(None),)):
                summed.append((grads[3 + k][span].astype(F32) + came_far[span].astype(F32)).astype(BF16))
        pairs = ((0, 1),) if layer else ((1, 0),)
        return returned, [(value, across(value, pairs)) for value in summed]

    grad_returned1, expert_sums1 = experts_backward(1, saved1, packed1)
    grad_own1, grad_other1, grad_in1, *grad_packed0, grad_weights0 = kernel_call(
        functools.partial(back_turn_kernel, count),
        (core_info, out0, *dense1, *common1, dest[1], cot, resid1, moe_in1, weights1, grad_weights1, qkv1, mixed1, lse1,
         *grad_returned1, weights0, back00, back01, dest_rows[0]),
        back_shapes(slot) + packed_shapes + [struct((slot, LANES), F32)], back_scratch(slot), back_cost,
    )
    grad_returned0, expert_sums0 = experts_backward(0, saved0, grad_packed0)
    grad_own0, grad_other0, grad_in0 = kernel_call(
        functools.partial(back_kernel, count),
        (core_info, x, *dense0, *common0, dest[0], grad_in1, resid0, moe_in0, weights0, grad_weights0, qkv0, mixed0, lse0,
         *grad_returned0),
        back_shapes(slot), back_scratch(slot), back_cost,
    )
    ended = [(sum0, sum1, came0, came1) for (sum0, came0), (sum1, came1) in zip(expert_sums0, expert_sums1)]
    grad_down = finish(first_info, ended[3], D, 0)[None, None]
    grad_gate_up = finish(first_info, ended[0], 2 * D, 0)
    grad_gate_up = finish(first_info, ended[1], 2 * D, D, grad_gate_up)
    grad_gate_up = finish(first_info, ended[2], 2 * D, D + D // 2, grad_gate_up).reshape(1, 1, 2, D, quarter)

    part = joined_cores(grad_own1, grad_other1).reshape(experts, 2, held // 2, WIDE)
    part = joined_chips((part[:, 0], part[:, 1]), top).reshape(-1, WIDE)
    reduced1 = gathered_sum(part, experts)
    part = gathered_sum(joined_cores(grad_own0, grad_other0), experts).astype(BF16)
    reduced0 = joined_chips((part[: held // 2], part[held // 2 :]), top).astype(F32)
    total = jnp.where(first, reduced0, reduced1)
    for value, pair in ((reduced1, (0, 1)), (reduced0, (1, 0))):
        total = total + across(value.astype(BF16), (pair,)).astype(F32)
    total = total.astype(BF16)
    total = jnp.concatenate(ordered(top, total, hop(total, 2)))
    grad_qkv, grad_out, small = kernel_call(
        spell_kernel, (core_info, total, hop(total, 1)),
        [struct((held, 3 * D), F32), struct((held, D), F32), struct((held, LANES), F32)], [], cost(held * D, held * D * 16),
    )

    def both_micro(value0, value1):
        own, swapped = jnp.where(first, value0, value1), across(jnp.where(first, value1, value0))
        return jnp.stack([jnp.where(first, own, swapped), jnp.where(first, swapped, own)])[None]

    return (
        both_micro(out0, out1),
        both_micro(grad_in0, grad_in1),
        small[:, LANE_GAIN : LANE_GAIN + 2].T[None],
        grad_qkv[None],
        grad_out[None],
        small[:, :experts][None],
        small[: rel_bias.shape[1], LANE_BIAS : LANE_BIAS + H][None],
        grad_gate_up,
        grad_down,
    )


def solution(mesh):
    tokens = P(None, (EXPERT, REPLICA), None)
    layered = P(SECTION, None, (EXPERT, REPLICA), None)
    dense = P(SECTION, EXPERT, None)
    gains = P(SECTION, None, EXPERT)
    in_specs = (tokens,) * 3 + (layered, gains) + (dense,) * 4
    in_specs += (P(SECTION, EXPERT, None, None, None), P(SECTION, EXPERT, None, None))
    out_specs = (layered, layered, gains) + (dense,) * 4
    out_specs += (P(SECTION, EXPERT, None, None, REPLICA), P(SECTION, EXPERT, REPLICA, None))
    return jax.shard_map(step, mesh=mesh, in_specs=in_specs, out_specs=out_specs, check_vma=False)
```

```python
import functools
import math

import jax
import jax.numpy as jnp
import numpy as np
from jax import lax
from jax.experimental import pallas as pl
from jax.experimental.pallas import tpu as pltpu
from jax.sharding import PartitionSpec as P


D = 768
H = 12
DH = 64
NB = 32
MAXDIST = 128
EPS = 1e-06
SCALE = 0.125
MASKED = -1000000000.0

LANES = 128
HALF = D // 2
COL_SMALL = 3 * HALF
WIDE_A = COL_SMALL + LANES
WIDE_B = HALF
WIDE = WIDE_A + WIDE_B
LANE_GAIN = 32
LANE_BIAS = 64
HOPS = (0, 2, 1, 3)
GROUPS = ((0, 1), (3, 2))
SECTION, EXPERT, REPLICA = "section", "expert", "replica"


F32 = jnp.float32
BF16 = jnp.bfloat16


def dot(a, b):
    return lax.dot_general(a, b, (((1,), (0,)), ((), ())), preferred_element_type=F32)


def dot_nt(a, b):
    return lax.dot_general(a, b, (((1,), (1,)), ((), ())), preferred_element_type=F32)


def dot_tn(a, b):
    return lax.dot_general(a, b, (((0,), (0,)), ((), ())), preferred_element_type=F32)


def bucket_ids(size, buckets, reach):
    distance = np.arange(size)
    exact = buckets // 2
    scaled = np.log(np.maximum(distance, 1) / exact) / math.log(reach / exact) * (buckets - exact)
    spread = exact + np.floor(np.maximum(scaled, 0.0)).astype(np.int64)
    return np.where(distance < exact, distance, np.minimum(spread, buckets - 1)).astype(np.int32)


def bucket_rows(slot, experts):
    ids = bucket_ids(slot, NB, MAXDIST)
    rows, held = D // experts, NB // experts
    table = np.zeros((D, slot), np.float32)
    for column in range(slot):
        bucket = ids[(slot - column) % slot]
        table[bucket // held * rows + bucket % held, column] = 1.0
    return table


def lane(shape):
    return lax.broadcasted_iota(jnp.int32, shape, 1)


def sublane(shape):
    return lax.broadcasted_iota(jnp.int32, shape, 0)


def one_hot(mask):
    return jnp.where(mask, 1.0, 0.0).astype(BF16)


def gain_rows(small):
    pick = one_hot(lane((8, LANES)) == sublane((8, LANES)) + LANE_GAIN)
    return dot_nt(pick, small)


def inverse_rms(x):
    return lax.rsqrt(jnp.mean(x * x, axis=-1, keepdims=True) + EPS)


def norm_back(x, gain, grad):
    inverse = inverse_rms(x)
    scaled = grad * gain
    along = jnp.mean(scaled * x, axis=-1, keepdims=True)
    return (
        inverse * scaled - x * (inverse * inverse * inverse * along),
        jnp.sum(grad * x * inverse, axis=0, keepdims=True),
    )


def column(values, index):
    return jnp.sum(jnp.where(lane(values.shape) == index, values, 0.0), axis=1, keepdims=True)


def set_masks(seg_col, seg_row, fence):
    slot = fence.shape[0]
    allowed = (sublane((slot, slot)) >= lane((slot, slot))) & (seg_col[...] == seg_row[...])
    fence[...] = jnp.where(allowed, 0.0, MASKED)


def bias_of(table, head, slot):
    row = table[pl.ds(LANE_BIAS + head, 1), :]
    return pltpu.roll(jnp.broadcast_to(row, (slot, slot)), 0, 1, stride=1, stride_axis=0)


def columns(core, other, part=0):
    half = 1 - core[0] if other else core[0]
    return pl.ds(pl.multiple_of(part * D + half * HALF, LANES), HALF)


def dense_views(refs):
    if len(refs) == 4:
        return refs
    return [ref.at[:, span] for ref in refs for span in (pl.ds(0, WIDE_A), pl.ds(WIDE_A, WIDE_B))]


def mix(x, core, dense, onehot, seg_col, seg_row, qkv, mixed, lse, table, fence):
    slot = x.shape[0]
    small = dense[0][:, COL_SMALL:]
    gains = gain_rows(small)
    table[...] = dot_tn(small, onehot[...])
    set_masks(seg_col, seg_row, fence)
    wide = x[...].astype(F32)
    attn_in = (wide * inverse_rms(wide) * gains[0:1]).astype(BF16)
    for other in range(2):
        value = dot(attn_in, dense[2 * other][...]).astype(BF16)
        for part in range(3):
            qkv[:, columns(core, other, part)] = value[:, part * HALF : (part + 1) * HALF]
    lse[...] = jnp.zeros_like(lse)

    def pair(index, _):
        start = pl.multiple_of(index * LANES, LANES)
        query = qkv[:, pl.ds(start, LANES)]
        keys = qkv[:, pl.ds(pl.multiple_of(D + start, LANES), LANES)]
        values = qkv[:, pl.ds(pl.multiple_of(2 * D + start, LANES), LANES)]
        total = jnp.zeros((slot, LANES), F32)
        for half in range(2):
            head = 2 * index + half
            own = lane((slot, LANES)) // DH == half
            scores = dot_nt(jnp.where(own, query, 0.0).astype(BF16), keys) * SCALE
            scores = scores + bias_of(table, head, slot) + fence[...]
            top = jnp.max(scores, axis=-1, keepdims=True)
            powers = jnp.exp(scores - top)
            norm = jnp.sum(powers, axis=-1, keepdims=True)
            probs = (powers / norm).astype(BF16)
            total = total + dot(probs, jnp.where(own, values, 0.0).astype(BF16))
            lse[...] = jnp.where(lane((slot, LANES)) == head, top + jnp.log(norm), lse[...])
        mixed[:, pl.ds(start, LANES)] = total.astype(BF16)
        return 0

    lax.fori_loop(0, H // 2, pair, 0, unroll=2)


def project(x, core, small, outs, mixed, routes, dest_row, resid, moe_in, weights, *packed):
    slot = x.shape[0]
    gains = gain_rows(small)
    for other in range(2):
        span = columns(core, other)
        resid[:, span] = x[:, span].astype(F32) + dot(mixed[...], outs[other][...])
    after = resid[...]
    normed = (after * inverse_rms(after) * gains[1:2]).astype(BF16)
    moe_in[...] = normed
    logits = dot(normed, small)
    chosen = [
        jnp.sum(jnp.where(lane(logits.shape) == routes[:, k : k + 1], logits, 0.0), axis=1, keepdims=True)
        for k in range(2)
    ]
    first = jax.nn.sigmoid(chosen[0] - chosen[1])
    second = jax.nn.sigmoid(chosen[1] - chosen[0])
    places = lane((slot, LANES))
    weights[...] = jnp.where(places == 0, first, jnp.where(places == 1, second, 0.0))
    for index, piece in enumerate(packed):
        rows = sublane((piece.shape[0], slot)) + index * piece.shape[0]
        spread = one_hot((rows == dest_row[0:1, :]) | (rows == dest_row[1:2, :]))
        piece[...] = dot(spread, normed).astype(BF16)


def fetch_rows(dest_col, returned, indices):
    slot = dest_col.shape[0]
    total = jnp.zeros((slot, D), F32)
    for number, piece in enumerate(returned):
        places = lane((slot, piece.shape[0])) + number * piece.shape[0]
        mask = places == dest_col[:, indices[0] : indices[0] + 1]
        for index in indices[1:]:
            mask = mask | (places == dest_col[:, index : index + 1])
        total = total + dot(one_hot(mask), piece[...])
    return total


def combine(resid, weights, dest_col, returned):
    back = [fetch_rows(dest_col, returned, [k]) for k in range(2)]
    out = resid[...] + column(weights[...], 0) * back[0] + column(weights[...], 1) * back[1]
    return out.astype(BF16), back


def dispatch_back(grad, weights, back, dest_row, packed, grad_weights):
    slot = grad.shape[0]
    places = lane((slot, LANES))
    sums = [jnp.sum(grad * back[k], axis=-1, keepdims=True) for k in range(2)]
    grad_weights[...] = jnp.where(places == 0, sums[0], jnp.where(places == 1, sums[1], 0.0))
    scaled = [(column(weights[...], k) * grad).astype(BF16) for k in range(2)]
    for index, piece in enumerate(packed):
        rows = sublane((piece.shape[0], slot)) + index * piece.shape[0]
        total = dot(one_hot(rows == dest_row[0:1, :]), scaled[0]) + dot(one_hot(rows == dest_row[1:2, :]), scaled[1])
        piece[...] = total.astype(BF16)


def mix_kernel(core, x, own_a, other_a, onehot, seg_col, seg_row, qkv, mixed, lse, small, *scratch):
    small[...] = own_a[:, COL_SMALL:]
    mix(x, core, (own_a, None, other_a), onehot, seg_col, seg_row, qkv, mixed, lse, *scratch)


def project_kernel(core, x, small, own_b, other_b, *refs):
    project(x, core, small[...], (own_b, other_b), *refs)


def middle_kernel(count, core, resid, weights, dest_col, *refs):
    returned, refs = refs[:count], refs[count:]
    dense, (onehot, seg_col, seg_row, routes, dest_row), refs = refs[:2], refs[2:7], refs[7:]
    (out, back0, back1, qkv, mixed, lse), projected, scratch, held = refs[:6], refs[6:-5], refs[-5:-3], refs[-3:]
    copies = [pltpu.make_async_copy(dense[k], held[k], held[2].at[k]) for k in range(2)]
    for copy in copies:
        copy.start()
    after, back = combine(resid, weights, dest_col, returned)
    out[...] = after
    back0[...] = back[0].astype(BF16)
    back1[...] = back[1].astype(BF16)
    for copy in copies:
        copy.wait()
    dense = dense_views(held[:2])
    mix(out, core, dense, onehot, seg_col, seg_row, qkv, mixed, lse, *scratch)
    project(out, core, dense[0][:, COL_SMALL:], (dense[1], dense[3]), mixed, routes, dest_row, *projected)


def turn_kernel(count, resid, weights, dest_col, dest_row, cotangent, *refs):
    returned, out, packed, grad_weights = refs[:count], refs[count], refs[count + 1 : -1], refs[-1]
    after, back = combine(resid, weights, dest_col, returned)
    out[...] = after
    dispatch_back(cotangent[...].astype(F32), weights, back, dest_row, packed, grad_weights)


def attend_back(core, x_ref, dense, onehot, seg_col, seg_row, routes, dest_col, grad_out, resid, moe_in, weights, grad_weights,
                qkv, mixed, lse, returned, grad_own, grad_other, grad_in, table, fence, grad_mixed, grad_qkv, sums, flip, grad_attn,
                small_held, held_a, held_b, sems):
    slot = resid.shape[0]
    outs = (grad_own, grad_other)
    first = pltpu.make_async_copy(dense[0].at[:, pl.ds(COL_SMALL, LANES)], small_held, sems.at[0])
    second = [pltpu.make_async_copy(dense[2 * k + 1], held_b.at[k], sems.at[1 + k]) for k in range(2)]
    third = [pltpu.make_async_copy(dense[2 * k], held_a.at[k], sems.at[3 + k]) for k in range(2)]
    for copy in (first, *second, *third):
        copy.start()
    first.wait()
    small = small_held[...]
    gains = gain_rows(small)
    table[...] = dot_tn(small, onehot[...])
    set_masks(seg_col, seg_row, fence)
    grad_moe = fetch_rows(dest_col, returned, [0, 1])
    one, two = column(weights[...], 0), column(weights[...], 1)
    diff = column(grad_weights[...], 0) * one * (1.0 - one) - column(grad_weights[...], 1) * two * (1.0 - two)
    spots = lane((slot, LANES))
    grad_logits = jnp.where(
        spots == routes[:, 0:1], diff, jnp.where(spots == routes[:, 1:2], -diff, 0.0)
    ).astype(BF16)
    grad_moe = grad_moe + dot_nt(grad_logits, small)
    back, gain_moe = norm_back(resid[...], gains[1:2], grad_moe)
    grad_resid = grad_out[...].astype(F32) + back
    grad_attn[...] = grad_resid.astype(BF16)
    parts = [grad_attn[:, columns(core, other)] for other in range(2)]
    for other in range(2):
        outs[other][:, WIDE_A:] = dot_tn(mixed[...], parts[other]).astype(BF16)
    for copy in second:
        copy.wait()
    grad_mixed[...] = (dot_nt(parts[0], held_b[0]) + dot_nt(parts[1], held_b[1])).astype(BF16)
    sums[...] = jnp.zeros_like(sums)
    flip[...] = one_hot(sublane((slot, slot)) + lane((slot, slot)) == slot - 1)

    def pair(index, _):
        start = pl.multiple_of(index * LANES, LANES)
        spans = [pl.ds(pl.multiple_of(part * D + start, LANES), LANES) for part in range(3)]
        query, keys, values = (qkv[:, span] for span in spans)
        grad = grad_mixed[:, pl.ds(start, LANES)]
        totals = [jnp.zeros((slot, LANES), F32) for _ in range(3)]
        for half in range(2):
            head = 2 * index + half
            own = lane((slot, LANES)) // DH == half
            query_own = jnp.where(own, query, 0.0).astype(BF16)
            grad_own = jnp.where(own, grad, 0.0).astype(BF16)
            scores = dot_nt(query_own, keys) * SCALE + bias_of(table, head, slot) + fence[...]
            probs = jnp.exp(scores - column(lse[...], head))
            grad_probs = dot_nt(grad_own, values)
            delta = jnp.sum(grad_probs * probs, axis=-1, keepdims=True)
            grad_scores = (probs * (grad_probs - delta)).astype(BF16)
            turned = pltpu.roll(dot(flip[...], grad_scores), 1, 1, stride=1, stride_axis=0)
            sums[pl.ds(LANE_BIAS + head, 1), :] = jnp.sum(turned, axis=0, keepdims=True)
            totals[0] = totals[0] + dot(grad_scores, jnp.where(own, keys, 0.0).astype(BF16))
            totals[1] = totals[1] + dot_tn(grad_scores, query_own)
            totals[2] = totals[2] + dot_tn(probs.astype(BF16), grad_own)
        for part, factor in enumerate((SCALE, SCALE, 1.0)):
            grad_qkv[:, spans[part]] = (totals[part] * factor).astype(BF16)
        return 0

    lax.fori_loop(0, H // 2, pair, 0, unroll=2)
    x = x_ref[...].astype(F32)
    attn_in = (x * inverse_rms(x) * gains[0:1]).astype(BF16)
    grad_attn_in = jnp.zeros((slot, D), F32)
    for copy in third:
        copy.wait()
    for other in range(2):
        grads = jnp.concatenate([grad_qkv[:, columns(core, other, part)] for part in range(3)], axis=1)
        outs[other][:, :COL_SMALL] = dot_tn(attn_in, grads).astype(BF16)
        grad_attn_in = grad_attn_in + dot_nt(grads, held_a[other, :, :COL_SMALL])
    back, gain_attn = norm_back(x, gains[0:1], grad_attn_in)
    total = (grad_resid + back).astype(BF16)
    grad_in[...] = total
    pick = one_hot(lane((8, LANES)) == sublane((8, LANES)) + LANE_GAIN)
    row = sublane((8, D))
    gain_grads = jnp.where(row == 0, gain_attn, jnp.where(row == 1, gain_moe, 0.0)).astype(BF16)
    grad_small = dot_tn(moe_in[...], grad_logits) + dot_tn(gain_grads, pick) + dot_nt(onehot[...], sums[...].astype(BF16))
    for out in outs:
        out[:, COL_SMALL:WIDE_A] = grad_small.astype(BF16)
    return total


def back_kernel(count, core, x, *refs):
    dense, refs = dense_views(refs[:4]), refs[4:]
    common, returned, rest = refs[:13], refs[13 : 13 + count], refs[13 + count :]
    attend_back(core, x, dense, *common, returned, *rest)


def back_turn_kernel(count, core, x, *refs):
    dense, refs = dense_views(refs[:2]), refs[2:]
    common, returned, refs = refs[:13], refs[13 : 13 + count], refs[13 + count :]
    own_weights, back0, back1, dest_row, grad_own, grad_other, grad_in = refs[:7]
    packed, grad_weights, scratch = refs[7 : 7 + count], refs[7 + count], refs[8 + count :]
    total = attend_back(core, x, dense, *common, returned, grad_own, grad_other, grad_in, *scratch)
    back = [back0[...].astype(F32), back1[...].astype(F32)]
    dispatch_back(total.astype(F32), own_weights, back, dest_row, packed, grad_weights)


def struct(shape, dtype):
    return jax.ShapeDtypeStruct(shape, dtype)


def cost(flops, moved, exps=0):
    return pl.CostEstimate(flops=int(flops), bytes_accessed=int(moved), transcendentals=int(exps))


def mix_shapes(slot):
    return [struct((slot, 3 * D), BF16), struct((slot, D), BF16), struct((slot, LANES), F32)]


def project_shapes(slot, packed):
    return [
        struct((slot, D), F32),
        struct((slot, D), BF16),
        struct((slot, LANES), F32),
    ] + packed


def attend_scratch(slot):
    return [pltpu.VMEM((LANES, slot), F32), pltpu.VMEM((slot, slot), F32)]


def back_scratch(slot):
    return attend_scratch(slot) + [
        pltpu.VMEM((slot, D), BF16),
        pltpu.VMEM((slot, 3 * D), BF16),
        pltpu.VMEM((LANES, slot), F32),
        pltpu.VMEM((slot, slot), BF16),
        pltpu.VMEM((slot, D), BF16),
        pltpu.VMEM((D, LANES), BF16),
        pltpu.VMEM((2, D, WIDE_A), BF16),
        pltpu.VMEM((2, D, WIDE_B), BF16),
        pltpu.SemaphoreType.DMA((5,)),
    ]


def back_shapes(slot):
    return [struct((D, WIDE), BF16)] * 2 + [struct((slot, D), BF16)]


def kernel_call(body, inputs, out_shape, scratch, estimate, scalars=1, lazy=()):
    specs = [
        pl.BlockSpec(memory_space=pltpu.SMEM if k < scalars else pl.ANY if k in lazy else pltpu.VMEM)
        for k in range(len(inputs))
    ]
    return pl.pallas_call(
        body,
        in_specs=specs,
        out_shape=out_shape,
        scratch_shapes=scratch,
        cost_estimate=estimate,
    )(*inputs)


def stream(info, local, pieces, wide, tall, sems):
    local_gate_up, local_down = local
    count = wide.shape[-1]

    half = count // 2

    def copies(slot, gate, up, low, high):
        return [
            pltpu.make_async_copy(gate, wide.at[slot, 0], sems.at[slot, 0]),
            pltpu.make_async_copy(up, wide.at[slot, 1], sems.at[slot, 1]),
            pltpu.make_async_copy(low, tall.at[slot, pl.ds(0, half)], sems.at[slot, 2]),
            pltpu.make_async_copy(high, tall.at[slot, pl.ds(half, half)], sems.at[slot, 3]),
        ]

    def start(step):
        slot = lax.rem(step, 2)

        @pl.when(info[0] == 0)
        def _():
            first = pl.multiple_of(info[1 + step] * count, LANES)
            gate, up = (local_gate_up.at[0, 0, c, :, pl.ds(first, count)] for c in range(2))
            low, high = (local_down.at[0, 0, pl.ds(first + c * half, half), :] for c in range(2))
            for copy in copies(slot, gate, up, low, high):
                copy.start()

        for which in range(len(pieces)):

            @pl.when((info[0] != 0) & (step == which))
            def _():
                for copy in copies(slot, *pieces[which]):
                    copy.start()

    step = pl.program_id(0)

    @pl.when(step == 0)
    def _():
        start(step)

    @pl.when(step + 1 < len(pieces))
    def _():
        start(step + 1)

    slot = lax.rem(step, 2)
    for copy in copies(slot, wide.at[slot, 0], wide.at[slot, 1], *(tall.at[slot, pl.ds(c * half, half)] for c in range(2))):
        copy.wait()
    return slot


ROOT = math.sqrt(2.0 / math.pi)


ARRAYS = 4


def join(refs, scratch):
    at = 0
    for ref in refs:
        span = slice(at, at + ref.shape[-2])
        at += ref.shape[-2]
        scratch[..., span, :] = ref[...]


def accumulate(total, part, results):
    @pl.when(pl.program_id(0) == 0)
    def _():
        total[...] = part

    @pl.when(pl.program_id(0) > 0)
    def _():
        total[...] += part

    @pl.when(pl.program_id(0) == len(HOPS) - 1)
    def _():
        for index, result in enumerate(results):
            count = result.shape[0]
            result[...] = total[index * count : (index + 1) * count, :].astype(BF16)


def split_refs(refs, count):
    sources, refs = refs[: ARRAYS * len(HOPS)], refs[ARRAYS * len(HOPS) :]
    return [sources[ARRAYS * k : ARRAYS * k + ARRAYS] for k in range(len(HOPS))], refs[:count], refs[count:]


def expert_kernel(count, info, *refs):
    rows, local, refs = refs[:count], refs[count : count + 2], refs[count + 2 :]
    pieces, results, (kept, shared, joined, total, wide, tall, sems) = split_refs(refs, count)

    @pl.when(pl.program_id(0) == 0)
    def _():
        join(rows, joined)

    @pl.when(pl.program_id(0) < len(pieces))
    def _():
        slot = stream(info, local, pieces, wide, tall, sems)
        gate = dot(joined[...], wide[slot, 0])
        up = dot(joined[...], wide[slot, 1])
        kept[0] = gate.astype(BF16)
        kept[1] = up.astype(BF16)
        bent = jnp.tanh(ROOT * (gate + 0.044715 * (gate * gate * gate)))
        hidden = (0.5 * gate * (1.0 + bent) * up).astype(BF16)
        shared[0] = hidden
        accumulate(total, dot(hidden, tall[slot]), results)

    @pl.when(pl.program_id(0) == len(pieces))
    def _():
        shared[0] = joined[...]


def expert_back_kernel(count, info, *refs):
    grads, kept, local, refs = refs[:count], refs[count], refs[count + 1 : count + 3], refs[count + 3 :]
    pieces, results, (shared, joined, total, wide, tall, sems) = split_refs(refs, count)

    @pl.when(pl.program_id(0) == 0)
    def _():
        join(grads, joined)

    @pl.when(pl.program_id(0) < len(pieces))
    def _():
        slot = stream(info, local, pieces, wide, tall, sems)
        grad_hidden = dot_nt(joined[...], tall[slot])
        gate, up = kept[0].astype(F32), kept[1].astype(F32)
        square = gate * gate
        bent = jnp.tanh(ROOT * gate * (1.0 + 0.044715 * square))
        half = 0.5 * (1.0 + bent)
        slope = half + (0.5 * ROOT) * gate * (1.0 - bent * bent) * (1.0 + (3 * 0.044715) * square)
        grad_gate = (grad_hidden * up * slope).astype(BF16)
        grad_up = (grad_hidden * gate * half).astype(BF16)
        shared[0, 0] = grad_gate
        shared[0, 1] = grad_up
        accumulate(total, dot_nt(grad_gate, wide[slot, 0]) + dot_nt(grad_up, wide[slot, 1]), results)

    @pl.when(pl.program_id(0) == len(pieces))
    def _():
        for c in range(2):
            shared[0, c] = joined[...]


def whole(shape):
    return pl.BlockSpec(shape, lambda j: (0,) * len(shape))


def expert_call(info, rows, weights, kept=None):
    steps, count = len(HOPS), len(rows)
    held, units = rows[0].shape[0], weights[1].shape[2]
    quarter, joint = units // steps, held * count
    anywhere = pl.BlockSpec(memory_space=pl.ANY)
    pair = pl.BlockSpec((2, joint, quarter), lambda j: (0, 0, jnp.minimum(j, steps - 1)))
    out_specs = [whole((held, D))] * count
    out_shape = [struct((held, D), BF16)] * count
    extra = [] if kept is None else [kept]
    if kept is None:
        out_specs += [pair, pl.BlockSpec((1, joint, quarter), lambda j: (j, 0, 0))]
        out_shape += [struct((2, joint, units), BF16), struct((steps + 1, joint, quarter), BF16)]
    else:
        out_specs.append(pl.BlockSpec((1, 2, joint, quarter), lambda j: (j, 0, 0, 0)))
        out_shape.append(struct((steps + 1, 2, joint, quarter), BF16))
    outs = pl.pallas_call(
        functools.partial(expert_kernel if kept is None else expert_back_kernel, count),
        grid=(steps + 1,),
        in_specs=[pl.BlockSpec(memory_space=pltpu.SMEM)]
        + [whole((held, D))] * count
        + [pair] * len(extra)
        + [anywhere] * len(weights),
        out_specs=out_specs,
        out_shape=out_shape,
        scratch_shapes=[
            pltpu.VMEM((joint, D), BF16),
            pltpu.VMEM((joint, D), F32),
            pltpu.VMEM((2, 2, D, quarter), BF16),
            pltpu.VMEM((2, quarter, D), BF16),
            pltpu.SemaphoreType.DMA((2, ARRAYS)),
        ],
        cost_estimate=cost(
            6 * joint * D * units, 2 * (3 * D * units + 2 * joint * units + 2 * joint * D), joint * units
        ),
    )(info, *rows, *extra, *weights)
    return outs[:count], *outs[count:]


THIRDS = 3


def grads_kernel(groups, *refs):
    rows_in, grads_in, hidden, both = (refs[2 * k * groups : 2 * (k + 1) * groups] for k in range(4))
    outs, (rows, grads, joined, pair) = refs[8 * groups : -4], refs[-4:]

    @pl.when(pl.program_id(0) + pl.program_id(1) == 0)
    def _():
        join([ref.at[0] for ref in rows_in], rows)
        join([ref.at[0, 0] for ref in grads_in], grads)

    join([ref.at[0] for ref in hidden], joined)
    join([ref.at[0] for ref in both], pair)
    values = [dot_tn(rows[...], pair[0]), dot_tn(rows[...], pair[1]), dot_tn(joined[...], grads[...])]
    for place in range(2):

        @pl.when(pl.program_id(0) == place)
        def _():
            for index, value in enumerate(values):
                outs[3 * place + index][...] = value.astype(BF16)


def grads_call(hidden, other_hidden, both, other_both):
    groups, steps, joint, quarter = len(hidden), len(HOPS), hidden[0].shape[1], hidden[0].shape[2]
    part, total = quarter // THIRDS, 2 * len(hidden) * hidden[0].shape[1]

    def specs(block, place):
        return [pl.BlockSpec(block, functools.partial(place, other)) for other in (0, 2) for _ in range(groups)]

    in_specs = [
        *specs((1, joint, quarter), lambda other, j, i: (steps, 0, 0)),
        *specs((1, 1, joint, quarter), lambda other, j, i: (steps, 0, 0, 0)),
        *specs((1, joint, part), lambda other, j, i: (1 - j + other, 0, i)),
        *specs((1, 2, joint, part), lambda other, j, i: (1 - j + other, 0, 0, i)),
    ]

    def placed(place, i, j):
        return jnp.where(j == place, i, (THIRDS - 1) * (1 - place))

    out_specs = []
    for place in range(2):
        out_specs += [pl.BlockSpec((D, part), functools.partial(lambda place, j, i: (0, placed(place, i, j)), place))] * 2
        out_specs.append(pl.BlockSpec((part, D), functools.partial(lambda place, j, i: (placed(place, i, j), 0), place)))
    hiddens, boths = [*hidden, *other_hidden], [*both, *other_both]
    return pl.pallas_call(
        functools.partial(grads_kernel, groups),
        grid=(2, THIRDS),
        in_specs=in_specs,
        out_specs=out_specs,
        out_shape=[struct((D, quarter), BF16)] * 6,
        scratch_shapes=[
            pltpu.VMEM((total, D), BF16),
            pltpu.VMEM((total, D), BF16),
            pltpu.VMEM((total, part), BF16),
            pltpu.VMEM((2, total, part), BF16),
        ],
        cost_estimate=cost(12 * total * D * quarter, 4 * total * (D + 3 * quarter)),
    )(*hiddens, *boths, *hiddens, *boths)


def finish_kernel(first, sums0, sums1, came0, came1, *refs):
    out = refs[-1]

    @pl.when(first[0] == 1)
    def _():
        out[...] = sums0[...].astype(F32) + came0[...].astype(F32)

    @pl.when(first[0] == 0)
    def _():
        out[...] = sums1[...].astype(F32) + came1[...].astype(F32)


def finish(first, arrays, rows, start, base=None):
    count, width = arrays[0].shape
    block = D // 4
    specs = [pl.BlockSpec(memory_space=pltpu.SMEM)] + [pl.BlockSpec((block, width), lambda j: (j, 0))] * 4
    extra = [] if base is None else [base]
    return pl.pallas_call(
        finish_kernel,
        grid=(count // block,),
        in_specs=specs + [pl.BlockSpec(memory_space=pl.ANY)] * len(extra),
        out_specs=pl.BlockSpec((block, width), lambda j: (j + start // block, 0)),
        out_shape=struct((rows, width), F32),
        input_output_aliases={5: 0} if extra else {},
        cost_estimate=cost(4 * count * width, 12 * count * width),
    )(first, *arrays, *extra)


def spell_kernel(core, own, near, qkv, out, small):
    for other, piece in enumerate((own, near)):
        for part in range(3):
            qkv[:, columns(core, other, part)] = piece[:, part * HALF : (part + 1) * HALF].astype(F32)
        out[:, columns(core, other)] = piece[:, WIDE_A:].astype(F32)
    small[...] = own[:, COL_SMALL:WIDE_A].astype(F32)


def across(value, pairs=((0, 1), (1, 0))):
    return lax.ppermute(value, SECTION, pairs)


def hop(value, step):
    return lax.ppermute(value, REPLICA, [(r, r ^ step) for r in range(lax.axis_size(REPLICA))])


def swap(value, step):
    if step == 0:
        return value
    return lax.ppermute(value, EXPERT, [(e, e ^ step) for e in range(lax.axis_size(EXPERT))])


def exchange(value, experts):
    return lax.all_to_all(
        value.reshape(experts, -1, value.shape[-1]), EXPERT, split_axis=0, concat_axis=0, tiled=True
    ).reshape(value.shape)


def groups_of(experts):
    return GROUPS if experts == 4 else ((None,),)


def group_exchange(groups, experts):
    def travel(which, pieces):
        if groups[which] == (None,):
            return [exchange(pieces[0], experts)]
        return [swap(piece, step) for piece, step in zip(pieces, groups[which])]

    return travel


def spread(value, experts, me):
    if experts != 4:
        return exchange(jnp.concatenate([value] * experts), experts)
    came = {step: swap(value, step) for step in (3, 2, 1, 0)}
    for bit in (1, 2):
        flag = me & bit != 0
        came = {step: jnp.where(flag, came[step ^ bit], came[step]) for step in came}
    return jnp.concatenate([came[step] for step in range(4)])


def gathered_sum(parts, experts):
    return jnp.sum(exchange(parts, experts).reshape(experts, -1, WIDE).astype(F32), axis=0)


def ordered(top, mine, theirs):
    return jnp.where(top, theirs, mine), jnp.where(top, mine, theirs)


def joined_cores(own, other):
    return (own.astype(F32) + hop(other, 1).astype(F32)).astype(BF16)


def joined_chips(pair, top):
    mine, theirs = ordered(top, *pair)
    return (mine.astype(F32) + hop(theirs, 2).astype(F32)).astype(BF16)


def anchor_kernel(value, out):
    for index in range(value.shape[0]):
        out[index] = value[index]


def anchor(value):
    scalars = pl.BlockSpec(memory_space=pltpu.SMEM)
    return pl.pallas_call(
        anchor_kernel, in_specs=[scalars], out_specs=scalars, out_shape=struct(value.shape, value.dtype)
    )(value)


def destinations(routes, experts, capacity, me):
    slot = routes.shape[1]
    hits = (routes[..., None] == jnp.arange(experts, dtype=jnp.int32)).astype(F32)
    places = np.arange(slot)
    before = jnp.asarray(places[:, None] > places[None, :], BF16)
    counts = jnp.einsum(
        "ts,lse->lte", before, jnp.sum(hits, axis=2).astype(BF16), preferred_element_type=F32
    )
    place = jnp.sum(hits * counts[:, :, None, :], axis=-1).astype(jnp.int32)
    if experts == 4:
        routes = routes ^ me
        routes = routes ^ (routes >> 1)
    return routes * capacity + place


def step(x_in, cotangent, segments, routes, gains, w_qkv, w_out, router, rel_bias, w_gate_up, w_down):
    section = lax.axis_index(SECTION)
    replica = lax.axis_index(REPLICA)
    me = lax.axis_index(EXPERT)
    first = section == 0
    core = replica % 2
    top = replica // 2 == 1
    experts = router.shape[2]
    held = w_qkv.shape[1]
    slot = x_in.shape[1]
    capacity = 5 * slot // (2 * experts)
    groups = groups_of(experts)
    count = sum(len(group) for group in groups)
    packed_shapes = [struct((experts * capacity // count, D), BF16)] * count
    units = w_down.shape[2]
    quarter = units // len(HOPS)
    core_info = anchor(core.astype(jnp.int32)[None])
    first_info = anchor(first.astype(jnp.int32)[None])
    last_info = anchor(first_info)

    def mine(value):
        return lax.dynamic_index_in_dim(value, section, 0, keepdims=False)

    def by_layer(value, swapped):
        return jnp.where(first, value, swapped), jnp.where(first, swapped, value)

    def half_of(value, part=0):
        return lax.dynamic_slice_in_dim(value, part * D + core * HALF, HALF, 1)

    def placed(value, start):
        return jnp.pad(value, ((0, held - value.shape[0]), (start, LANES - start - value.shape[1])))

    def grouped(values):
        values = list(values)
        return [[values.pop(0) for _ in group] for group in groups]

    routed = jnp.stack(
        by_layer(mine(routes[0]), across(lax.dynamic_index_in_dim(routes[0], 1 - section, 0, keepdims=False)))
    )
    small = placed(router[0], 0) + placed(gains[0].T, LANE_GAIN) + placed(rel_bias[0], LANE_BIAS)
    dense_a = jnp.concatenate([half_of(w_qkv[0], part) for part in range(3)] + [small], axis=1)
    dense_b = half_of(w_out[0])
    halves_a, halves_b = by_layer(dense_a, across(dense_a)), by_layer(dense_b, across(dense_b))

    start = replica * quarter
    near = [
        lax.dynamic_slice(w_gate_up, (0, 0, c, 0, start), (1, 1, 1, D, quarter)).reshape(D, quarter) for c in range(2)
    ] + [lax.dynamic_slice_in_dim(w_down[0, 0], start + c * (quarter // 2), quarter // 2, 0) for c in range(2)]
    near = [across(piece) for piece in near]
    far = [hop(piece, 2) for piece in near]
    weights = [w_gate_up, w_down, *near, *far]
    weights += [hop(piece, 1) for piece in near + far]
    owners = [replica ^ h for h in HOPS]
    infos = [
        anchor(jnp.stack([jnp.where(first, layer, 1 - layer).astype(jnp.int32)] + owners).astype(jnp.int32))
        for layer in range(2)
    ]

    dest = destinations(routed, experts, capacity, me)
    dest_rows = jnp.swapaxes(dest, 1, 2)
    onehot = jnp.asarray(bucket_rows(slot, experts), BF16)
    segment = mine(segments[:, 0])
    seg_col, seg_row = segment[:, None], segment[None, :]
    x = mine(x_in)
    cot = mine(cotangent)

    own_a0 = spread(halves_a[0], experts, me)
    own_b0 = spread(halves_b[0], experts, me)
    dense0 = (own_a0, own_b0, hop(own_a0, 1), hop(own_b0, 1))
    block = held // 4
    part = jnp.concatenate([halves_a[1], halves_b[1]], axis=1)
    part = lax.dynamic_slice_in_dim(part, (replica // 2 * 2 + section) * block, block, 0)
    part = spread(part, experts, me)

    def doubled(flag, value, came):
        pair = ordered(flag, value.reshape(experts, -1, WIDE), came.reshape(experts, -1, WIDE))
        return jnp.concatenate(pair, axis=1).reshape(-1, WIDE)

    part = doubled(jnp.logical_not(first), part, across(part))
    own1 = doubled(top, part, hop(part, 2))
    dense1 = (own1, hop(own1, 1))

    attend_cost = cost(4 * 10**9, 10**7, 10**6)
    back_cost = cost(10**10, 2 * 10**7, 10**6)

    def experts_forward(layer, packed):
        send = group_exchange(groups, experts)
        give = group_exchange(groups, experts)
        kept, hidden, came, returned = [], [], [], []
        for g, pieces in enumerate(grouped(packed)):
            results, both, shared = expert_call(infos[layer], send(g, pieces), weights)
            kept.append(both)
            hidden.append(shared)
            returned += give(g, results)
            came.append(hop(shared, 1))
        return (kept, hidden, came), returned

    common0 = (onehot, seg_col, seg_row, routed[0])
    common1 = (onehot, seg_col, seg_row, routed[1])
    qkv0, mixed0, lse0, small0 = kernel_call(
        mix_kernel, (core_info, x, own_a0, dense0[2], onehot, seg_col, seg_row),
        mix_shapes(slot) + [struct((D, LANES), BF16)], attend_scratch(slot), attend_cost,
    )
    resid0, moe_in0, weights0, *packed0 = kernel_call(
        project_kernel, (core_info, x, small0, own_b0, dense0[3], mixed0, routed[0], dest_rows[0]),
        project_shapes(slot, packed_shapes), [], cost(10**9, 4 * 10**6),
    )
    saved0, returned0 = experts_forward(0, packed0)
    out0, back00, back01, qkv1, mixed1, lse1, resid1, moe_in1, weights1, *packed1 = kernel_call(
        functools.partial(middle_kernel, count),
        (core_info, resid0, weights0, dest[0], *returned0, *dense1, *common1, dest_rows[1]),
        [struct((slot, D), BF16)] * 3 + mix_shapes(slot) + project_shapes(slot, packed_shapes),
        attend_scratch(slot) + [pltpu.VMEM((D, WIDE), BF16)] * 2 + [pltpu.SemaphoreType.DMA((2,))],
        attend_cost, lazy=(4 + count, 5 + count),
    )
    saved1, returned1 = experts_forward(1, packed1)
    out1, *packed1, grad_weights1 = kernel_call(
        functools.partial(turn_kernel, count), (resid1, weights1, dest[1], dest_rows[1], cot, *returned1),
        [struct((slot, D), BF16)] + packed_shapes + [struct((slot, LANES), F32)], [],
        cost(10**9, 4 * 10**6), scalars=0,
    )

    def experts_backward(layer, saved, packed):
        kept, hidden, came = saved
        send = group_exchange(groups, experts)
        give = group_exchange(groups, experts)
        both, came_back, returned = [], [], []
        for g, pieces in enumerate(grouped(packed)):
            results, shared = expert_call(infos[layer], send(g, pieces), weights, kept[g])
            both.append(shared)
            returned += give(g, results)
            came_back.append(hop(shared, 1))
        grads = grads_call(hidden, came, both, came_back)
        summed = []
        for k in range(3):
            came_far = hop(grads[k], 2)
            if layer and k:
                came_far = lax.optimization_barrier((came_far, first_info))[0]
            for span in ((slice(0, D // 2), slice(D // 2, D)) if k == 1 else (slice(None),)):
                summed.append((grads[3 + k][span].astype(F32) + came_far[span].astype(F32)).astype(BF16))
        pairs = ((0, 1),) if layer else ((1, 0),)
        return returned, [(value, across(value, pairs)) for value in summed]

    grad_returned1, expert_sums1 = experts_backward(1, saved1, packed1)
    grad_own1, grad_other1, grad_in1, *grad_packed0, grad_weights0 = kernel_call(
        functools.partial(back_turn_kernel, count),
        (core_info, out0, *dense1, *common1, dest[1], cot, resid1, moe_in1, weights1, grad_weights1, qkv1, mixed1, lse1,
         *grad_returned1, weights0, back00, back01, dest_rows[0]),
        back_shapes(slot) + packed_shapes + [struct((slot, LANES), F32)], back_scratch(slot), back_cost, lazy=(2, 3),
    )
    grad_returned0, expert_sums0 = experts_backward(0, saved0, grad_packed0)
    grad_own0, grad_other0, grad_in0 = kernel_call(
        functools.partial(back_kernel, count),
        (core_info, x, *dense0, *common0, dest[0], grad_in1, resid0, moe_in0, weights0, grad_weights0, qkv0, mixed0, lse0,
         *grad_returned0),
        back_shapes(slot), back_scratch(slot), back_cost, lazy=(2, 3, 4, 5),
    )
    ended = [(sum0, sum1, came0, came1) for (sum0, came0), (sum1, came1) in zip(expert_sums0, expert_sums1)]
    grad_down = finish(last_info, ended[3], D, 0)[None, None]
    grad_gate_up = finish(last_info, ended[0], 2 * D, 0)
    grad_gate_up = finish(last_info, ended[1], 2 * D, D, grad_gate_up)
    grad_gate_up = finish(last_info, ended[2], 2 * D, D + D // 2, grad_gate_up).reshape(1, 1, 2, D, quarter)

    part = joined_cores(grad_own1, grad_other1).reshape(experts, 2, held // 2, WIDE)
    part = joined_chips((part[:, 0], part[:, 1]), top).reshape(-1, WIDE)
    reduced1 = gathered_sum(part, experts)
    part = gathered_sum(joined_cores(grad_own0, grad_other0), experts).astype(BF16)
    reduced0 = joined_chips((part[: held // 2], part[held // 2 :]), top).astype(F32)
    total = jnp.where(first, reduced0, reduced1)
    for value, pair in ((reduced1, (0, 1)), (reduced0, (1, 0))):
        total = total + across(value.astype(BF16), (pair,)).astype(F32)
    total = total.astype(BF16)
    total = jnp.concatenate(ordered(top, total, hop(total, 2)))
    grad_qkv, grad_out, small = kernel_call(
        spell_kernel, (core_info, total, hop(total, 1)),
        [struct((held, 3 * D), F32), struct((held, D), F32), struct((held, LANES), F32)], [], cost(held * D, held * D * 16),
    )

    def both_micro(value0, value1):
        own, swapped = jnp.where(first, value0, value1), across(jnp.where(first, value1, value0))
        return jnp.stack([jnp.where(first, own, swapped), jnp.where(first, swapped, own)])[None]

    return (
        both_micro(out0, out1),
        both_micro(grad_in0, grad_in1),
        small[:, LANE_GAIN : LANE_GAIN + 2].T[None],
        grad_qkv[None],
        grad_out[None],
        small[:, :experts][None],
        small[: rel_bias.shape[1], LANE_BIAS : LANE_BIAS + H][None],
        grad_gate_up,
        grad_down,
    )


def solution(mesh):
    tokens = P(None, (EXPERT, REPLICA), None)
    layered = P(SECTION, None, (EXPERT, REPLICA), None)
    dense = P(SECTION, EXPERT, None)
    gains = P(SECTION, None, EXPERT)
    in_specs = (tokens,) * 3 + (layered, gains) + (dense,) * 4
    in_specs += (P(SECTION, EXPERT, None, None, None), P(SECTION, EXPERT, None, None))
    out_specs = (layered, layered, gains) + (dense,) * 4
    out_specs += (P(SECTION, EXPERT, None, None, REPLICA), P(SECTION, EXPERT, REPLICA, None))
    return jax.shard_map(step, mesh=mesh, in_specs=in_specs, out_specs=out_specs, check_vma=False)
```

```python
import functools
import math

import jax
import jax.numpy as jnp
import numpy as np
from jax import lax
from jax.experimental import pallas as pl
from jax.experimental.pallas import tpu as pltpu
from jax.sharding import PartitionSpec as P


D = 768
H = 12
DH = 64
NB = 32
MAXDIST = 128
EPS = 1e-06
SCALE = 0.125
MASKED = -1000000000.0

LANES = 128
HALF = D // 2
COL_SMALL = 3 * HALF
WIDE_A = COL_SMALL + LANES
WIDE_B = HALF
WIDE = WIDE_A + WIDE_B
LANE_GAIN = 32
LANE_BIAS = 64
HOPS = (0, 2, 1, 3)
GROUPS = ((0, 1), (3, 2))
SECTION, EXPERT, REPLICA = "section", "expert", "replica"


F32 = jnp.float32
BF16 = jnp.bfloat16


def dot(a, b):
    return lax.dot_general(a, b, (((1,), (0,)), ((), ())), preferred_element_type=F32)


def dot_nt(a, b):
    return lax.dot_general(a, b, (((1,), (1,)), ((), ())), preferred_element_type=F32)


def dot_tn(a, b):
    return lax.dot_general(a, b, (((0,), (0,)), ((), ())), preferred_element_type=F32)


def bucket_ids(size, buckets, reach):
    distance = np.arange(size)
    exact = buckets // 2
    scaled = np.log(np.maximum(distance, 1) / exact) / math.log(reach / exact) * (buckets - exact)
    spread = exact + np.floor(np.maximum(scaled, 0.0)).astype(np.int64)
    return np.where(distance < exact, distance, np.minimum(spread, buckets - 1)).astype(np.int32)


def bucket_rows(slot, experts):
    ids = bucket_ids(slot, NB, MAXDIST)
    rows, held = D // experts, NB // experts
    table = np.zeros((D, slot), np.float32)
    for column in range(slot):
        bucket = ids[(slot - column) % slot]
        table[bucket // held * rows + bucket % held, column] = 1.0
    return table


def lane(shape):
    return lax.broadcasted_iota(jnp.int32, shape, 1)


def sublane(shape):
    return lax.broadcasted_iota(jnp.int32, shape, 0)


def one_hot(mask):
    return jnp.where(mask, 1.0, 0.0).astype(BF16)


def gain_rows(small):
    pick = one_hot(lane((8, LANES)) == sublane((8, LANES)) + LANE_GAIN)
    return dot_nt(pick, small)


def inverse_rms(x):
    return lax.rsqrt(jnp.mean(x * x, axis=-1, keepdims=True) + EPS)


def norm_back(x, gain, grad):
    inverse = inverse_rms(x)
    scaled = grad * gain
    along = jnp.mean(scaled * x, axis=-1, keepdims=True)
    return (
        inverse * scaled - x * (inverse * inverse * inverse * along),
        jnp.sum(grad * x * inverse, axis=0, keepdims=True),
    )


def column(values, index):
    return jnp.sum(jnp.where(lane(values.shape) == index, values, 0.0), axis=1, keepdims=True)


def set_masks(seg_col, seg_row, fence):
    slot = fence.shape[0]
    allowed = (sublane((slot, slot)) >= lane((slot, slot))) & (seg_col[...] == seg_row[...])
    fence[...] = jnp.where(allowed, 0.0, MASKED)


def bias_of(table, head, slot):
    row = table[pl.ds(LANE_BIAS + head, 1), :]
    return pltpu.roll(jnp.broadcast_to(row, (slot, slot)), 0, 1, stride=1, stride_axis=0)


def columns(core, other, part=0):
    half = 1 - core[0] if other else core[0]
    return pl.ds(pl.multiple_of(part * D + half * HALF, LANES), HALF)


def dense_views(refs):
    if len(refs) == 4:
        return refs
    return [ref.at[:, span] for ref in refs for span in (pl.ds(0, WIDE_A), pl.ds(WIDE_A, WIDE_B))]


def mix(x, core, dense, onehot, seg_col, seg_row, qkv, mixed, lse, table, fence):
    slot = x.shape[0]
    small = dense[0][:, COL_SMALL:]
    gains = gain_rows(small)
    table[...] = dot_tn(small, onehot[...])
    set_masks(seg_col, seg_row, fence)
    wide = x[...].astype(F32)
    attn_in = (wide * inverse_rms(wide) * gains[0:1]).astype(BF16)
    for other in range(2):
        value = dot(attn_in, dense[2 * other][...]).astype(BF16)
        for part in range(3):
            qkv[:, columns(core, other, part)] = value[:, part * HALF : (part + 1) * HALF]
    lse[...] = jnp.zeros_like(lse)

    def pair(index, _):
        start = pl.multiple_of(index * LANES, LANES)
        query = qkv[:, pl.ds(start, LANES)]
        keys = qkv[:, pl.ds(pl.multiple_of(D + start, LANES), LANES)]
        values = qkv[:, pl.ds(pl.multiple_of(2 * D + start, LANES), LANES)]
        total = jnp.zeros((slot, LANES), F32)
        for half in range(2):
            head = 2 * index + half
            own = lane((slot, LANES)) // DH == half
            scores = dot_nt(jnp.where(own, query, 0.0).astype(BF16), keys) * SCALE
            scores = scores + bias_of(table, head, slot) + fence[...]
            top = jnp.max(scores, axis=-1, keepdims=True)
            powers = jnp.exp(scores - top)
            norm = jnp.sum(powers, axis=-1, keepdims=True)
            probs = (powers / norm).astype(BF16)
            total = total + dot(probs, jnp.where(own, values, 0.0).astype(BF16))
            lse[...] = jnp.where(lane((slot, LANES)) == head, top + jnp.log(norm), lse[...])
        mixed[:, pl.ds(start, LANES)] = total.astype(BF16)
        return 0

    lax.fori_loop(0, H // 2, pair, 0, unroll=2)


def project(x, core, small, outs, mixed, routes, dest_row, resid, moe_in, weights, *packed):
    slot = x.shape[0]
    gains = gain_rows(small)
    for other in range(2):
        span = columns(core, other)
        resid[:, span] = x[:, span].astype(F32) + dot(mixed[...], outs[other][...])
    after = resid[...]
    normed = (after * inverse_rms(after) * gains[1:2]).astype(BF16)
    moe_in[...] = normed
    logits = dot(normed, small)
    chosen = [
        jnp.sum(jnp.where(lane(logits.shape) == routes[:, k : k + 1], logits, 0.0), axis=1, keepdims=True)
        for k in range(2)
    ]
    first = jax.nn.sigmoid(chosen[0] - chosen[1])
    second = jax.nn.sigmoid(chosen[1] - chosen[0])
    places = lane((slot, LANES))
    weights[...] = jnp.where(places == 0, first, jnp.where(places == 1, second, 0.0))
    for index, piece in enumerate(packed):
        rows = sublane((piece.shape[0], slot)) + index * piece.shape[0]
        spread = one_hot((rows == dest_row[0:1, :]) | (rows == dest_row[1:2, :]))
        piece[...] = dot(spread, normed).astype(BF16)


def fetch_rows(dest_col, returned, indices):
    slot = dest_col.shape[0]
    total = jnp.zeros((slot, D), F32)
    for number, piece in enumerate(returned):
        places = lane((slot, piece.shape[0])) + number * piece.shape[0]
        mask = places == dest_col[:, indices[0] : indices[0] + 1]
        for index in indices[1:]:
            mask = mask | (places == dest_col[:, index : index + 1])
        total = total + dot(one_hot(mask), piece[...])
    return total


def combine(resid, weights, dest_col, returned):
    back = [fetch_rows(dest_col, returned, [k]) for k in range(2)]
    out = resid[...] + column(weights[...], 0) * back[0] + column(weights[...], 1) * back[1]
    return out.astype(BF16), back


def dispatch_back(grad, weights, back, dest_row, packed, grad_weights):
    slot = grad.shape[0]
    places = lane((slot, LANES))
    sums = [jnp.sum(grad * back[k], axis=-1, keepdims=True) for k in range(2)]
    grad_weights[...] = jnp.where(places == 0, sums[0], jnp.where(places == 1, sums[1], 0.0))
    scaled = [(column(weights[...], k) * grad).astype(BF16) for k in range(2)]
    for index, piece in enumerate(packed):
        rows = sublane((piece.shape[0], slot)) + index * piece.shape[0]
        total = dot(one_hot(rows == dest_row[0:1, :]), scaled[0]) + dot(one_hot(rows == dest_row[1:2, :]), scaled[1])
        piece[...] = total.astype(BF16)


def mix_kernel(core, x, own_a, other_a, onehot, seg_col, seg_row, qkv, mixed, lse, small, *scratch):
    small[...] = own_a[:, COL_SMALL:]
    mix(x, core, (own_a, None, other_a), onehot, seg_col, seg_row, qkv, mixed, lse, *scratch)


def project_kernel(core, x, small, own_b, other_b, *refs):
    project(x, core, small[...], (own_b, other_b), *refs)


def middle_kernel(count, core, resid, weights, dest_col, *refs):
    returned, refs = refs[:count], refs[count:]
    dense, (onehot, seg_col, seg_row, routes, dest_row), refs = refs[:2], refs[2:7], refs[7:]
    (out, back0, back1, qkv, mixed, lse), projected, scratch, held = refs[:6], refs[6:-5], refs[-5:-3], refs[-3:]
    copies = [pltpu.make_async_copy(dense[k], held[k], held[2].at[k]) for k in range(2)]
    for copy in copies:
        copy.start()
    after, back = combine(resid, weights, dest_col, returned)
    out[...] = after
    back0[...] = back[0].astype(BF16)
    back1[...] = back[1].astype(BF16)
    for copy in copies:
        copy.wait()
    dense = dense_views(held[:2])
    mix(out, core, dense, onehot, seg_col, seg_row, qkv, mixed, lse, *scratch)
    project(out, core, dense[0][:, COL_SMALL:], (dense[1], dense[3]), mixed, routes, dest_row, *projected)


def turn_kernel(count, resid, weights, dest_col, dest_row, cotangent, *refs):
    returned, out, packed, grad_weights = refs[:count], refs[count], refs[count + 1 : -1], refs[-1]
    after, back = combine(resid, weights, dest_col, returned)
    out[...] = after
    dispatch_back(cotangent[...].astype(F32), weights, back, dest_row, packed, grad_weights)


def attend_back(core, x_ref, dense, onehot, seg_col, seg_row, routes, dest_col, grad_out, resid, moe_in, weights, grad_weights,
                qkv, mixed, lse, returned, grad_own, grad_other, grad_in, table, fence, grad_mixed, grad_qkv, sums, flip, grad_attn,
                small_held, held_a, held_b, sems):
    slot = resid.shape[0]
    outs = (grad_own, grad_other)
    first = pltpu.make_async_copy(dense[0].at[:, pl.ds(COL_SMALL, LANES)], small_held, sems.at[0])
    second = [pltpu.make_async_copy(dense[2 * k + 1], held_b.at[k], sems.at[1 + k]) for k in range(2)]
    third = [pltpu.make_async_copy(dense[2 * k], held_a.at[k], sems.at[3 + k]) for k in range(2)]
    for copy in (first, *second, *third):
        copy.start()
    first.wait()
    small = small_held[...]
    gains = gain_rows(small)
    table[...] = dot_tn(small, onehot[...])
    set_masks(seg_col, seg_row, fence)
    grad_moe = fetch_rows(dest_col, returned, [0, 1])
    one, two = column(weights[...], 0), column(weights[...], 1)
    diff = column(grad_weights[...], 0) * one * (1.0 - one) - column(grad_weights[...], 1) * two * (1.0 - two)
    spots = lane((slot, LANES))
    grad_logits = jnp.where(
        spots == routes[:, 0:1], diff, jnp.where(spots == routes[:, 1:2], -diff, 0.0)
    ).astype(BF16)
    grad_moe = grad_moe + dot_nt(grad_logits, small)
    back, gain_moe = norm_back(resid[...], gains[1:2], grad_moe)
    grad_resid = grad_out[...].astype(F32) + back
    grad_attn[...] = grad_resid.astype(BF16)
    parts = [grad_attn[:, columns(core, other)] for other in range(2)]
    for other in range(2):
        outs[other][:, WIDE_A:] = dot_tn(mixed[...], parts[other]).astype(BF16)
    for copy in second:
        copy.wait()
    grad_mixed[...] = (dot_nt(parts[0], held_b[0]) + dot_nt(parts[1], held_b[1])).astype(BF16)
    sums[...] = jnp.zeros_like(sums)
    flip[...] = one_hot(sublane((slot, slot)) + lane((slot, slot)) == slot - 1)

    def pair(index, _):
        start = pl.multiple_of(index * LANES, LANES)
        spans = [pl.ds(pl.multiple_of(part * D + start, LANES), LANES) for part in range(3)]
        query, keys, values = (qkv[:, span] for span in spans)
        grad = grad_mixed[:, pl.ds(start, LANES)]
        totals = [jnp.zeros((slot, LANES), F32) for _ in range(3)]
        for half in range(2):
            head = 2 * index + half
            own = lane((slot, LANES)) // DH == half
            query_own = jnp.where(own, query, 0.0).astype(BF16)
            grad_own = jnp.where(own, grad, 0.0).astype(BF16)
            scores = dot_nt(query_own, keys) * SCALE + bias_of(table, head, slot) + fence[...]
            probs = jnp.exp(scores - column(lse[...], head))
            grad_probs = dot_nt(grad_own, values)
            delta = jnp.sum(grad_probs * probs, axis=-1, keepdims=True)
            grad_scores = (probs * (grad_probs - delta)).astype(BF16)
            turned = pltpu.roll(dot(flip[...], grad_scores), 1, 1, stride=1, stride_axis=0)
            sums[pl.ds(LANE_BIAS + head, 1), :] = jnp.sum(turned, axis=0, keepdims=True)
            totals[0] = totals[0] + dot(grad_scores, jnp.where(own, keys, 0.0).astype(BF16))
            totals[1] = totals[1] + dot_tn(grad_scores, query_own)
            totals[2] = totals[2] + dot_tn(probs.astype(BF16), grad_own)
        for part, factor in enumerate((SCALE, SCALE, 1.0)):
            grad_qkv[:, spans[part]] = (totals[part] * factor).astype(BF16)
        return 0

    lax.fori_loop(0, H // 2, pair, 0, unroll=2)
    x = x_ref[...].astype(F32)
    attn_in = (x * inverse_rms(x) * gains[0:1]).astype(BF16)
    grad_attn_in = jnp.zeros((slot, D), F32)
    for copy in third:
        copy.wait()
    for other in range(2):
        grads = jnp.concatenate([grad_qkv[:, columns(core, other, part)] for part in range(3)], axis=1)
        outs[other][:, :COL_SMALL] = dot_tn(attn_in, grads).astype(BF16)
        grad_attn_in = grad_attn_in + dot_nt(grads, held_a[other, :, :COL_SMALL])
    back, gain_attn = norm_back(x, gains[0:1], grad_attn_in)
    total = (grad_resid + back).astype(BF16)
    grad_in[...] = total
    pick = one_hot(lane((8, LANES)) == sublane((8, LANES)) + LANE_GAIN)
    row = sublane((8, D))
    gain_grads = jnp.where(row == 0, gain_attn, jnp.where(row == 1, gain_moe, 0.0)).astype(BF16)
    grad_small = dot_tn(moe_in[...], grad_logits) + dot_tn(gain_grads, pick) + dot_nt(onehot[...], sums[...].astype(BF16))
    for out in outs:
        out[:, COL_SMALL:WIDE_A] = grad_small.astype(BF16)
    return total


def back_kernel(count, core, x, *refs):
    dense, refs = dense_views(refs[:4]), refs[4:]
    common, returned, rest = refs[:13], refs[13 : 13 + count], refs[13 + count :]
    attend_back(core, x, dense, *common, returned, *rest)


def back_turn_kernel(count, core, x, *refs):
    dense, refs = dense_views(refs[:2]), refs[2:]
    common, returned, refs = refs[:13], refs[13 : 13 + count], refs[13 + count :]
    own_weights, back0, back1, dest_row, grad_own, grad_other, grad_in = refs[:7]
    packed, grad_weights, scratch = refs[7 : 7 + count], refs[7 + count], refs[8 + count :]
    total = attend_back(core, x, dense, *common, returned, grad_own, grad_other, grad_in, *scratch)
    back = [back0[...].astype(F32), back1[...].astype(F32)]
    dispatch_back(total.astype(F32), own_weights, back, dest_row, packed, grad_weights)


def struct(shape, dtype):
    return jax.ShapeDtypeStruct(shape, dtype)


def cost(flops, moved, exps=0):
    return pl.CostEstimate(flops=int(flops), bytes_accessed=int(moved), transcendentals=int(exps))


def mix_shapes(slot):
    return [struct((slot, 3 * D), BF16), struct((slot, D), BF16), struct((slot, LANES), F32)]


def project_shapes(slot, packed):
    return [
        struct((slot, D), F32),
        struct((slot, D), BF16),
        struct((slot, LANES), F32),
    ] + packed


def attend_scratch(slot):
    return [pltpu.VMEM((LANES, slot), F32), pltpu.VMEM((slot, slot), F32)]


def back_scratch(slot):
    return attend_scratch(slot) + [
        pltpu.VMEM((slot, D), BF16),
        pltpu.VMEM((slot, 3 * D), BF16),
        pltpu.VMEM((LANES, slot), F32),
        pltpu.VMEM((slot, slot), BF16),
        pltpu.VMEM((slot, D), BF16),
        pltpu.VMEM((D, LANES), BF16),
        pltpu.VMEM((2, D, WIDE_A), BF16),
        pltpu.VMEM((2, D, WIDE_B), BF16),
        pltpu.SemaphoreType.DMA((5,)),
    ]


def back_shapes(slot):
    return [struct((D, WIDE), BF16)] * 2 + [struct((slot, D), BF16)]


def kernel_call(body, inputs, out_shape, scratch, estimate, scalars=1, lazy=()):
    specs = [
        pl.BlockSpec(memory_space=pltpu.SMEM if k < scalars else pl.ANY if k in lazy else pltpu.VMEM)
        for k in range(len(inputs))
    ]
    return pl.pallas_call(
        body,
        in_specs=specs,
        out_shape=out_shape,
        scratch_shapes=scratch,
        cost_estimate=estimate,
    )(*inputs)


def stream(info, local, pieces, wide, tall, sems):
    local_gate_up, local_down = local
    count = wide.shape[-1]

    half = count // 2

    def copies(slot, gate, up, low, high):
        return [
            pltpu.make_async_copy(gate, wide.at[slot, 0], sems.at[slot, 0]),
            pltpu.make_async_copy(up, wide.at[slot, 1], sems.at[slot, 1]),
            pltpu.make_async_copy(low, tall.at[slot, pl.ds(0, half)], sems.at[slot, 2]),
            pltpu.make_async_copy(high, tall.at[slot, pl.ds(half, half)], sems.at[slot, 3]),
        ]

    def start(step):
        slot = lax.rem(step, 2)

        @pl.when(info[0] == 0)
        def _():
            first = pl.multiple_of(info[1 + step] * count, LANES)
            gate, up = (local_gate_up.at[0, 0, c, :, pl.ds(first, count)] for c in range(2))
            low, high = (local_down.at[0, 0, pl.ds(first + c * half, half), :] for c in range(2))
            for copy in copies(slot, gate, up, low, high):
                copy.start()

        for which in range(len(pieces)):

            @pl.when((info[0] != 0) & (step == which))
            def _():
                for copy in copies(slot, *pieces[which]):
                    copy.start()

    step = pl.program_id(0)

    @pl.when(step == 0)
    def _():
        start(step)

    @pl.when(step + 1 < len(pieces))
    def _():
        start(step + 1)

    slot = lax.rem(step, 2)
    for copy in copies(slot, wide.at[slot, 0], wide.at[slot, 1], *(tall.at[slot, pl.ds(c * half, half)] for c in range(2))):
        copy.wait()
    return slot


ROOT = math.sqrt(2.0 / math.pi)


ARRAYS = 4


def join(refs, scratch):
    at = 0
    for ref in refs:
        span = slice(at, at + ref.shape[-2])
        at += ref.shape[-2]
        scratch[..., span, :] = ref[...]


def accumulate(total, part, results):
    @pl.when(pl.program_id(0) == 0)
    def _():
        total[...] = part

    @pl.when(pl.program_id(0) > 0)
    def _():
        total[...] += part

    @pl.when(pl.program_id(0) == len(HOPS) - 1)
    def _():
        for index, result in enumerate(results):
            count = result.shape[0]
            result[...] = total[index * count : (index + 1) * count, :].astype(BF16)


def split_refs(refs, count):
    sources, refs = refs[: ARRAYS * len(HOPS)], refs[ARRAYS * len(HOPS) :]
    return [sources[ARRAYS * k : ARRAYS * k + ARRAYS] for k in range(len(HOPS))], refs[:count], refs[count:]


def expert_kernel(count, info, *refs):
    rows, local, refs = refs[:count], refs[count : count + 2], refs[count + 2 :]
    pieces, results, (kept, shared, joined, total, wide, tall, sems) = split_refs(refs, count)

    @pl.when(pl.program_id(0) == 0)
    def _():
        join(rows, joined)

    @pl.when(pl.program_id(0) < len(pieces))
    def _():
        slot = stream(info, local, pieces, wide, tall, sems)
        gate = dot(joined[...], wide[slot, 0])
        up = dot(joined[...], wide[slot, 1])
        kept[0] = gate.astype(BF16)
        kept[1] = up.astype(BF16)
        bent = jnp.tanh(ROOT * (gate + 0.044715 * (gate * gate * gate)))
        hidden = (0.5 * gate * (1.0 + bent) * up).astype(BF16)
        shared[0] = hidden
        accumulate(total, dot(hidden, tall[slot]), results)

    @pl.when(pl.program_id(0) == len(pieces))
    def _():
        shared[0] = joined[...]


def expert_back_kernel(count, info, *refs):
    grads, kept, local, refs = refs[:count], refs[count], refs[count + 1 : count + 3], refs[count + 3 :]
    pieces, results, (shared, joined, total, wide, tall, sems) = split_refs(refs, count)

    @pl.when(pl.program_id(0) == 0)
    def _():
        join(grads, joined)

    @pl.when(pl.program_id(0) < len(pieces))
    def _():
        slot = stream(info, local, pieces, wide, tall, sems)
        grad_hidden = dot_nt(joined[...], tall[slot])
        gate, up = kept[0].astype(F32), kept[1].astype(F32)
        square = gate * gate
        bent = jnp.tanh(ROOT * gate * (1.0 + 0.044715 * square))
        half = 0.5 * (1.0 + bent)
        slope = half + (0.5 * ROOT) * gate * (1.0 - bent * bent) * (1.0 + (3 * 0.044715) * square)
        grad_gate = (grad_hidden * up * slope).astype(BF16)
        grad_up = (grad_hidden * gate * half).astype(BF16)
        shared[0, 0] = grad_gate
        shared[0, 1] = grad_up
        accumulate(total, dot_nt(grad_gate, wide[slot, 0]) + dot_nt(grad_up, wide[slot, 1]), results)

    @pl.when(pl.program_id(0) == len(pieces))
    def _():
        for c in range(2):
            shared[0, c] = joined[...]


def whole(shape):
    return pl.BlockSpec(shape, lambda j: (0,) * len(shape))


def expert_call(info, rows, weights, kept=None):
    steps, count = len(HOPS), len(rows)
    held, units = rows[0].shape[0], weights[1].shape[2]
    quarter, joint = units // steps, held * count
    anywhere = pl.BlockSpec(memory_space=pl.ANY)
    pair = pl.BlockSpec((2, joint, quarter), lambda j: (0, 0, jnp.minimum(j, steps - 1)))
    out_specs = [whole((held, D))] * count
    out_shape = [struct((held, D), BF16)] * count
    extra = [] if kept is None else [kept]
    if kept is None:
        out_specs += [pair, pl.BlockSpec((1, joint, quarter), lambda j: (j, 0, 0))]
        out_shape += [struct((2, joint, units), BF16), struct((steps + 1, joint, quarter), BF16)]
    else:
        out_specs.append(pl.BlockSpec((1, 2, joint, quarter), lambda j: (j, 0, 0, 0)))
        out_shape.append(struct((steps + 1, 2, joint, quarter), BF16))
    outs = pl.pallas_call(
        functools.partial(expert_kernel if kept is None else expert_back_kernel, count),
        grid=(steps + 1,),
        in_specs=[pl.BlockSpec(memory_space=pltpu.SMEM)]
        + [whole((held, D))] * count
        + [pair] * len(extra)
        + [anywhere] * len(weights),
        out_specs=out_specs,
        out_shape=out_shape,
        scratch_shapes=[
            pltpu.VMEM((joint, D), BF16),
            pltpu.VMEM((joint, D), F32),
            pltpu.VMEM((2, 2, D, quarter), BF16),
            pltpu.VMEM((2, quarter, D), BF16),
            pltpu.SemaphoreType.DMA((2, ARRAYS)),
        ],
        cost_estimate=cost(
            6 * joint * D * units, 2 * (3 * D * units + 2 * joint * units + 2 * joint * D), joint * units
        ),
    )(info, *rows, *extra, *weights)
    return outs[:count], *outs[count:]


THIRDS = 3


def grads_kernel(groups, *refs):
    rows_in, grads_in, hidden, both = (refs[2 * k * groups : 2 * (k + 1) * groups] for k in range(4))
    outs, (rows, grads, joined, pair) = refs[8 * groups : -4], refs[-4:]

    @pl.when(pl.program_id(0) + pl.program_id(1) == 0)
    def _():
        join([ref.at[0] for ref in rows_in], rows)
        join([ref.at[0, 0] for ref in grads_in], grads)

    join([ref.at[0] for ref in hidden], joined)
    join([ref.at[0] for ref in both], pair)
    values = [dot_tn(rows[...], pair[0]), dot_tn(rows[...], pair[1]), dot_tn(joined[...], grads[...])]
    for place in range(2):

        @pl.when(pl.program_id(0) == place)
        def _():
            for index, value in enumerate(values):
                outs[3 * place + index][...] = value.astype(BF16)


def grads_call(hidden, other_hidden, both, other_both):
    groups, steps, joint, quarter = len(hidden), len(HOPS), hidden[0].shape[1], hidden[0].shape[2]
    part, total = quarter // THIRDS, 2 * len(hidden) * hidden[0].shape[1]

    def specs(block, place):
        return [pl.BlockSpec(block, functools.partial(place, other)) for other in (0, 2) for _ in range(groups)]

    in_specs = [
        *specs((1, joint, quarter), lambda other, j, i: (steps, 0, 0)),
        *specs((1, 1, joint, quarter), lambda other, j, i: (steps, 0, 0, 0)),
        *specs((1, joint, part), lambda other, j, i: (1 - j + other, 0, i)),
        *specs((1, 2, joint, part), lambda other, j, i: (1 - j + other, 0, 0, i)),
    ]

    def placed(place, i, j):
        return jnp.where(j == place, i, (THIRDS - 1) * (1 - place))

    out_specs = []
    for place in range(2):
        out_specs += [pl.BlockSpec((D, part), functools.partial(lambda place, j, i: (0, placed(place, i, j)), place))] * 2
        out_specs.append(pl.BlockSpec((part, D), functools.partial(lambda place, j, i: (placed(place, i, j), 0), place)))
    hiddens, boths = [*hidden, *other_hidden], [*both, *other_both]
    return pl.pallas_call(
        functools.partial(grads_kernel, groups),
        grid=(2, THIRDS),
        in_specs=in_specs,
        out_specs=out_specs,
        out_shape=[struct((D, quarter), BF16)] * 6,
        scratch_shapes=[
            pltpu.VMEM((total, D), BF16),
            pltpu.VMEM((total, D), BF16),
            pltpu.VMEM((total, part), BF16),
            pltpu.VMEM((2, total, part), BF16),
        ],
        cost_estimate=cost(12 * total * D * quarter, 4 * total * (D + 3 * quarter)),
    )(*hiddens, *boths, *hiddens, *boths)


def finish_kernel(first, sums0, sums1, came0, came1, *refs):
    out = refs[-1]

    @pl.when(first[0] == 1)
    def _():
        out[...] = sums0[...].astype(F32) + came0[...].astype(F32)

    @pl.when(first[0] == 0)
    def _():
        out[...] = sums1[...].astype(F32) + came1[...].astype(F32)


def finish(first, arrays, rows, start, base=None):
    count, width = arrays[0].shape
    block = D // 4
    specs = [pl.BlockSpec(memory_space=pltpu.SMEM)] + [pl.BlockSpec((block, width), lambda j: (j, 0))] * 4
    extra = [] if base is None else [base]
    return pl.pallas_call(
        finish_kernel,
        grid=(count // block,),
        in_specs=specs + [pl.BlockSpec(memory_space=pl.ANY)] * len(extra),
        out_specs=pl.BlockSpec((block, width), lambda j: (j + start // block, 0)),
        out_shape=struct((rows, width), F32),
        input_output_aliases={5: 0} if extra else {},
        cost_estimate=cost(4 * count * width, 12 * count * width),
    )(first, *arrays, *extra)


def spell_kernel(core, own, near, qkv, out, gains, router, bias):
    for other, piece in enumerate((own, near)):
        for part in range(3):
            qkv[:, columns(core, other, part)] = piece[:, part * HALF : (part + 1) * HALF].astype(F32)
        out[:, columns(core, other)] = piece[:, WIDE_A:].astype(F32)
    small = own[:, COL_SMALL:WIDE_A]
    gains[...] = gain_rows(small)[:2]
    router[...] = small[:, : router.shape[1]].astype(F32)
    shape = (LANES, bias.shape[1])
    pick = one_hot(sublane(shape) == lane(shape) + LANE_BIAS)
    bias[...] = dot(small, pick)[: bias.shape[0]]


def across(value, pairs=((0, 1), (1, 0))):
    return lax.ppermute(value, SECTION, pairs)


def hop(value, step):
    return lax.ppermute(value, REPLICA, [(r, r ^ step) for r in range(lax.axis_size(REPLICA))])


def swap(value, step):
    if step == 0:
        return value
    return lax.ppermute(value, EXPERT, [(e, e ^ step) for e in range(lax.axis_size(EXPERT))])


def exchange(value, experts):
    return lax.all_to_all(
        value.reshape(experts, -1, value.shape[-1]), EXPERT, split_axis=0, concat_axis=0, tiled=True
    ).reshape(value.shape)


def groups_of(experts):
    return GROUPS if experts == 4 else ((None,),)


def group_exchange(groups, experts):
    def travel(which, pieces):
        if groups[which] == (None,):
            return [exchange(pieces[0], experts)]
        return [swap(piece, step) for piece, step in zip(pieces, groups[which])]

    return travel


def spread(value, experts, me):
    if experts != 4:
        return exchange(jnp.concatenate([value] * experts), experts)
    came = {step: swap(value, step) for step in (3, 2, 1, 0)}
    for bit in (1, 2):
        flag = me & bit != 0
        came = {step: jnp.where(flag, came[step ^ bit], came[step]) for step in came}
    return jnp.concatenate([came[step] for step in range(4)])


def gathered_sum(parts, experts):
    return jnp.sum(exchange(parts, experts).reshape(experts, -1, WIDE).astype(F32), axis=0)


def ordered(top, mine, theirs):
    return jnp.where(top, theirs, mine), jnp.where(top, mine, theirs)


def joined_cores(own, other):
    return (own.astype(F32) + hop(other, 1).astype(F32)).astype(BF16)


def joined_chips(pair, top):
    mine, theirs = ordered(top, *pair)
    return (mine.astype(F32) + hop(theirs, 2).astype(F32)).astype(BF16)


def anchor_kernel(value, out):
    for index in range(value.shape[0]):
        out[index] = value[index]


def anchor(value):
    scalars = pl.BlockSpec(memory_space=pltpu.SMEM)
    return pl.pallas_call(
        anchor_kernel, in_specs=[scalars], out_specs=scalars, out_shape=struct(value.shape, value.dtype)
    )(value)


def destinations(routes, experts, capacity, me):
    slot = routes.shape[1]
    hits = (routes[..., None] == jnp.arange(experts, dtype=jnp.int32)).astype(F32)
    places = np.arange(slot)
    before = jnp.asarray(places[:, None] > places[None, :], BF16)
    counts = jnp.einsum(
        "ts,lse->lte", before, jnp.sum(hits, axis=2).astype(BF16), preferred_element_type=F32
    )
    place = jnp.sum(hits * counts[:, :, None, :], axis=-1).astype(jnp.int32)
    if experts == 4:
        routes = routes ^ me
        routes = routes ^ (routes >> 1)
    return routes * capacity + place


def step(x_in, cotangent, segments, routes, gains, w_qkv, w_out, router, rel_bias, w_gate_up, w_down):
    section = lax.axis_index(SECTION)
    replica = lax.axis_index(REPLICA)
    me = lax.axis_index(EXPERT)
    first = section == 0
    core = replica % 2
    top = replica // 2 == 1
    experts = router.shape[2]
    held = w_qkv.shape[1]
    slot = x_in.shape[1]
    capacity = 5 * slot // (2 * experts)
    groups = groups_of(experts)
    count = sum(len(group) for group in groups)
    packed_shapes = [struct((experts * capacity // count, D), BF16)] * count
    units = w_down.shape[2]
    quarter = units // len(HOPS)
    core_info = anchor(core.astype(jnp.int32)[None])
    first_info = anchor(first.astype(jnp.int32)[None])
    last_info = anchor(first_info)

    def mine(value):
        return lax.dynamic_index_in_dim(value, section, 0, keepdims=False)

    def by_layer(value, swapped):
        return jnp.where(first, value, swapped), jnp.where(first, swapped, value)

    def half_of(value, part=0):
        return lax.dynamic_slice_in_dim(value, part * D + core * HALF, HALF, 1)

    def placed(value, start):
        return jnp.pad(value, ((0, held - value.shape[0]), (start, LANES - start - value.shape[1])))

    def grouped(values):
        values = list(values)
        return [[values.pop(0) for _ in group] for group in groups]

    routed = jnp.stack(
        by_layer(mine(routes[0]), across(lax.dynamic_index_in_dim(routes[0], 1 - section, 0, keepdims=False)))
    )
    small = placed(router[0], 0) + placed(gains[0].T, LANE_GAIN) + placed(rel_bias[0], LANE_BIAS)
    dense_a = jnp.concatenate([half_of(w_qkv[0], part) for part in range(3)] + [small], axis=1)
    dense_b = half_of(w_out[0])
    halves_a, halves_b = by_layer(dense_a, across(dense_a)), by_layer(dense_b, across(dense_b))

    start = replica * quarter
    near = [
        lax.dynamic_slice(w_gate_up, (0, 0, c, 0, start), (1, 1, 1, D, quarter)).reshape(D, quarter) for c in range(2)
    ] + [lax.dynamic_slice_in_dim(w_down[0, 0], start + c * (quarter // 2), quarter // 2, 0) for c in range(2)]
    near = [across(piece) for piece in near]
    far = [hop(piece, 2) for piece in near]
    weights = [w_gate_up, w_down, *near, *far]
    weights += [hop(piece, 1) for piece in near + far]
    owners = [replica ^ h for h in HOPS]
    infos = [
        anchor(jnp.stack([jnp.where(first, layer, 1 - layer).astype(jnp.int32)] + owners).astype(jnp.int32))
        for layer in range(2)
    ]

    dest = destinations(routed, experts, capacity, me)
    dest_rows = jnp.swapaxes(dest, 1, 2)
    onehot = jnp.asarray(bucket_rows(slot, experts), BF16)
    segment = mine(segments[:, 0])
    seg_col, seg_row = segment[:, None], segment[None, :]
    x = mine(x_in)
    cot = mine(cotangent)

    own_a0 = spread(halves_a[0], experts, me)
    own_b0 = spread(halves_b[0], experts, me)
    dense0 = (own_a0, own_b0, hop(own_a0, 1), hop(own_b0, 1))
    block = held // 4
    part = jnp.concatenate([halves_a[1], halves_b[1]], axis=1)
    part = lax.dynamic_slice_in_dim(part, (replica // 2 * 2 + section) * block, block, 0)
    part = spread(part, experts, me)

    def doubled(flag, value, came):
        pair = ordered(flag, value.reshape(experts, -1, WIDE), came.reshape(experts, -1, WIDE))
        return jnp.concatenate(pair, axis=1).reshape(-1, WIDE)

    part = doubled(jnp.logical_not(first), part, across(part))
    own1 = doubled(top, part, hop(part, 2))
    dense1 = (own1, hop(own1, 1))

    attend_cost = cost(4 * 10**9, 10**7, 10**6)
    back_cost = cost(10**10, 2 * 10**7, 10**6)

    def experts_forward(layer, packed):
        send = group_exchange(groups, experts)
        give = group_exchange(groups, experts)
        kept, hidden, came, returned = [], [], [], []
        for g, pieces in enumerate(grouped(packed)):
            results, both, shared = expert_call(infos[layer], send(g, pieces), weights)
            kept.append(both)
            hidden.append(shared)
            returned += give(g, results)
            came.append(hop(shared, 1))
        return (kept, hidden, came), returned

    common0 = (onehot, seg_col, seg_row, routed[0])
    common1 = (onehot, seg_col, seg_row, routed[1])
    qkv0, mixed0, lse0, small0 = kernel_call(
        mix_kernel, (core_info, x, own_a0, dense0[2], onehot, seg_col, seg_row),
        mix_shapes(slot) + [struct((D, LANES), BF16)], attend_scratch(slot), attend_cost,
    )
    resid0, moe_in0, weights0, *packed0 = kernel_call(
        project_kernel, (core_info, x, small0, own_b0, dense0[3], mixed0, routed[0], dest_rows[0]),
        project_shapes(slot, packed_shapes), [], cost(10**9, 4 * 10**6),
    )
    saved0, returned0 = experts_forward(0, packed0)
    out0, back00, back01, qkv1, mixed1, lse1, resid1, moe_in1, weights1, *packed1 = kernel_call(
        functools.partial(middle_kernel, count),
        (core_info, resid0, weights0, dest[0], *returned0, *dense1, *common1, dest_rows[1]),
        [struct((slot, D), BF16)] * 3 + mix_shapes(slot) + project_shapes(slot, packed_shapes),
        attend_scratch(slot) + [pltpu.VMEM((D, WIDE), BF16)] * 2 + [pltpu.SemaphoreType.DMA((2,))],
        attend_cost, lazy=(4 + count, 5 + count),
    )
    saved1, returned1 = experts_forward(1, packed1)
    out1, *packed1, grad_weights1 = kernel_call(
        functools.partial(turn_kernel, count), (resid1, weights1, dest[1], dest_rows[1], cot, *returned1),
        [struct((slot, D), BF16)] + packed_shapes + [struct((slot, LANES), F32)], [],
        cost(10**9, 4 * 10**6), scalars=0,
    )

    def experts_backward(layer, saved, packed):
        kept, hidden, came = saved
        send = group_exchange(groups, experts)
        give = group_exchange(groups, experts)
        both, came_back, returned = [], [], []
        for g, pieces in enumerate(grouped(packed)):
            results, shared = expert_call(infos[layer], send(g, pieces), weights, kept[g])
            both.append(shared)
            returned += give(g, results)
            came_back.append(hop(shared, 1))
        grads = grads_call(hidden, came, both, came_back)
        summed = []
        for k in range(3):
            came_far = hop(grads[k], 2)
            if layer and k:
                came_far = lax.optimization_barrier((came_far, first_info))[0]
            for span in ((slice(0, D // 2), slice(D // 2, D)) if k == 1 else (slice(None),)):
                summed.append((grads[3 + k][span].astype(F32) + came_far[span].astype(F32)).astype(BF16))
        pairs = ((0, 1),) if layer else ((1, 0),)
        return returned, [(value, across(value, pairs)) for value in summed]

    grad_returned1, expert_sums1 = experts_backward(1, saved1, packed1)
    grad_own1, grad_other1, grad_in1, *grad_packed0, grad_weights0 = kernel_call(
        functools.partial(back_turn_kernel, count),
        (core_info, out0, *dense1, *common1, dest[1], cot, resid1, moe_in1, weights1, grad_weights1, qkv1, mixed1, lse1,
         *grad_returned1, weights0, back00, back01, dest_rows[0]),
        back_shapes(slot) + packed_shapes + [struct((slot, LANES), F32)], back_scratch(slot), back_cost, lazy=(2, 3),
    )
    grad_returned0, expert_sums0 = experts_backward(0, saved0, grad_packed0)
    grad_own0, grad_other0, grad_in0 = kernel_call(
        functools.partial(back_kernel, count),
        (core_info, x, *dense0, *common0, dest[0], grad_in1, resid0, moe_in0, weights0, grad_weights0, qkv0, mixed0, lse0,
         *grad_returned0),
        back_shapes(slot), back_scratch(slot), back_cost, lazy=(2, 3, 4, 5),
    )
    ended = [(sum0, sum1, came0, came1) for (sum0, came0), (sum1, came1) in zip(expert_sums0, expert_sums1)]
    grad_down = finish(last_info, ended[3], D, 0)[None, None]
    grad_gate_up = finish(last_info, ended[0], 2 * D, 0)
    grad_gate_up = finish(last_info, ended[1], 2 * D, D, grad_gate_up)
    grad_gate_up = finish(last_info, ended[2], 2 * D, D + D // 2, grad_gate_up).reshape(1, 1, 2, D, quarter)

    part = joined_cores(grad_own1, grad_other1).reshape(experts, 2, held // 2, WIDE)
    part = joined_chips((part[:, 0], part[:, 1]), top).reshape(-1, WIDE)
    reduced1 = gathered_sum(part, experts)
    part = gathered_sum(joined_cores(grad_own0, grad_other0), experts).astype(BF16)
    reduced0 = joined_chips((part[: held // 2], part[held // 2 :]), top).astype(F32)
    total = jnp.where(first, reduced0, reduced1)
    for value, pair in ((reduced1, (0, 1)), (reduced0, (1, 0))):
        total = total + across(value.astype(BF16), (pair,)).astype(F32)
    total = total.astype(BF16)
    total = jnp.concatenate(ordered(top, total, hop(total, 2)))
    dense_grads = kernel_call(
        spell_kernel, (core_info, total, hop(total, 1)),
        [
            struct((held, 3 * D), F32),
            struct((held, D), F32),
            struct((2, held), F32),
            struct((held, experts), F32),
            struct(rel_bias.shape[1:], F32),
        ],
        [],
        cost(held * D, held * D * 16),
    )
    grad_qkv, grad_out, grad_gains, grad_router, grad_bias = (value[None] for value in dense_grads)

    def both_micro(value0, value1):
        own, swapped = jnp.where(first, value0, value1), across(jnp.where(first, value1, value0))
        return jnp.stack([jnp.where(first, own, swapped), jnp.where(first, swapped, own)])[None]

    return (
        both_micro(out0, out1),
        both_micro(grad_in0, grad_in1),
        grad_gains,
        grad_qkv,
        grad_out,
        grad_router,
        grad_bias,
        grad_gate_up,
        grad_down,
    )


def solution(mesh):
    tokens = P(None, (EXPERT, REPLICA), None)
    layered = P(SECTION, None, (EXPERT, REPLICA), None)
    dense = P(SECTION, EXPERT, None)
    gains = P(SECTION, None, EXPERT)
    in_specs = (tokens,) * 3 + (layered, gains) + (dense,) * 4
    in_specs += (P(SECTION, EXPERT, None, None, None), P(SECTION, EXPERT, None, None))
    out_specs = (layered, layered, gains) + (dense,) * 4
    out_specs += (P(SECTION, EXPERT, None, None, REPLICA), P(SECTION, EXPERT, REPLICA, None))
    return jax.shard_map(step, mesh=mesh, in_specs=in_specs, out_specs=out_specs, check_vma=False)
```

```python
import functools
import math

import jax
import jax.numpy as jnp
import numpy as np
from jax import lax
from jax.experimental import pallas as pl
from jax.experimental.pallas import tpu as pltpu
from jax.sharding import PartitionSpec as P


D = 768
H = 12
DH = 64
NB = 32
MAXDIST = 128
EPS = 1e-06
SCALE = 0.125
MASKED = -1000000000.0

LANES = 128
HALF = D // 2
COL_SMALL = 3 * HALF
WIDE_A = COL_SMALL + LANES
WIDE_B = HALF
WIDE = WIDE_A + WIDE_B
LANE_GAIN = 32
LANE_BIAS = 64
HOPS = (0, 2, 1, 3)
GROUPS = ((0, 1), (3, 2))
SECTION, EXPERT, REPLICA = "section", "expert", "replica"


F32 = jnp.float32
BF16 = jnp.bfloat16


def dot(a, b):
    return lax.dot_general(a, b, (((1,), (0,)), ((), ())), preferred_element_type=F32)


def dot_nt(a, b):
    return lax.dot_general(a, b, (((1,), (1,)), ((), ())), preferred_element_type=F32)


def dot_tn(a, b):
    return lax.dot_general(a, b, (((0,), (0,)), ((), ())), preferred_element_type=F32)


def bucket_ids(size, buckets, reach):
    distance = np.arange(size)
    exact = buckets // 2
    scaled = np.log(np.maximum(distance, 1) / exact) / math.log(reach / exact) * (buckets - exact)
    spread = exact + np.floor(np.maximum(scaled, 0.0)).astype(np.int64)
    return np.where(distance < exact, distance, np.minimum(spread, buckets - 1)).astype(np.int32)


def bucket_rows(slot, experts):
    ids = bucket_ids(slot, NB, MAXDIST)
    rows, held = D // experts, NB // experts
    table = np.zeros((D, slot), np.float32)
    for column in range(slot):
        bucket = ids[(slot - column) % slot]
        table[bucket // held * rows + bucket % held, column] = 1.0
    return table


def lane(shape):
    return lax.broadcasted_iota(jnp.int32, shape, 1)


def sublane(shape):
    return lax.broadcasted_iota(jnp.int32, shape, 0)


def one_hot(mask):
    return jnp.where(mask, 1.0, 0.0).astype(BF16)


def gain_rows(small):
    pick = one_hot(lane((8, LANES)) == sublane((8, LANES)) + LANE_GAIN)
    return dot_nt(pick, small)


def inverse_rms(x):
    return lax.rsqrt(jnp.mean(x * x, axis=-1, keepdims=True) + EPS)


def norm_back(x, gain, grad):
    inverse = inverse_rms(x)
    scaled = grad * gain
    along = jnp.mean(scaled * x, axis=-1, keepdims=True)
    return (
        inverse * scaled - x * (inverse * inverse * inverse * along),
        jnp.sum(grad * x * inverse, axis=0, keepdims=True),
    )


def column(values, index):
    return jnp.sum(jnp.where(lane(values.shape) == index, values, 0.0), axis=1, keepdims=True)


def set_masks(seg_col, seg_row, fence):
    slot = fence.shape[0]
    allowed = (sublane((slot, slot)) >= lane((slot, slot))) & (seg_col[...] == seg_row[...])
    fence[...] = jnp.where(allowed, 0.0, MASKED)


def bias_of(table, head, slot):
    row = table[pl.ds(LANE_BIAS + head, 1), :]
    return pltpu.roll(jnp.broadcast_to(row, (slot, slot)), 0, 1, stride=1, stride_axis=0)


def columns(core, other, part=0):
    half = 1 - core[0] if other else core[0]
    return pl.ds(pl.multiple_of(part * D + half * HALF, LANES), HALF)


def dense_views(refs):
    if len(refs) == 4:
        return refs
    return [ref.at[:, span] for ref in refs for span in (pl.ds(0, WIDE_A), pl.ds(WIDE_A, WIDE_B))]


def mix(x, core, dense, onehot, seg_col, seg_row, qkv, mixed, lse, table, fence):
    slot = x.shape[0]
    small = dense[0][:, COL_SMALL:]
    gains = gain_rows(small)
    table[...] = dot_tn(small, onehot[...])
    set_masks(seg_col, seg_row, fence)
    wide = x[...].astype(F32)
    attn_in = (wide * inverse_rms(wide) * gains[0:1]).astype(BF16)
    for other in range(2):
        value = dot(attn_in, dense[2 * other][...]).astype(BF16)
        for part in range(3):
            qkv[:, columns(core, other, part)] = value[:, part * HALF : (part + 1) * HALF]
    lse[...] = jnp.zeros_like(lse)

    def pair(index, _):
        start = pl.multiple_of(index * LANES, LANES)
        query = qkv[:, pl.ds(start, LANES)]
        keys = qkv[:, pl.ds(pl.multiple_of(D + start, LANES), LANES)]
        values = qkv[:, pl.ds(pl.multiple_of(2 * D + start, LANES), LANES)]
        total = jnp.zeros((slot, LANES), F32)
        for half in range(2):
            head = 2 * index + half
            own = lane((slot, LANES)) // DH == half
            scores = dot_nt(jnp.where(own, query, 0.0).astype(BF16), keys) * SCALE
            scores = scores + bias_of(table, head, slot) + fence[...]
            top = jnp.max(scores, axis=-1, keepdims=True)
            powers = jnp.exp(scores - top)
            norm = jnp.sum(powers, axis=-1, keepdims=True)
            probs = (powers / norm).astype(BF16)
            total = total + dot(probs, jnp.where(own, values, 0.0).astype(BF16))
            lse[...] = jnp.where(lane((slot, LANES)) == head, top + jnp.log(norm), lse[...])
        mixed[:, pl.ds(start, LANES)] = total.astype(BF16)
        return 0

    lax.fori_loop(0, H // 2, pair, 0, unroll=2)


def project(x, core, small, outs, mixed, routes, dest_row, resid, moe_in, weights, *packed):
    slot = x.shape[0]
    gains = gain_rows(small)
    for other in range(2):
        span = columns(core, other)
        resid[:, span] = x[:, span].astype(F32) + dot(mixed[...], outs[other][...])
    after = resid[...]
    normed = (after * inverse_rms(after) * gains[1:2]).astype(BF16)
    moe_in[...] = normed
    logits = dot(normed, small)
    chosen = [
        jnp.sum(jnp.where(lane(logits.shape) == routes[:, k : k + 1], logits, 0.0), axis=1, keepdims=True)
        for k in range(2)
    ]
    first = jax.nn.sigmoid(chosen[0] - chosen[1])
    second = jax.nn.sigmoid(chosen[1] - chosen[0])
    places = lane((slot, LANES))
    weights[...] = jnp.where(places == 0, first, jnp.where(places == 1, second, 0.0))
    for index, piece in enumerate(packed):
        rows = sublane((piece.shape[0], slot)) + index * piece.shape[0]
        spread = one_hot((rows == dest_row[0:1, :]) | (rows == dest_row[1:2, :]))
        piece[...] = dot(spread, normed).astype(BF16)


def fetch_rows(dest_col, returned, indices):
    slot = dest_col.shape[0]
    total = jnp.zeros((slot, D), F32)
    for number, piece in enumerate(returned):
        places = lane((slot, piece.shape[0])) + number * piece.shape[0]
        mask = places == dest_col[:, indices[0] : indices[0] + 1]
        for index in indices[1:]:
            mask = mask | (places == dest_col[:, index : index + 1])
        total = total + dot(one_hot(mask), piece[...])
    return total


def combine(resid, weights, dest_col, returned):
    back = [fetch_rows(dest_col, returned, [k]) for k in range(2)]
    out = resid[...] + column(weights[...], 0) * back[0] + column(weights[...], 1) * back[1]
    return out.astype(BF16), back


def dispatch_back(grad, weights, back, dest_row, packed, grad_weights):
    slot = grad.shape[0]
    places = lane((slot, LANES))
    sums = [jnp.sum(grad * back[k], axis=-1, keepdims=True) for k in range(2)]
    grad_weights[...] = jnp.where(places == 0, sums[0], jnp.where(places == 1, sums[1], 0.0))
    scaled = [(column(weights[...], k) * grad).astype(BF16) for k in range(2)]
    for index, piece in enumerate(packed):
        rows = sublane((piece.shape[0], slot)) + index * piece.shape[0]
        total = dot(one_hot(rows == dest_row[0:1, :]), scaled[0]) + dot(one_hot(rows == dest_row[1:2, :]), scaled[1])
        piece[...] = total.astype(BF16)


def mix_kernel(core, x, own_a, other_a, onehot, seg_col, seg_row, qkv, mixed, lse, small, *scratch):
    small[...] = own_a[:, COL_SMALL:]
    mix(x, core, (own_a, None, other_a), onehot, seg_col, seg_row, qkv, mixed, lse, *scratch)


def project_kernel(core, x, small, own_b, other_b, *refs):
    project(x, core, small[...], (own_b, other_b), *refs)


def middle_kernel(count, core, resid, weights, dest_col, *refs):
    returned, refs = refs[:count], refs[count:]
    dense, (onehot, seg_col, seg_row, routes, dest_row), refs = refs[:2], refs[2:7], refs[7:]
    (out, back0, back1, qkv, mixed, lse), projected, scratch, held = refs[:6], refs[6:-5], refs[-5:-3], refs[-3:]
    copies = [pltpu.make_async_copy(dense[k], held[k], held[2].at[k]) for k in range(2)]
    for copy in copies:
        copy.start()
    after, back = combine(resid, weights, dest_col, returned)
    out[...] = after
    back0[...] = back[0].astype(BF16)
    back1[...] = back[1].astype(BF16)
    for copy in copies:
        copy.wait()
    dense = dense_views(held[:2])
    mix(out, core, dense, onehot, seg_col, seg_row, qkv, mixed, lse, *scratch)
    project(out, core, dense[0][:, COL_SMALL:], (dense[1], dense[3]), mixed, routes, dest_row, *projected)


def turn_kernel(count, resid, weights, dest_col, dest_row, cotangent, *refs):
    returned, out, packed, grad_weights = refs[:count], refs[count], refs[count + 1 : -1], refs[-1]
    after, back = combine(resid, weights, dest_col, returned)
    out[...] = after
    dispatch_back(cotangent[...].astype(F32), weights, back, dest_row, packed, grad_weights)


def attend_back(core, x_ref, dense, onehot, seg_col, seg_row, routes, dest_col, grad_out, resid, moe_in, weights, grad_weights,
                qkv, mixed, lse, returned, grad_own, grad_other, grad_in, table, fence, grad_mixed, grad_qkv, sums, flip, grad_attn,
                small_held, held_a, held_b, sems):
    slot = resid.shape[0]
    outs = (grad_own, grad_other)
    first = pltpu.make_async_copy(dense[0].at[:, pl.ds(COL_SMALL, LANES)], small_held, sems.at[0])
    second = [pltpu.make_async_copy(dense[2 * k + 1], held_b.at[k], sems.at[1 + k]) for k in range(2)]
    third = [pltpu.make_async_copy(dense[2 * k], held_a.at[k], sems.at[3 + k]) for k in range(2)]
    for copy in (first, *second, *third):
        copy.start()
    first.wait()
    small = small_held[...]
    gains = gain_rows(small)
    table[...] = dot_tn(small, onehot[...])
    set_masks(seg_col, seg_row, fence)
    grad_moe = fetch_rows(dest_col, returned, [0, 1])
    one, two = column(weights[...], 0), column(weights[...], 1)
    diff = column(grad_weights[...], 0) * one * (1.0 - one) - column(grad_weights[...], 1) * two * (1.0 - two)
    spots = lane((slot, LANES))
    grad_logits = jnp.where(
        spots == routes[:, 0:1], diff, jnp.where(spots == routes[:, 1:2], -diff, 0.0)
    ).astype(BF16)
    grad_moe = grad_moe + dot_nt(grad_logits, small)
    back, gain_moe = norm_back(resid[...], gains[1:2], grad_moe)
    grad_resid = grad_out[...].astype(F32) + back
    grad_attn[...] = grad_resid.astype(BF16)
    parts = [grad_attn[:, columns(core, other)] for other in range(2)]
    for other in range(2):
        outs[other][:, WIDE_A:] = dot_tn(mixed[...], parts[other]).astype(BF16)
    for copy in second:
        copy.wait()
    grad_mixed[...] = (dot_nt(parts[0], held_b[0]) + dot_nt(parts[1], held_b[1])).astype(BF16)
    sums[...] = jnp.zeros_like(sums)
    flip[...] = one_hot(sublane((slot, slot)) + lane((slot, slot)) == slot - 1)

    def pair(index, _):
        start = pl.multiple_of(index * LANES, LANES)
        spans = [pl.ds(pl.multiple_of(part * D + start, LANES), LANES) for part in range(3)]
        query, keys, values = (qkv[:, span] for span in spans)
        grad = grad_mixed[:, pl.ds(start, LANES)]
        totals = [jnp.zeros((slot, LANES), F32) for _ in range(3)]
        for half in range(2):
            head = 2 * index + half
            own = lane((slot, LANES)) // DH == half
            query_own = jnp.where(own, query, 0.0).astype(BF16)
            grad_own = jnp.where(own, grad, 0.0).astype(BF16)
            scores = dot_nt(query_own, keys) * SCALE + bias_of(table, head, slot) + fence[...]
            probs = jnp.exp(scores - column(lse[...], head))
            grad_probs = dot_nt(grad_own, values)
            delta = jnp.sum(grad_probs * probs, axis=-1, keepdims=True)
            grad_scores = (probs * (grad_probs - delta)).astype(BF16)
            turned = pltpu.roll(dot(flip[...], grad_scores), 1, 1, stride=1, stride_axis=0)
            sums[pl.ds(LANE_BIAS + head, 1), :] = jnp.sum(turned, axis=0, keepdims=True)
            totals[0] = totals[0] + dot(grad_scores, jnp.where(own, keys, 0.0).astype(BF16))
            totals[1] = totals[1] + dot_tn(grad_scores, query_own)
            totals[2] = totals[2] + dot_tn(probs.astype(BF16), grad_own)
        for part, factor in enumerate((SCALE, SCALE, 1.0)):
            grad_qkv[:, spans[part]] = (totals[part] * factor).astype(BF16)
        return 0

    lax.fori_loop(0, H // 2, pair, 0, unroll=2)
    x = x_ref[...].astype(F32)
    attn_in = (x * inverse_rms(x) * gains[0:1]).astype(BF16)
    grad_attn_in = jnp.zeros((slot, D), F32)
    for copy in third:
        copy.wait()
    for other in range(2):
        grads = jnp.concatenate([grad_qkv[:, columns(core, other, part)] for part in range(3)], axis=1)
        outs[other][:, :COL_SMALL] = dot_tn(attn_in, grads).astype(BF16)
        grad_attn_in = grad_attn_in + dot_nt(grads, held_a[other, :, :COL_SMALL])
    back, gain_attn = norm_back(x, gains[0:1], grad_attn_in)
    total = (grad_resid + back).astype(BF16)
    grad_in[...] = total
    pick = one_hot(lane((8, LANES)) == sublane((8, LANES)) + LANE_GAIN)
    row = sublane((8, D))
    gain_grads = jnp.where(row == 0, gain_attn, jnp.where(row == 1, gain_moe, 0.0)).astype(BF16)
    grad_small = dot_tn(moe_in[...], grad_logits) + dot_tn(gain_grads, pick) + dot_nt(onehot[...], sums[...].astype(BF16))
    for out in outs:
        out[:, COL_SMALL:WIDE_A] = grad_small.astype(BF16)
    return total


def back_kernel(count, core, x, *refs):
    dense, refs = dense_views(refs[:4]), refs[4:]
    common, returned, rest = refs[:13], refs[13 : 13 + count], refs[13 + count :]
    attend_back(core, x, dense, *common, returned, *rest)


def back_turn_kernel(count, core, x, *refs):
    dense, refs = dense_views(refs[:2]), refs[2:]
    common, returned, refs = refs[:13], refs[13 : 13 + count], refs[13 + count :]
    own_weights, back0, back1, dest_row, grad_own, grad_other, grad_in = refs[:7]
    packed, grad_weights, scratch = refs[7 : 7 + count], refs[7 + count], refs[8 + count :]
    total = attend_back(core, x, dense, *common, returned, grad_own, grad_other, grad_in, *scratch)
    back = [back0[...].astype(F32), back1[...].astype(F32)]
    dispatch_back(total.astype(F32), own_weights, back, dest_row, packed, grad_weights)


def struct(shape, dtype):
    return jax.ShapeDtypeStruct(shape, dtype)


def cost(flops, moved, exps=0):
    return pl.CostEstimate(flops=int(flops), bytes_accessed=int(moved), transcendentals=int(exps))


def mix_shapes(slot):
    return [struct((slot, 3 * D), BF16), struct((slot, D), BF16), struct((slot, LANES), F32)]


def project_shapes(slot, packed):
    return [
        struct((slot, D), F32),
        struct((slot, D), BF16),
        struct((slot, LANES), F32),
    ] + packed


def attend_scratch(slot):
    return [pltpu.VMEM((LANES, slot), F32), pltpu.VMEM((slot, slot), F32)]


def back_scratch(slot):
    return attend_scratch(slot) + [
        pltpu.VMEM((slot, D), BF16),
        pltpu.VMEM((slot, 3 * D), BF16),
        pltpu.VMEM((LANES, slot), F32),
        pltpu.VMEM((slot, slot), BF16),
        pltpu.VMEM((slot, D), BF16),
        pltpu.VMEM((D, LANES), BF16),
        pltpu.VMEM((2, D, WIDE_A), BF16),
        pltpu.VMEM((2, D, WIDE_B), BF16),
        pltpu.SemaphoreType.DMA((5,)),
    ]


def back_shapes(slot):
    return [struct((D, WIDE), BF16)] * 2 + [struct((slot, D), BF16)]


def kernel_call(body, inputs, out_shape, scratch, estimate, scalars=1, lazy=()):
    specs = [
        pl.BlockSpec(memory_space=pltpu.SMEM if k < scalars else pl.ANY if k in lazy else pltpu.VMEM)
        for k in range(len(inputs))
    ]
    return pl.pallas_call(
        body,
        in_specs=specs,
        out_shape=out_shape,
        scratch_shapes=scratch,
        cost_estimate=estimate,
    )(*inputs)


def stream(info, local, pieces, wide, tall, sems):
    local_gate_up, local_down = local
    count = wide.shape[-1]

    half = count // 2

    def copies(slot, gate, up, low, high):
        return [
            pltpu.make_async_copy(gate, wide.at[slot, 0], sems.at[slot, 0]),
            pltpu.make_async_copy(up, wide.at[slot, 1], sems.at[slot, 1]),
            pltpu.make_async_copy(low, tall.at[slot, pl.ds(0, half)], sems.at[slot, 2]),
            pltpu.make_async_copy(high, tall.at[slot, pl.ds(half, half)], sems.at[slot, 3]),
        ]

    def start(step):
        slot = lax.rem(step, 2)

        @pl.when(info[0] == 0)
        def _():
            first = pl.multiple_of(info[1 + step] * count, LANES)
            gate, up = (local_gate_up.at[0, 0, c, :, pl.ds(first, count)] for c in range(2))
            low, high = (local_down.at[0, 0, pl.ds(first + c * half, half), :] for c in range(2))
            for copy in copies(slot, gate, up, low, high):
                copy.start()

        for which in range(len(pieces)):

            @pl.when((info[0] != 0) & (step == which))
            def _():
                for copy in copies(slot, *pieces[which]):
                    copy.start()

    step = pl.program_id(0)

    @pl.when(step == 0)
    def _():
        start(step)

    @pl.when(step + 1 < len(pieces))
    def _():
        start(step + 1)

    slot = lax.rem(step, 2)
    for copy in copies(slot, wide.at[slot, 0], wide.at[slot, 1], *(tall.at[slot, pl.ds(c * half, half)] for c in range(2))):
        copy.wait()
    return slot


ROOT = math.sqrt(2.0 / math.pi)


ARRAYS = 4


def join(refs, scratch):
    at = 0
    for ref in refs:
        span = slice(at, at + ref.shape[-2])
        at += ref.shape[-2]
        scratch[..., span, :] = ref[...]


def accumulate(total, part, results):
    @pl.when(pl.program_id(0) == 0)
    def _():
        total[...] = part

    @pl.when(pl.program_id(0) > 0)
    def _():
        total[...] += part

    @pl.when(pl.program_id(0) == len(HOPS) - 1)
    def _():
        for index, result in enumerate(results):
            count = result.shape[0]
            result[...] = total[index * count : (index + 1) * count, :].astype(BF16)


def split_refs(refs, count):
    sources, refs = refs[: ARRAYS * len(HOPS)], refs[ARRAYS * len(HOPS) :]
    return [sources[ARRAYS * k : ARRAYS * k + ARRAYS] for k in range(len(HOPS))], refs[:count], refs[count:]


def expert_kernel(count, info, *refs):
    rows, local, refs = refs[:count], refs[count : count + 2], refs[count + 2 :]
    pieces, results, (kept, shared, joined, total, wide, tall, sems) = split_refs(refs, count)

    @pl.when(pl.program_id(0) == 0)
    def _():
        join(rows, joined)

    @pl.when(pl.program_id(0) < len(pieces))
    def _():
        slot = stream(info, local, pieces, wide, tall, sems)
        gate = dot(joined[...], wide[slot, 0])
        up = dot(joined[...], wide[slot, 1])
        kept[0] = gate.astype(BF16)
        kept[1] = up.astype(BF16)
        bent = jnp.tanh(ROOT * (gate + 0.044715 * (gate * gate * gate)))
        hidden = (0.5 * gate * (1.0 + bent) * up).astype(BF16)
        shared[0] = hidden
        accumulate(total, dot(hidden, tall[slot]), results)

    @pl.when(pl.program_id(0) == len(pieces))
    def _():
        shared[0] = joined[...]


def expert_back_kernel(count, info, *refs):
    grads, kept, local, refs = refs[:count], refs[count], refs[count + 1 : count + 3], refs[count + 3 :]
    pieces, results, (shared, joined, total, wide, tall, sems) = split_refs(refs, count)

    @pl.when(pl.program_id(0) == 0)
    def _():
        join(grads, joined)

    @pl.when(pl.program_id(0) < len(pieces))
    def _():
        slot = stream(info, local, pieces, wide, tall, sems)
        grad_hidden = dot_nt(joined[...], tall[slot])
        gate, up = kept[0].astype(F32), kept[1].astype(F32)
        square = gate * gate
        bent = jnp.tanh(ROOT * gate * (1.0 + 0.044715 * square))
        half = 0.5 * (1.0 + bent)
        slope = half + (0.5 * ROOT) * gate * (1.0 - bent * bent) * (1.0 + (3 * 0.044715) * square)
        grad_gate = (grad_hidden * up * slope).astype(BF16)
        grad_up = (grad_hidden * gate * half).astype(BF16)
        shared[0, 0] = grad_gate
        shared[0, 1] = grad_up
        accumulate(total, dot_nt(grad_gate, wide[slot, 0]) + dot_nt(grad_up, wide[slot, 1]), results)

    @pl.when(pl.program_id(0) == len(pieces))
    def _():
        for c in range(2):
            shared[0, c] = joined[...]


def whole(shape):
    return pl.BlockSpec(shape, lambda j: (0,) * len(shape))


def expert_call(info, rows, weights, kept=None):
    steps, count = len(HOPS), len(rows)
    held, units = rows[0].shape[0], weights[1].shape[2]
    quarter, joint = units // steps, held * count
    anywhere = pl.BlockSpec(memory_space=pl.ANY)
    pair = pl.BlockSpec((2, joint, quarter), lambda j: (0, 0, jnp.minimum(j, steps - 1)))
    out_specs = [whole((held, D))] * count
    out_shape = [struct((held, D), BF16)] * count
    extra = [] if kept is None else [kept]
    if kept is None:
        out_specs += [pair, pl.BlockSpec((1, joint, quarter), lambda j: (j, 0, 0))]
        out_shape += [struct((2, joint, units), BF16), struct((steps + 1, joint, quarter), BF16)]
    else:
        out_specs.append(pl.BlockSpec((1, 2, joint, quarter), lambda j: (j, 0, 0, 0)))
        out_shape.append(struct((steps + 1, 2, joint, quarter), BF16))
    outs = pl.pallas_call(
        functools.partial(expert_kernel if kept is None else expert_back_kernel, count),
        grid=(steps + 1,),
        in_specs=[pl.BlockSpec(memory_space=pltpu.SMEM)]
        + [whole((held, D))] * count
        + [pair] * len(extra)
        + [anywhere] * len(weights),
        out_specs=out_specs,
        out_shape=out_shape,
        scratch_shapes=[
            pltpu.VMEM((joint, D), BF16),
            pltpu.VMEM((joint, D), F32),
            pltpu.VMEM((2, 2, D, quarter), BF16),
            pltpu.VMEM((2, quarter, D), BF16),
            pltpu.SemaphoreType.DMA((2, ARRAYS)),
        ],
        cost_estimate=cost(
            6 * joint * D * units, 2 * (3 * D * units + 2 * joint * units + 2 * joint * D), joint * units
        ),
    )(info, *rows, *extra, *weights)
    return outs[:count], *outs[count:]


THIRDS = 3


def grads_kernel(groups, *refs):
    rows_in, grads_in, hidden, both = (refs[2 * k * groups : 2 * (k + 1) * groups] for k in range(4))
    outs, (rows, grads, joined, pair) = refs[8 * groups : -4], refs[-4:]

    @pl.when(pl.program_id(0) + pl.program_id(1) == 0)
    def _():
        join([ref.at[0] for ref in rows_in], rows)
        join([ref.at[0, 0] for ref in grads_in], grads)

    join([ref.at[0] for ref in hidden], joined)
    join([ref.at[0] for ref in both], pair)
    values = [dot_tn(rows[...], pair[0]), dot_tn(rows[...], pair[1]), dot_tn(joined[...], grads[...])]
    for place in range(2):

        @pl.when(pl.program_id(0) == place)
        def _():
            for index, value in enumerate(values):
                outs[3 * place + index][...] = value.astype(BF16)


def grads_call(hidden, other_hidden, both, other_both):
    groups, steps, joint, quarter = len(hidden), len(HOPS), hidden[0].shape[1], hidden[0].shape[2]
    part, total = quarter // THIRDS, 2 * len(hidden) * hidden[0].shape[1]

    def specs(block, place):
        return [pl.BlockSpec(block, functools.partial(place, other)) for other in (0, 2) for _ in range(groups)]

    in_specs = [
        *specs((1, joint, quarter), lambda other, j, i: (steps, 0, 0)),
        *specs((1, 1, joint, quarter), lambda other, j, i: (steps, 0, 0, 0)),
        *specs((1, joint, part), lambda other, j, i: (1 - j + other, 0, i)),
        *specs((1, 2, joint, part), lambda other, j, i: (1 - j + other, 0, 0, i)),
    ]

    def placed(place, i, j):
        return jnp.where(j == place, i, (THIRDS - 1) * (1 - place))

    out_specs = []
    for place in range(2):
        out_specs += [pl.BlockSpec((D, part), functools.partial(lambda place, j, i: (0, placed(place, i, j)), place))] * 2
        out_specs.append(pl.BlockSpec((part, D), functools.partial(lambda place, j, i: (placed(place, i, j), 0), place)))
    hiddens, boths = [*hidden, *other_hidden], [*both, *other_both]
    return pl.pallas_call(
        functools.partial(grads_kernel, groups),
        grid=(2, THIRDS),
        in_specs=in_specs,
        out_specs=out_specs,
        out_shape=[struct((D, quarter), BF16)] * 6,
        scratch_shapes=[
            pltpu.VMEM((total, D), BF16),
            pltpu.VMEM((total, D), BF16),
            pltpu.VMEM((total, part), BF16),
            pltpu.VMEM((2, total, part), BF16),
        ],
        cost_estimate=cost(12 * total * D * quarter, 4 * total * (D + 3 * quarter)),
    )(*hiddens, *boths, *hiddens, *boths)


def finish_kernel(first, sums0, sums1, came0, came1, *refs):
    out = refs[-1]

    @pl.when(first[0] == 1)
    def _():
        out[...] = sums0[...].astype(F32) + came0[...].astype(F32)

    @pl.when(first[0] == 0)
    def _():
        out[...] = sums1[...].astype(F32) + came1[...].astype(F32)


def finish(first, arrays, rows, start, base=None):
    count, width = arrays[0].shape
    block = D // 4
    specs = [pl.BlockSpec(memory_space=pltpu.SMEM)] + [pl.BlockSpec((block, width), lambda j: (j, 0))] * 4
    extra = [] if base is None else [base]
    return pl.pallas_call(
        finish_kernel,
        grid=(count // block,),
        in_specs=specs + [pl.BlockSpec(memory_space=pl.ANY)] * len(extra),
        out_specs=pl.BlockSpec((block, width), lambda j: (j + start // block, 0)),
        out_shape=struct((rows, width), F32),
        input_output_aliases={5: 0} if extra else {},
        cost_estimate=cost(4 * count * width, 12 * count * width),
    )(first, *arrays, *extra)


def spell_kernel(core, own, near, qkv, out, gains, router, bias):
    for other, piece in enumerate((own, near)):
        for part in range(3):
            qkv[:, columns(core, other, part)] = piece[:, part * HALF : (part + 1) * HALF].astype(F32)
        out[:, columns(core, other)] = piece[:, WIDE_A:].astype(F32)
    small = own[:, COL_SMALL:WIDE_A]
    gains[...] = gain_rows(small)[:2]
    shape = (max(8, router.shape[0]), LANES)
    router[...] = dot_nt(one_hot(lane(shape) == sublane(shape)), small)[: router.shape[0]]
    shape = (LANES, bias.shape[1])
    pick = one_hot(sublane(shape) == lane(shape) + LANE_BIAS)
    bias[...] = dot(small, pick)[: bias.shape[0]]


def across(value, pairs=((0, 1), (1, 0))):
    return lax.ppermute(value, SECTION, pairs)


def hop(value, step):
    return lax.ppermute(value, REPLICA, [(r, r ^ step) for r in range(lax.axis_size(REPLICA))])


def swap(value, step):
    if step == 0:
        return value
    return lax.ppermute(value, EXPERT, [(e, e ^ step) for e in range(lax.axis_size(EXPERT))])


def exchange(value, experts):
    return lax.all_to_all(
        value.reshape(experts, -1, value.shape[-1]), EXPERT, split_axis=0, concat_axis=0, tiled=True
    ).reshape(value.shape)


def groups_of(experts):
    return GROUPS if experts == 4 else ((None,),)


def group_exchange(groups, experts):
    def travel(which, pieces):
        if groups[which] == (None,):
            return [exchange(pieces[0], experts)]
        return [swap(piece, step) for piece, step in zip(pieces, groups[which])]

    return travel


def spread(value, experts, me):
    if experts != 4:
        return exchange(jnp.concatenate([value] * experts), experts)
    came = {step: swap(value, step) for step in (3, 2, 1, 0)}
    for bit in (1, 2):
        flag = me & bit != 0
        came = {step: jnp.where(flag, came[step ^ bit], came[step]) for step in came}
    return jnp.concatenate([came[step] for step in range(4)])


def gathered_sum(parts, experts):
    return jnp.sum(exchange(parts, experts).reshape(experts, -1, WIDE).astype(F32), axis=0)


def ordered(top, mine, theirs):
    return jnp.where(top, theirs, mine), jnp.where(top, mine, theirs)


def joined_cores(own, other):
    return (own.astype(F32) + hop(other, 1).astype(F32)).astype(BF16)


def joined_chips(pair, top):
    mine, theirs = ordered(top, *pair)
    return (mine.astype(F32) + hop(theirs, 2).astype(F32)).astype(BF16)


def anchor_kernel(value, out):
    for index in range(value.shape[0]):
        out[index] = value[index]


def anchor(value):
    scalars = pl.BlockSpec(memory_space=pltpu.SMEM)
    return pl.pallas_call(
        anchor_kernel, in_specs=[scalars], out_specs=scalars, out_shape=struct(value.shape, value.dtype)
    )(value)


def destinations(routes, experts, capacity, me):
    slot = routes.shape[1]
    hits = (routes[..., None] == jnp.arange(experts, dtype=jnp.int32)).astype(F32)
    places = np.arange(slot)
    before = jnp.asarray(places[:, None] > places[None, :], BF16)
    counts = jnp.einsum(
        "ts,lse->lte", before, jnp.sum(hits, axis=2).astype(BF16), preferred_element_type=F32
    )
    place = jnp.sum(hits * counts[:, :, None, :], axis=-1).astype(jnp.int32)
    if experts == 4:
        routes = routes ^ me
        routes = routes ^ (routes >> 1)
    return routes * capacity + place


def step(x_in, cotangent, segments, routes, gains, w_qkv, w_out, router, rel_bias, w_gate_up, w_down):
    section = lax.axis_index(SECTION)
    replica = lax.axis_index(REPLICA)
    me = lax.axis_index(EXPERT)
    first = section == 0
    core = replica % 2
    top = replica // 2 == 1
    experts = router.shape[2]
    held = w_qkv.shape[1]
    slot = x_in.shape[1]
    capacity = 5 * slot // (2 * experts)
    groups = groups_of(experts)
    count = sum(len(group) for group in groups)
    packed_shapes = [struct((experts * capacity // count, D), BF16)] * count
    units = w_down.shape[2]
    quarter = units // len(HOPS)
    core_info = anchor(core.astype(jnp.int32)[None])
    first_info = anchor(first.astype(jnp.int32)[None])
    last_info = anchor(first_info)

    def mine(value):
        return lax.dynamic_index_in_dim(value, section, 0, keepdims=False)

    def by_layer(value, swapped):
        return jnp.where(first, value, swapped), jnp.where(first, swapped, value)

    def half_of(value, part=0):
        return lax.dynamic_slice_in_dim(value, part * D + core * HALF, HALF, 1)

    def placed(value, start):
        return jnp.pad(value, ((0, held - value.shape[0]), (start, LANES - start - value.shape[1])))

    def grouped(values):
        values = list(values)
        return [[values.pop(0) for _ in group] for group in groups]

    routed = jnp.stack(
        by_layer(mine(routes[0]), across(lax.dynamic_index_in_dim(routes[0], 1 - section, 0, keepdims=False)))
    )
    small = placed(router[0], 0) + placed(gains[0].T, LANE_GAIN) + placed(rel_bias[0], LANE_BIAS)
    dense_a = jnp.concatenate([half_of(w_qkv[0], part) for part in range(3)] + [small], axis=1)
    dense_b = half_of(w_out[0])
    halves_a, halves_b = by_layer(dense_a, across(dense_a)), by_layer(dense_b, across(dense_b))

    start = replica * quarter
    near = [
        lax.dynamic_slice(w_gate_up, (0, 0, c, 0, start), (1, 1, 1, D, quarter)).reshape(D, quarter) for c in range(2)
    ] + [lax.dynamic_slice_in_dim(w_down[0, 0], start + c * (quarter // 2), quarter // 2, 0) for c in range(2)]
    near = [across(piece) for piece in near]
    far = [hop(piece, 2) for piece in near]
    weights = [w_gate_up, w_down, *near, *far]
    weights += [hop(piece, 1) for piece in near + far]
    owners = [replica ^ h for h in HOPS]
    infos = [
        anchor(jnp.stack([jnp.where(first, layer, 1 - layer).astype(jnp.int32)] + owners).astype(jnp.int32))
        for layer in range(2)
    ]

    dest = destinations(routed, experts, capacity, me)
    dest_rows = jnp.swapaxes(dest, 1, 2)
    onehot = jnp.asarray(bucket_rows(slot, experts), BF16)
    segment = mine(segments[:, 0])
    seg_col, seg_row = segment[:, None], segment[None, :]
    x = mine(x_in)
    cot = mine(cotangent)

    own_a0 = spread(halves_a[0], experts, me)
    own_b0 = spread(halves_b[0], experts, me)
    dense0 = (own_a0, own_b0, hop(own_a0, 1), hop(own_b0, 1))
    block = held // 4
    part = jnp.concatenate([halves_a[1], halves_b[1]], axis=1)
    part = lax.dynamic_slice_in_dim(part, (replica // 2 * 2 + section) * block, block, 0)
    part = spread(part, experts, me)

    def doubled(flag, value, came):
        pair = ordered(flag, value.reshape(experts, -1, WIDE), came.reshape(experts, -1, WIDE))
        return jnp.concatenate(pair, axis=1).reshape(-1, WIDE)

    part = doubled(jnp.logical_not(first), part, across(part))
    own1 = doubled(top, part, hop(part, 2))
    dense1 = (own1, hop(own1, 1))

    attend_cost = cost(4 * 10**9, 10**7, 10**6)
    back_cost = cost(10**10, 2 * 10**7, 10**6)

    def experts_forward(layer, packed):
        send = group_exchange(groups, experts)
        give = group_exchange(groups, experts)
        kept, hidden, came, returned = [], [], [], []
        for g, pieces in enumerate(grouped(packed)):
            results, both, shared = expert_call(infos[layer], send(g, pieces), weights)
            kept.append(both)
            hidden.append(shared)
            returned += give(g, results)
            came.append(hop(shared, 1))
        return (kept, hidden, came), returned

    common0 = (onehot, seg_col, seg_row, routed[0])
    common1 = (onehot, seg_col, seg_row, routed[1])
    qkv0, mixed0, lse0, small0 = kernel_call(
        mix_kernel, (core_info, x, own_a0, dense0[2], onehot, seg_col, seg_row),
        mix_shapes(slot) + [struct((D, LANES), BF16)], attend_scratch(slot), attend_cost,
    )
    resid0, moe_in0, weights0, *packed0 = kernel_call(
        project_kernel, (core_info, x, small0, own_b0, dense0[3], mixed0, routed[0], dest_rows[0]),
        project_shapes(slot, packed_shapes), [], cost(10**9, 4 * 10**6),
    )
    saved0, returned0 = experts_forward(0, packed0)
    out0, back00, back01, qkv1, mixed1, lse1, resid1, moe_in1, weights1, *packed1 = kernel_call(
        functools.partial(middle_kernel, count),
        (core_info, resid0, weights0, dest[0], *returned0, *dense1, *common1, dest_rows[1]),
        [struct((slot, D), BF16)] * 3 + mix_shapes(slot) + project_shapes(slot, packed_shapes),
        attend_scratch(slot) + [pltpu.VMEM((D, WIDE), BF16)] * 2 + [pltpu.SemaphoreType.DMA((2,))],
        attend_cost, lazy=(4 + count, 5 + count),
    )
    saved1, returned1 = experts_forward(1, packed1)
    out1, *packed1, grad_weights1 = kernel_call(
        functools.partial(turn_kernel, count), (resid1, weights1, dest[1], dest_rows[1], cot, *returned1),
        [struct((slot, D), BF16)] + packed_shapes + [struct((slot, LANES), F32)], [],
        cost(10**9, 4 * 10**6), scalars=0,
    )

    def experts_backward(layer, saved, packed):
        kept, hidden, came = saved
        send = group_exchange(groups, experts)
        give = group_exchange(groups, experts)
        both, came_back, returned = [], [], []
        for g, pieces in enumerate(grouped(packed)):
            results, shared = expert_call(infos[layer], send(g, pieces), weights, kept[g])
            both.append(shared)
            returned += give(g, results)
            came_back.append(hop(shared, 1))
        grads = grads_call(hidden, came, both, came_back)
        summed = []
        for k in range(3):
            came_far = hop(grads[k], 2)
            if layer and k:
                came_far = lax.optimization_barrier((came_far, first_info))[0]
            for span in ((slice(0, D // 2), slice(D // 2, D)) if k == 1 else (slice(None),)):
                summed.append((grads[3 + k][span].astype(F32) + came_far[span].astype(F32)).astype(BF16))
        pairs = ((0, 1),) if layer else ((1, 0),)
        return returned, [(value, across(value, pairs)) for value in summed]

    grad_returned1, expert_sums1 = experts_backward(1, saved1, packed1)
    grad_own1, grad_other1, grad_in1, *grad_packed0, grad_weights0 = kernel_call(
        functools.partial(back_turn_kernel, count),
        (core_info, out0, *dense1, *common1, dest[1], cot, resid1, moe_in1, weights1, grad_weights1, qkv1, mixed1, lse1,
         *grad_returned1, weights0, back00, back01, dest_rows[0]),
        back_shapes(slot) + packed_shapes + [struct((slot, LANES), F32)], back_scratch(slot), back_cost, lazy=(2, 3),
    )
    grad_returned0, expert_sums0 = experts_backward(0, saved0, grad_packed0)
    grad_own0, grad_other0, grad_in0 = kernel_call(
        functools.partial(back_kernel, count),
        (core_info, x, *dense0, *common0, dest[0], grad_in1, resid0, moe_in0, weights0, grad_weights0, qkv0, mixed0, lse0,
         *grad_returned0),
        back_shapes(slot), back_scratch(slot), back_cost, lazy=(2, 3, 4, 5),
    )
    ended = [(sum0, sum1, came0, came1) for (sum0, came0), (sum1, came1) in zip(expert_sums0, expert_sums1)]
    grad_down = finish(last_info, ended[3], D, 0)[None, None]
    grad_gate_up = finish(last_info, ended[0], 2 * D, 0)
    grad_gate_up = finish(last_info, ended[1], 2 * D, D, grad_gate_up)
    grad_gate_up = finish(last_info, ended[2], 2 * D, D + D // 2, grad_gate_up).reshape(1, 1, 2, D, quarter)

    part = joined_cores(grad_own1, grad_other1).reshape(experts, 2, held // 2, WIDE)
    part = joined_chips((part[:, 0], part[:, 1]), top).reshape(-1, WIDE)
    reduced1 = gathered_sum(part, experts)
    part = gathered_sum(joined_cores(grad_own0, grad_other0), experts).astype(BF16)
    reduced0 = joined_chips((part[: held // 2], part[held // 2 :]), top).astype(F32)
    total = jnp.where(first, reduced0, reduced1)
    for value, pair in ((reduced1, (0, 1)), (reduced0, (1, 0))):
        total = total + across(value.astype(BF16), (pair,)).astype(F32)
    total = total.astype(BF16)
    total = jnp.concatenate(ordered(top, total, hop(total, 2)))
    dense_grads = kernel_call(
        spell_kernel, (core_info, total, hop(total, 1)),
        [
            struct((held, 3 * D), F32),
            struct((held, D), F32),
            struct((2, held), F32),
            struct((experts, held), F32),
            struct(rel_bias.shape[1:], F32),
        ],
        [],
        cost(held * D, held * D * 16),
    )
    grad_qkv, grad_out, grad_gains, grad_router, grad_bias = (value[None] for value in dense_grads)

    def both_micro(value0, value1):
        own, swapped = jnp.where(first, value0, value1), across(jnp.where(first, value1, value0))
        return jnp.stack([jnp.where(first, own, swapped), jnp.where(first, swapped, own)])[None]

    return (
        both_micro(out0, out1),
        both_micro(grad_in0, grad_in1),
        grad_gains,
        grad_qkv,
        grad_out,
        jnp.swapaxes(grad_router, 1, 2),
        grad_bias,
        grad_gate_up,
        grad_down,
    )


def solution(mesh):
    tokens = P(None, (EXPERT, REPLICA), None)
    layered = P(SECTION, None, (EXPERT, REPLICA), None)
    dense = P(SECTION, EXPERT, None)
    gains = P(SECTION, None, EXPERT)
    in_specs = (tokens,) * 3 + (layered, gains) + (dense,) * 4
    in_specs += (P(SECTION, EXPERT, None, None, None), P(SECTION, EXPERT, None, None))
    out_specs = (layered, layered, gains) + (dense,) * 4
    out_specs += (P(SECTION, EXPERT, None, None, REPLICA), P(SECTION, EXPERT, REPLICA, None))
    return jax.shard_map(step, mesh=mesh, in_specs=in_specs, out_specs=out_specs, check_vma=False)
```
